128 devices in a mesh: gossip: 4 (over x_hi, core), field: 32 (over x_lo, z, y).
Axes of the slice: x: 4 (x_hi: 2, x_lo: 2; x = x_hi * 2 + x_lo), y: 4, z: 4, core: 2. Of those that a mesh axis runs over, the one named last changes fastest.
Arguments:
- measured_features: bfloat16 [8, 128, 96, 512], P('gossip', 'field'), may hold values from -6 to 6
- feeder_of_row: int32 [128], P('field'), may hold values from 0 to 127, each once
- feeder_table: bfloat16 [128, 512], replicated, may hold values from -3 to 3
- time_qkv: bfloat16 [512, 1536], replicated, may hold values from -0.25 to 0.25
- time_out: bfloat16 [512, 512], replicated, may hold values from -0.25 to 0.25
- feed_qkv: bfloat16 [512, 1536], replicated, may hold values from -0.25 to 0.25
- feed_out: bfloat16 [512, 512], replicated, may hold values from -0.25 to 0.25
- adjoint_of_prediction: bfloat16 [8, 128, 96, 512], P('gossip', None, 'field'), may hold values from -0.09375 to 0.09375
- round_index: int32 [1], replicated, may hold values from 0 to 1
Outputs:
- predicted_load: bfloat16 [8, 128, 96, 512], P('gossip', None, 'field')
- peer_mean_derivatives: float32 [4, 4096, 512], P('gossip')
The draws below stay inside these ranges and needn't reach their ends.
All inputs are finite; a program needn't handle non-finite values.
Results may differ from the reference program's by a relative error of at most 0.02.
Values may be sent and summed in bfloat16 or wider, within the bound.
A program may use at most 128 MiB of HBM per device.

```python
import math
from functools import partial
import jax
import jax.numpy as jnp
from jax import lax

D = 512
HEADS = 8
BATCH = 2
ROUNDS = 2
FEEDERS = 128
SLOTS = 96
SAMPLES = 8
N_GOSSIP = 4


def steps_of(stream_key, extent, cuts, smallest, largest):
    def one(axis_at, shards_of):
        steps = jax.random.uniform(jax.random.fold_in(jax.random.fold_in(stream_key, 6), axis_at), (shards_of,), jnp.float32, smallest / len(cuts), largest / len(cuts))
        return jnp.repeat(jnp.exp(steps), extent[axis_at] // shards_of).reshape((-1,) + (1,) * (len(extent) - axis_at - 1))

    gain = one(*cuts[0])
    for cut in cuts[1:]:
        gain = gain * one(*cut)
    return gain


def scatter_about(stream_key, dims, spread, limit, shards=(), held_as=jnp.bfloat16):
    array = spread * jax.random.normal(stream_key, dims, jnp.float32)
    if shards:
        array = array * steps_of(stream_key, dims, shards, -0.22, 0.18)
    return jnp.clip(array, -limit, limit).astype(held_as)


def setup_inputs(seed: int = 0) -> dict:
    arg_keys = jax.random.split(jax.random.key(seed), 10)
    return {
        "measured_features": scatter_about(arg_keys[0], (SAMPLES, FEEDERS, SLOTS, D), 1.0, 6.0, ((0, 4), (1, 32))),
        "feeder_of_row": jax.random.permutation(arg_keys[1], FEEDERS).astype(jnp.int32),
        "feeder_table": scatter_about(arg_keys[2], (FEEDERS, D), 0.5, 3.0),
        "time_qkv": scatter_about(arg_keys[3], (D, 3 * D), D ** -0.5, 0.25),
        "time_out": scatter_about(arg_keys[4], (D, D), D ** -0.5, 0.25),
        "feed_qkv": scatter_about(arg_keys[5], (D, 3 * D), D ** -0.5, 0.25),
        "feed_out": scatter_about(arg_keys[6], (D, D), D ** -0.5, 0.25),
        "adjoint_of_prediction": scatter_about(arg_keys[7], (SAMPLES, FEEDERS, SLOTS, D), (1.0 / (BATCH * FEEDERS * SLOTS) ** 0.5), 0.09375, ((0, 4), (2, 32))),
        "round_index": jax.random.randint(arg_keys[8], (1,), 0, ROUNDS).astype(jnp.int32),
    }


epsilon = 1e-05

def normalize(hidden):
    wide = hidden.astype(jnp.float32)
    factor = lax.rsqrt(lax.optimization_barrier(jnp.mean(wide * wide, axis=-1, keepdims=True)) + epsilon)
    return (wide * factor).astype(jnp.bfloat16)

def attend(stacked_array, heads, causal):
    groups, length, triple = stacked_array.shape
    width = triple // 3
    size = width // heads
    parts = stacked_array.reshape(groups, length, 3, heads, size)
    query = parts[:, :, 0]
    keys = parts[:, :, 1]
    values = parts[:, :, 2]
    scores = jnp.einsum('glhe,gmhe->ghlm', query, keys, preferred_element_type=jnp.float32) * (1.0 / math.sqrt(size))
    powers = jnp.exp(scores)
    if causal:
        allowed = jnp.arange(length)[:, None] >= jnp.arange(length)[None, :]
        powers = jnp.where(allowed, powers, 0.0)
    shares = powers / lax.optimization_barrier(jnp.sum(powers, axis=-1, keepdims=True))
    rounded = shares.astype(jnp.bfloat16)
    mixed_slope_estimate = jnp.einsum('ghlm,gmhe->glhe', rounded, values, preferred_element_type=jnp.float32)
    return mixed_slope_estimate.reshape(groups, length, width).astype(jnp.bfloat16)

def sublayer_forward(hidden, w_qkv, w_out, heads, causal):
    groups, length, width = hidden.shape
    normed, norm_back = jax.vjp(normalize, hidden)
    stacked_array = jnp.dot(normed.reshape(-1, width), w_qkv, preferred_element_type=jnp.float32)
    stacked_array = stacked_array.astype(jnp.bfloat16).reshape(groups, length, 3 * width)
    mixed_slope_estimate, attend_back = jax.vjp(partial(attend, heads=heads, causal=causal), stacked_array)
    result = hidden.astype(jnp.float32) + jnp.dot(mixed_slope_estimate.reshape(-1, width), w_out, preferred_element_type=jnp.float32).reshape(groups, length, width)
    return (result, (normed, mixed_slope_estimate, norm_back, attend_back))

def sublayer_backward(upstream, saved, w_qkv, w_out, need_input):
    normed, mixed_slope_estimate, norm_back, attend_back = saved
    groups, length, width = upstream.shape
    flat_up = upstream.reshape(-1, width)
    grad_out = jnp.dot(mixed_slope_estimate.reshape(-1, width).T, flat_up, preferred_element_type=jnp.float32)
    grad_mixed = jnp.dot(flat_up, w_out.T, preferred_element_type=jnp.float32).astype(jnp.bfloat16).reshape(groups, length, width)
    grad_packed, = attend_back(grad_mixed)
    flat_packed = grad_packed.reshape(-1, 3 * width)
    grad_qkv = jnp.dot(normed.reshape(-1, width).T, flat_packed, preferred_element_type=jnp.float32)
    if not need_input:
        return (grad_qkv, grad_out, None)
    grad_normed = jnp.dot(flat_packed, w_qkv.T, preferred_element_type=jnp.float32).astype(jnp.bfloat16).reshape(groups, length, width)
    grad_hidden, = norm_back(grad_normed)
    combined = (grad_hidden.astype(jnp.float32) + upstream.astype(jnp.float32)).astype(jnp.bfloat16)
    return (grad_qkv, grad_out, combined)

def embed(rows, feeder_table):
    table_rows = feeder_table.shape[0]
    onehot = (rows[:, None] == jnp.arange(table_rows, dtype=jnp.int32)[None, :]).astype(jnp.bfloat16)
    return jnp.dot(onehot, feeder_table, preferred_element_type=jnp.float32)

def reference(measured_features, feeder_of_row, feeder_table, time_qkv, time_out, feed_qkv, feed_out, adjoint_of_prediction, round_index):
    width = measured_features.shape[-1]
    added = embed(feeder_of_row, feeder_table)

    def lone_example_features(pair):
        sample_x, sample_dy = pair
        start = sample_x.astype(jnp.float32) + added[:, None, :]
        first, saved_time = sublayer_forward(start, time_qkv, time_out, HEADS, True)
        regrouped = jnp.transpose(first.astype(jnp.bfloat16), (1, 0, 2))
        right_factor, saved_feed = sublayer_forward(regrouped, feed_qkv, feed_out, HEADS, False)
        predicted_load = jnp.transpose(right_factor.astype(jnp.bfloat16), (1, 0, 2))
        upstream = jnp.transpose(sample_dy, (1, 0, 2))
        feeder_query_gradient, grad_fo, regrouped_gradient_rows = sublayer_backward(upstream, saved_feed, feed_qkv, feed_out, True)
        grad_first = jnp.transpose(regrouped_gradient_rows, (1, 0, 2))
        grad_tq, grad_to, unused = sublayer_backward(grad_first, saved_time, time_qkv, time_out, False)
        stacked_array = jnp.concatenate([grad_tq.reshape(-1, width), grad_to, feeder_query_gradient.reshape(-1, width), grad_fo], axis=0)
        return (predicted_load, stacked_array)
    predicted_load, example_wise_derivatives = lax.map(lone_example_features, (measured_features, adjoint_of_prediction))
    totals = example_wise_derivatives.reshape(N_GOSSIP, BATCH, 8 * width, width).sum(axis=1)
    rounded = lax.optimization_barrier(totals.astype(jnp.bfloat16)).astype(jnp.float32)
    partner = jnp.bitwise_xor(jnp.arange(N_GOSSIP, dtype=jnp.int32), jnp.left_shift(jnp.int32(1), round_index[0]))
    peer_mean_derivatives = (rounded + rounded[partner]) * 0.5
    return (predicted_load, peer_mean_derivatives)
```

```python
from functools import partial
import math

import jax
import jax.numpy as jnp
from jax import lax
from jax.experimental import pallas as pl
from jax.experimental.pallas import tpu as pltpu
from jax.sharding import PartitionSpec as P

HEADS = 8


epsilon = 1e-05


def normalize(hidden):
    wide = hidden.astype(jnp.float32)
    factor = lax.rsqrt(jnp.mean(wide * wide, axis=-1, keepdims=True) + epsilon)
    return (wide * factor).astype(jnp.bfloat16)


def attend(stacked_array, heads, causal):
    groups, length, triple = stacked_array.shape
    width = triple // 3
    size = width // heads
    parts = stacked_array.reshape(groups, length, 3, heads, size)
    query = parts[:, :, 0]
    keys = parts[:, :, 1]
    values = parts[:, :, 2]
    scores = jnp.einsum("glhe,gmhe->ghlm", query, keys, preferred_element_type=jnp.float32) * (
        1.0 / math.sqrt(size)
    )
    powers = jnp.exp(scores)
    if causal:
        allowed = jnp.arange(length)[:, None] >= jnp.arange(length)[None, :]
        powers = jnp.where(allowed, powers, 0.0)
    shares = powers / jnp.sum(powers, axis=-1, keepdims=True)
    rounded = shares.astype(jnp.bfloat16)
    mixed_slope_estimate = jnp.einsum(
        "ghlm,gmhe->glhe", rounded, values, preferred_element_type=jnp.float32
    )
    return mixed_slope_estimate.reshape(groups, length, width).astype(jnp.bfloat16)


def sublayer_forward(hidden, w_qkv, w_out, heads, causal):
    groups, length, width = hidden.shape
    normed, norm_back = jax.vjp(normalize, hidden)
    stacked_array = jnp.dot(normed.reshape(-1, width), w_qkv, preferred_element_type=jnp.float32)
    stacked_array = stacked_array.astype(jnp.bfloat16).reshape(groups, length, 3 * width)
    mixed_slope_estimate, attend_back = jax.vjp(
        partial(attend, heads=heads, causal=causal), stacked_array
    )
    result = hidden.astype(jnp.float32) + jnp.dot(
        mixed_slope_estimate.reshape(-1, width), w_out, preferred_element_type=jnp.float32
    ).reshape(groups, length, width)
    return (result, (normed, mixed_slope_estimate, norm_back, attend_back))


def sublayer_backward(upstream, saved, w_qkv, w_out, need_input):
    normed, mixed_slope_estimate, norm_back, attend_back = saved
    groups, length, width = upstream.shape
    flat_up = upstream.reshape(-1, width)
    grad_out = jnp.dot(
        mixed_slope_estimate.reshape(-1, width).T, flat_up, preferred_element_type=jnp.float32
    )
    grad_mixed = (
        jnp.dot(flat_up, w_out.T, preferred_element_type=jnp.float32)
        .astype(jnp.bfloat16)
        .reshape(groups, length, width)
    )
    (grad_packed,) = attend_back(grad_mixed)
    flat_packed = grad_packed.reshape(-1, 3 * width)
    grad_qkv = jnp.dot(normed.reshape(-1, width).T, flat_packed, preferred_element_type=jnp.float32)
    if not need_input:
        return (grad_qkv, grad_out, None)
    grad_normed = (
        jnp.dot(flat_packed, w_qkv.T, preferred_element_type=jnp.float32)
        .astype(jnp.bfloat16)
        .reshape(groups, length, width)
    )
    (grad_hidden,) = norm_back(grad_normed)
    combined = (grad_hidden.astype(jnp.float32) + upstream.astype(jnp.float32)).astype(jnp.bfloat16)
    return (grad_qkv, grad_out, combined)


def embed(rows, feeder_table):
    table_rows = feeder_table.shape[0]
    onehot = (rows[:, None] == jnp.arange(table_rows, dtype=jnp.int32)[None, :]).astype(
        jnp.bfloat16
    )
    return jnp.dot(onehot, feeder_table, preferred_element_type=jnp.float32)


MESH = pl.DeviceIdType.MESH
LANES = 128
UNIT = 1024


def coordinates():
    gossip = lax.axis_index("gossip")
    field = lax.axis_index("field")
    x_hi, core = gossip // 2, gossip % 2
    x_lo, z, y = field // 16, (field // 4) % 4, field % 4

    def at(x_hi, core, x_lo, z, y):
        return (x_hi * 2 + core, (x_lo * 4 + z) * 4 + y)

    def even(position):
        return position + 1 - 2 * (position % 2)

    return {
        "ya": (((y + 1) // 2) % 2, at(x_hi, core, x_lo, z, even(y))),
        "yb": (y // 2, at(x_hi, core, x_lo, z, 3 - y)),
        "za": (((z + 1) // 2) % 2, at(x_hi, core, x_lo, even(z), y)),
        "zb": (z // 2, at(x_hi, core, x_lo, 3 - z, y)),
        "xa": ((x_hi + x_lo) % 2, at(x_hi, core, 1 - x_lo, z, y)),
        "xb": (x_hi, at(1 - x_hi, core, 1 - x_lo, z, y)),
        "core": (core, at(x_hi, 1 - core, x_lo, z, y)),
    }


def block_of(rows):
    for parts in range(1, rows + 1):
        if rows % parts == 0 and rows // parts <= 256 and (rows // parts) % 16 == 0:
            return rows // parts
    return rows


def reduce_kernel(chains, used, g_ref, out_ref, acc, full, inbox, rs_send, rs_recv, ag_send, ag_recv, out_sem):
    links = coordinates()
    barrier = pltpu.get_barrier_semaphore()
    for name in used:
        pl.semaphore_signal(barrier, inc=1, device_id=links[name][1], device_id_type=MESH)
    pl.semaphore_wait(barrier, len(used))

    steps = len(used)
    state = []
    for start, wave, order in chains:
        state.append({"at": [start], "start": start})

    def halves(j, s):
        start, wave, order = chains[j]
        bit, peer = links[order[s]]
        rows = UNIT >> (s + 1)
        base = state[j]["at"][s]
        return base + bit * rows, base + (1 - bit) * rows, rows, peer

    def rs_copy(j, s):
        keep, leave, rows, peer = halves(j, s)
        source = g_ref if s == 0 else acc
        slot = chains[j][0] + UNIT - 2 * rows
        return pltpu.make_async_remote_copy(
            src_ref=source.at[pl.ds(pl.multiple_of(leave, 16), rows)],
            dst_ref=inbox.at[pl.ds(slot, rows)],
            send_sem=rs_send.at[j, s],
            recv_sem=rs_recv.at[j, s],
            device_id=peer,
            device_id_type=MESH,
        )

    def rs_add(j, s):
        keep, leave, rows, peer = halves(j, s)
        slot = chains[j][0] + UNIT - 2 * rows
        source = g_ref if s == 0 else acc
        target = full if s == steps - 1 else acc
        block = block_of(rows)

        def add(i, carry):
            here = pl.ds(pl.multiple_of(keep + i * block, 16), block)
            there = pl.ds(pl.multiple_of(slot + i * block, 16), block)
            total = source[here, :].astype(jnp.float32) + inbox[there, :].astype(jnp.float32)
            if s == steps - 1:
                total = total * 0.5
            target[here, :] = total.astype(jnp.bfloat16)
            return carry

        lax.fori_loop(0, rows // block, add, 0)
        state[j]["at"].append(keep)

    def ag_copy(j, s):
        keep, leave, rows, peer = halves(j, s)
        mine = full.at[pl.ds(pl.multiple_of(keep, 16), rows)]
        return pltpu.make_async_remote_copy(
            src_ref=mine,
            dst_ref=mine,
            send_sem=ag_send.at[j, s],
            recv_sem=ag_recv.at[j, s],
            device_id=peer,
            device_id_type=MESH,
        )

    for j in range(len(chains)):
        rs_copy(j, 0).start()
    waves = 1 + max(chain[1] for chain in chains)
    for turn in range(2 * steps + waves - 1):
        for wave in range(waves):
            stage = turn - wave
            if not 0 <= stage < 2 * steps:
                continue
            for j in range(len(chains)):
                if chains[j][1] != wave:
                    continue
                if stage < steps:
                    rs_copy(j, stage).wait()
                    rs_add(j, stage)
                    if stage + 1 < steps:
                        rs_copy(j, stage + 1).start()
                    else:
                        ag_copy(j, steps - 1).start()
                else:
                    s = 2 * steps - 1 - stage
                    ag_copy(j, s).wait()
                    if s > 0:
                        ag_copy(j, s - 1).start()
                    else:
                        part = pl.ds(chains[j][0], UNIT)
                        pltpu.make_async_copy(full.at[part], out_ref.at[part], out_sem.at[j]).start()
    for j in range(len(chains)):
        part = pl.ds(chains[j][0], UNIT)
        pltpu.make_async_copy(full.at[part], out_ref.at[part], out_sem.at[j]).wait()


def reduce_over(first, links, collective_id):
    used = tuple(first) + tuple(links)

    def run(g):
        rows = g.shape[0]
        count = rows // UNIT
        chains = []
        for j in range(count):
            turn = j % len(links)
            order = tuple(first) + tuple(links[(turn + s) % len(links)] for s in range(len(links)))
            chains.append((j * UNIT, j // len(links), order))
        steps = len(used)
        return pl.pallas_call(
            partial(reduce_kernel, tuple(chains), used),
            out_shape=jax.ShapeDtypeStruct(g.shape, jnp.bfloat16),
            in_specs=[pl.BlockSpec(memory_space=pltpu.VMEM)],
            out_specs=pl.BlockSpec(memory_space=pl.ANY),
            scratch_shapes=[
                pltpu.VMEM(g.shape, jnp.bfloat16),
                pltpu.VMEM(g.shape, jnp.bfloat16),
                pltpu.VMEM(g.shape, jnp.bfloat16),
                pltpu.SemaphoreType.DMA((count, steps)),
                pltpu.SemaphoreType.DMA((count, steps)),
                pltpu.SemaphoreType.DMA((count, steps)),
                pltpu.SemaphoreType.DMA((count, steps)),
                pltpu.SemaphoreType.DMA((count,)),
            ],
            compiler_params=pltpu.CompilerParams(
                collective_id=collective_id, has_side_effects=True, vmem_limit_bytes=40 << 20
            ),
        )(g)

    return run


def pair_mean(g, round_index):
    links = ("ya", "za", "xa", "yb", "zb")
    return lax.cond(
        round_index[0] == 0,
        reduce_over(("core",), links, 1),
        reduce_over((), links + ("xb",), 2),
        g,
    )


def on_device(
    measured_features,
    feeder_of_row,
    feeder_table,
    time_qkv,
    time_out,
    feed_qkv,
    feed_out,
    adjoint_of_prediction,
    round_index,
):
    batch, feed_local, slot_count, width = measured_features.shape
    feeder_count = adjoint_of_prediction.shape[1]
    slot_local = adjoint_of_prediction.shape[2]
    added = embed(feeder_of_row, feeder_table)
    start = measured_features.astype(jnp.float32) + added[None, :, None, :]
    start = start.reshape(batch * feed_local, slot_count, width)
    first, saved_time = sublayer_forward(start, time_qkv, time_out, HEADS, True)
    first = first.astype(jnp.bfloat16).reshape(batch, feed_local, slot_count, width)
    by_slot = lax.all_to_all(first, "field", split_axis=2, concat_axis=1, tiled=True)
    regrouped = jnp.transpose(by_slot, (0, 2, 1, 3)).reshape(
        batch * slot_local, feeder_count, width
    )
    right_factor, saved_feed = sublayer_forward(regrouped, feed_qkv, feed_out, HEADS, False)
    right_factor = right_factor.astype(jnp.bfloat16).reshape(batch, slot_local, feeder_count, width)
    predicted_load = jnp.transpose(right_factor, (0, 2, 1, 3))
    upstream = jnp.transpose(adjoint_of_prediction, (0, 2, 1, 3)).reshape(
        batch * slot_local, feeder_count, width
    )
    feeder_query_gradient, grad_fo, regrouped_gradient_rows = sublayer_backward(
        upstream, saved_feed, feed_qkv, feed_out, True
    )
    grad_slots = jnp.transpose(
        regrouped_gradient_rows.reshape(batch, slot_local, feeder_count, width), (0, 2, 1, 3)
    )
    grad_first = lax.all_to_all(grad_slots, "field", split_axis=1, concat_axis=2, tiled=True)
    grad_first = grad_first.reshape(batch * feed_local, slot_count, width)
    grad_tq, grad_to, unused = sublayer_backward(grad_first, saved_time, time_qkv, time_out, False)
    local_grads = jnp.concatenate(
        [grad_tq.reshape(-1, width), grad_to, feeder_query_gradient.reshape(-1, width), grad_fo],
        axis=0,
    )
    tiles = local_grads.astype(jnp.bfloat16).reshape(512, 8, 4, LANES).transpose(0, 2, 1, 3).reshape(-1, LANES)
    mean = pair_mean(tiles, round_index)
    mean = mean.reshape(512, 4, 8, LANES).transpose(0, 2, 1, 3).reshape(4096, 512).astype(jnp.float32)
    return (predicted_load, mean[None])


def solution(mesh):
    placed = (
        P("gossip", "field", None, None),
        P("field"),
        P(),
        P(),
        P(),
        P(),
        P(),
        P("gossip", None, "field", None),
        P(),
    )
    return jax.shard_map(
        on_device,
        mesh=mesh,
        in_specs=placed,
        out_specs=(P("gossip", None, "field", None), P("gossip", None, None)),
        check_vma=False,
    )
```

```python
from functools import partial
import math

import jax
import jax.numpy as jnp
from jax import lax
from jax.experimental import pallas as pl
from jax.experimental.pallas import tpu as pltpu
from jax.sharding import PartitionSpec as P

epsilon = 1e-05


MESH = pl.DeviceIdType.MESH
LANES = 128
UNIT = 1024


def coordinates():
    gossip = lax.axis_index("gossip")
    field = lax.axis_index("field")
    x_hi, core = gossip // 2, gossip % 2
    x_lo, z, y = field // 16, (field // 4) % 4, field % 4

    def at(x_hi, core, x_lo, z, y):
        return (x_hi * 2 + core, (x_lo * 4 + z) * 4 + y)

    def even(position):
        return position + 1 - 2 * (position % 2)

    return {
        "ya": (((y + 1) // 2) % 2, at(x_hi, core, x_lo, z, even(y))),
        "yb": (y // 2, at(x_hi, core, x_lo, z, 3 - y)),
        "za": (((z + 1) // 2) % 2, at(x_hi, core, x_lo, even(z), y)),
        "zb": (z // 2, at(x_hi, core, x_lo, 3 - z, y)),
        "xa": ((x_hi + x_lo) % 2, at(x_hi, core, 1 - x_lo, z, y)),
        "xb": (x_hi, at(1 - x_hi, core, 1 - x_lo, z, y)),
        "core": (core, at(x_hi, 1 - core, x_lo, z, y)),
    }


def block_of(rows):
    for parts in range(1, rows + 1):
        if rows % parts == 0 and rows // parts <= 256 and (rows // parts) % 16 == 0:
            return rows // parts
    return rows


def reduce_kernel(chains, used, g_ref, out_ref, acc, full, inbox, rs_send, rs_recv, ag_send, ag_recv, out_sem):
    links = coordinates()
    barrier = pltpu.get_barrier_semaphore()
    for name in used:
        pl.semaphore_signal(barrier, inc=1, device_id=links[name][1], device_id_type=MESH)
    pl.semaphore_wait(barrier, len(used))

    steps = len(used)
    state = []
    for start, wave, order in chains:
        state.append({"at": [start], "start": start})

    def halves(j, s):
        start, wave, order = chains[j]
        bit, peer = links[order[s]]
        rows = UNIT >> (s + 1)
        base = state[j]["at"][s]
        return base + bit * rows, base + (1 - bit) * rows, rows, peer

    def rs_copy(j, s):
        keep, leave, rows, peer = halves(j, s)
        source = g_ref if s == 0 else acc
        slot = chains[j][0] + UNIT - 2 * rows
        return pltpu.make_async_remote_copy(
            src_ref=source.at[pl.ds(pl.multiple_of(leave, 16), rows)],
            dst_ref=inbox.at[pl.ds(slot, rows)],
            send_sem=rs_send.at[j, s],
            recv_sem=rs_recv.at[j, s],
            device_id=peer,
            device_id_type=MESH,
        )

    def rs_add(j, s):
        keep, leave, rows, peer = halves(j, s)
        slot = chains[j][0] + UNIT - 2 * rows
        source = g_ref if s == 0 else acc
        target = full if s == steps - 1 else acc
        block = block_of(rows)

        def add(i, carry):
            here = pl.ds(pl.multiple_of(keep + i * block, 16), block)
            there = pl.ds(pl.multiple_of(slot + i * block, 16), block)
            total = source[here, :].astype(jnp.float32) + inbox[there, :].astype(jnp.float32)
            if s == steps - 1:
                total = total * 0.5
            target[here, :] = total.astype(jnp.bfloat16)
            return carry

        lax.fori_loop(0, rows // block, add, 0)
        state[j]["at"].append(keep)

    def ag_copy(j, s):
        keep, leave, rows, peer = halves(j, s)
        mine = full.at[pl.ds(pl.multiple_of(keep, 16), rows)]
        return pltpu.make_async_remote_copy(
            src_ref=mine,
            dst_ref=mine,
            send_sem=ag_send.at[j, s],
            recv_sem=ag_recv.at[j, s],
            device_id=peer,
            device_id_type=MESH,
        )

    for j in range(len(chains)):
        rs_copy(j, 0).start()
    waves = 1 + max(chain[1] for chain in chains)
    for turn in range(2 * steps + waves - 1):
        for wave in range(waves):
            stage = turn - wave
            if not 0 <= stage < 2 * steps:
                continue
            for j in range(len(chains)):
                if chains[j][1] != wave:
                    continue
                if stage < steps:
                    rs_copy(j, stage).wait()
                    rs_add(j, stage)
                    if stage + 1 < steps:
                        rs_copy(j, stage + 1).start()
                    else:
                        ag_copy(j, steps - 1).start()
                else:
                    s = 2 * steps - 1 - stage
                    ag_copy(j, s).wait()
                    if s > 0:
                        ag_copy(j, s - 1).start()
                    else:
                        part = pl.ds(chains[j][0], UNIT)
                        pltpu.make_async_copy(full.at[part], out_ref.at[part], out_sem.at[j]).start()
    for j in range(len(chains)):
        part = pl.ds(chains[j][0], UNIT)
        pltpu.make_async_copy(full.at[part], out_ref.at[part], out_sem.at[j]).wait()


def reduce_over(first, links, collective_id):
    used = tuple(first) + tuple(links)

    def run(g):
        rows = g.shape[0]
        count = rows // UNIT
        chains = []
        for j in range(count):
            turn = j % len(links)
            order = tuple(first) + tuple(links[(turn + s) % len(links)] for s in range(len(links)))
            chains.append((j * UNIT, j // len(links), order))
        steps = len(used)
        return pl.pallas_call(
            partial(reduce_kernel, tuple(chains), used),
            out_shape=jax.ShapeDtypeStruct(g.shape, jnp.bfloat16),
            in_specs=[pl.BlockSpec(memory_space=pltpu.VMEM)],
            out_specs=pl.BlockSpec(memory_space=pl.ANY),
            scratch_shapes=[
                pltpu.VMEM(g.shape, jnp.bfloat16),
                pltpu.VMEM(g.shape, jnp.bfloat16),
                pltpu.VMEM(g.shape, jnp.bfloat16),
                pltpu.SemaphoreType.DMA((count, steps)),
                pltpu.SemaphoreType.DMA((count, steps)),
                pltpu.SemaphoreType.DMA((count, steps)),
                pltpu.SemaphoreType.DMA((count, steps)),
                pltpu.SemaphoreType.DMA((count,)),
            ],
            compiler_params=pltpu.CompilerParams(
                collective_id=collective_id, has_side_effects=True, vmem_limit_bytes=40 << 20
            ),
        )(g)

    return run


def pair_mean(g, round_index):
    links = ("ya", "za", "xa", "yb", "zb")
    return lax.cond(
        round_index[0] == 0,
        reduce_over(("core",), links, 1),
        reduce_over((), links + ("xb",), 2),
        g,
    )


def exchange_kernel(count, send_ref, got_ref, send_sem, recv_sem, own_sem):
    gossip = lax.axis_index("gossip")
    me = lax.axis_index("field")
    rows = send_ref.shape[0] // count

    def block(i):
        return pl.ds(pl.multiple_of(i * rows, 8), rows)

    def peer(i):
        return (gossip, lax.rem(me + i, count))

    barrier = pltpu.get_barrier_semaphore()

    def greet(i, carry):
        pl.semaphore_signal(barrier, inc=1, device_id=peer(i), device_id_type=MESH)
        return carry

    lax.fori_loop(1, count, greet, 0)
    own = pltpu.make_async_copy(send_ref.at[block(me)], got_ref.at[block(me)], own_sem)
    own.start()
    pl.semaphore_wait(barrier, count - 1)

    def copy(i):
        to = lax.rem(me + i, count)
        return pltpu.make_async_remote_copy(
            src_ref=send_ref.at[block(to)],
            dst_ref=got_ref.at[block(me)],
            send_sem=send_sem.at[i],
            recv_sem=recv_sem.at[i],
            device_id=(gossip, to),
            device_id_type=MESH,
        )

    def start(i, carry):
        copy(i).start()
        return carry

    def finish(i, carry):
        copy(i).wait()
        return carry

    lax.fori_loop(1, count, start, 0)
    lax.fori_loop(1, count, finish, 0)
    own.wait()


def exchange(blocks, count, collective_id):
    return pl.pallas_call(
        partial(exchange_kernel, count),
        out_shape=jax.ShapeDtypeStruct(blocks.shape, blocks.dtype),
        in_specs=[pl.BlockSpec(memory_space=pltpu.VMEM)],
        out_specs=pl.BlockSpec(memory_space=pltpu.VMEM),
        scratch_shapes=[
            pltpu.SemaphoreType.DMA((count,)),
            pltpu.SemaphoreType.DMA((count,)),
            pltpu.SemaphoreType.DMA(()),
        ],
        compiler_params=pltpu.CompilerParams(collective_id=collective_id, has_side_effects=True),
    )(blocks)


SIZE = 64
PAIR = 2 * SIZE


def dot(a, b, contract=((1,), (0,))):
    return lax.dot_general(a, b, (contract, ((), ())), preferred_element_type=jnp.float32)


NT = ((1,), (1,))
TN = ((0,), (0,))


def first_lanes(rows):
    return lax.broadcasted_iota(jnp.int32, (rows, PAIR), 1) < SIZE


def stacked(pair):
    low = first_lanes(pair.shape[0])
    nothing = jnp.zeros_like(pair)
    return jnp.concatenate([jnp.where(low, pair, nothing), jnp.where(low, nothing, pair)], axis=0)


def unstacked(both):
    rows = both.shape[0] // 2
    return jnp.where(first_lanes(rows), both[:rows], both[rows:])


def norm_factor(wide):
    return lax.rsqrt(jnp.mean(wide * wide, axis=-1, keepdims=True) + epsilon)


def weights_of(q, k, causal):
    length = k.shape[0]
    powers = jnp.exp(dot(stacked(q), k, NT) * (1.0 / math.sqrt(SIZE)))
    if causal:
        query = lax.broadcasted_iota(jnp.int32, powers.shape, 0) % length
        key = lax.broadcasted_iota(jnp.int32, powers.shape, 1)
        powers = jnp.where(query >= key, powers, 0.0)
    return powers / jnp.sum(powers, axis=-1, keepdims=True)


def attend_forward(packed, mixed, weights, sequences, length, causal):
    width = mixed.shape[1]

    def one(n, carry):
        rows = pl.ds(pl.multiple_of(n * length, 16), length)
        for p in range(width // PAIR):
            lanes = p * PAIR
            q = packed[rows, lanes : lanes + PAIR]
            k = packed[rows, width + lanes : width + lanes + PAIR]
            v = packed[rows, 2 * width + lanes : 2 * width + lanes + PAIR]
            w = weights_of(q, k, causal).astype(jnp.bfloat16)
            weights[n, p] = w
            mixed[rows, lanes : lanes + PAIR] = unstacked(dot(w, v)).astype(jnp.bfloat16)
        return carry

    lax.fori_loop(0, sequences, one, 0)


def attend_backward(packed, weights, d_mixed, d_packed, sequences, length):
    width = d_mixed.shape[1]

    def one(n, carry):
        rows = pl.ds(pl.multiple_of(n * length, 16), length)
        for p in range(width // PAIR):
            lanes = p * PAIR
            q = packed[rows, lanes : lanes + PAIR]
            k = packed[rows, width + lanes : width + lanes + PAIR]
            v = packed[rows, 2 * width + lanes : 2 * width + lanes + PAIR]
            up = stacked(d_mixed[rows, lanes : lanes + PAIR])
            w = weights[n, p]
            wide = w.astype(jnp.float32)
            d_w = dot(up, v, NT).astype(jnp.bfloat16).astype(jnp.float32)
            d_scores = wide * (d_w - jnp.sum(d_w * wide, axis=-1, keepdims=True))
            d_scores = (d_scores * (1.0 / math.sqrt(SIZE))).astype(jnp.bfloat16)
            d_q = unstacked(dot(d_scores, k))
            d_k = dot(d_scores, stacked(q), TN)
            d_v = dot(w, up, TN)
            d_packed[rows, lanes : lanes + PAIR] = d_q.astype(jnp.bfloat16)
            d_packed[rows, width + lanes : width + lanes + PAIR] = d_k.astype(jnp.bfloat16)
            d_packed[rows, 2 * width + lanes : 2 * width + lanes + PAIR] = d_v.astype(jnp.bfloat16)
        return carry

    lax.fori_loop(0, sequences, one, 0)


def permuted(order, values):
    rows = order.shape[0]
    lane = lax.broadcasted_iota(jnp.int32, (rows, values.shape[0]), 1)
    onehot = jnp.where(order == lane, 1.0, 0.0).astype(jnp.bfloat16)
    return dot(onehot, values).astype(jnp.bfloat16)


def time_forward_kernel(
    batch, x_ref, row_ref, table_ref, qkv_ref, out_ref, order_ref, sent, normed, packed, weights, mixed, first
):
    sequences, length, width = x_ref.shape
    feeders = sequences // batch
    table_rows = table_ref.shape[0]
    onehot = (row_ref[...] == lax.broadcasted_iota(jnp.int32, (row_ref.shape[0], table_rows), 1)).astype(jnp.bfloat16)
    added = dot(onehot, table_ref[...])
    for n in range(sequences):
        rows = pl.ds(n * length, length)
        start = x_ref[n].astype(jnp.float32) + added[n % feeders : n % feeders + 1]
        first[rows, :] = start
        normed[rows, :] = (start * norm_factor(start)).astype(jnp.bfloat16)
    packed[...] = dot(normed[...], qkv_ref[...]).astype(jnp.bfloat16)
    attend_forward(packed, mixed, weights, sequences, length, True)
    result = (first[...] + dot(mixed[...], out_ref[...])).astype(jnp.bfloat16)
    sent[...] = permuted(order_ref[...], result)


def feed_kernel(
    got_ref, order_ref, back_ref, adjoint_ref, qkv_ref, out_ref,
    load, sent, grad_qkv, grad_out, hidden, normed, packed, weights, mixed, d_mixed, d_packed,
):
    sequences, length, width = load.shape
    hidden[...] = permuted(order_ref[...], got_ref[...])
    wide = hidden[...].astype(jnp.float32)
    normed[...] = (wide * norm_factor(wide)).astype(jnp.bfloat16)
    packed[...] = dot(normed[...], qkv_ref[...]).astype(jnp.bfloat16)
    attend_forward(packed, mixed, weights, sequences, length, False)
    result = hidden[...].astype(jnp.float32) + dot(mixed[...], out_ref[...])
    load[...] = result.astype(jnp.bfloat16).reshape(load.shape)
    up = adjoint_ref[...]
    d_mixed[...] = dot(up, out_ref[...], NT).astype(jnp.bfloat16)
    attend_backward(packed, weights, d_mixed, d_packed, sequences, length)
    g = dot(d_packed[...], qkv_ref[...], NT).astype(jnp.bfloat16).astype(jnp.float32)
    wide = hidden[...].astype(jnp.float32)
    factor = norm_factor(wide)
    along = jnp.sum(g * wide, axis=-1, keepdims=True) * (factor * factor * factor) * (1.0 / width)
    d_hidden = (g * factor - wide * along).astype(jnp.bfloat16)
    total = (d_hidden.astype(jnp.float32) + up.astype(jnp.float32)).astype(jnp.bfloat16)
    sent[...] = permuted(back_ref[...], total)
    grad_out[...] = dot(mixed[...], up, TN).astype(jnp.bfloat16)
    for part in range(3):
        lanes = slice(part * width, (part + 1) * width)
        grad_qkv[part] = dot(normed[...], d_packed[:, lanes], TN).astype(jnp.bfloat16)


def time_backward_kernel(
    got_ref, order_ref, normed, packed, weights, mixed, out_ref, grad_qkv, grad_out, up, d_mixed, d_packed
):
    sequences = weights.shape[0]
    length = weights.shape[3]
    width = mixed.shape[1]
    up[...] = permuted(order_ref[...], got_ref[...])
    d_mixed[...] = dot(up[...], out_ref[...], NT).astype(jnp.bfloat16)
    attend_backward(packed, weights, d_mixed, d_packed, sequences, length)
    grad_out[...] = dot(mixed[...], up[...], TN).astype(jnp.bfloat16)
    for part in range(3):
        lanes = slice(part * width, (part + 1) * width)
        grad_qkv[part] = dot(normed[...], d_packed[:, lanes], TN).astype(jnp.bfloat16)


VMEM = pl.BlockSpec(memory_space=pltpu.VMEM)


def call(kernel, outs, scratch, *args):
    return pl.pallas_call(
        kernel,
        out_shape=tuple(jax.ShapeDtypeStruct(shape, jnp.bfloat16) for shape in outs),
        in_specs=[VMEM] * len(args),
        out_specs=tuple(VMEM for _ in outs),
        scratch_shapes=[pltpu.VMEM(shape, held) for shape, held in scratch],
        compiler_params=pltpu.CompilerParams(vmem_limit_bytes=48 << 20),
    )(*args)


def on_device(
    measured_features,
    feeder_of_row,
    feeder_table,
    time_qkv,
    time_out,
    feed_qkv,
    feed_out,
    adjoint_of_prediction,
    round_index,
):
    batch, feed_local, slot_count, width = measured_features.shape
    feeder_count = adjoint_of_prediction.shape[1]
    slot_local = adjoint_of_prediction.shape[2]
    count = feeder_count // feed_local
    rows = batch * feed_local * slot_count
    pairs = width // PAIR
    bf16 = jnp.bfloat16

    at = jnp.arange(rows, dtype=jnp.int32)
    wire = at.reshape(batch, feed_local, count, slot_local)
    to_wire = wire.transpose(2, 3, 0, 1).reshape(rows, 1)
    wired = at.reshape(count, slot_local, batch, feed_local)
    from_wire = wired.transpose(2, 3, 0, 1).reshape(rows, 1)
    feed = at.reshape(batch, slot_local, count, feed_local)
    feed_to_wire = feed.transpose(2, 1, 0, 3).reshape(rows, 1)
    wire_to_feed = wired.transpose(2, 1, 0, 3).reshape(rows, 1)

    row_column = jnp.pad(feeder_of_row, (0, 8 - feed_local)).reshape(8, 1)
    sequences = batch * feed_local
    sent, normed, packed, weights, mixed = call(
        partial(time_forward_kernel, batch),
        (
            (rows, width),
            (rows, width),
            (rows, 3 * width),
            (sequences, pairs, 2 * slot_count, slot_count),
            (rows, width),
        ),
        (((rows, width), jnp.float32),),
        measured_features.reshape(sequences, slot_count, width),
        row_column,
        feeder_table,
        time_qkv,
        time_out,
        to_wire,
    )
    got = exchange(sent, count, 3)
    groups = batch * slot_local
    upstream = jnp.transpose(adjoint_of_prediction, (0, 2, 1, 3)).reshape(rows, width)
    load, back, feed_grad_qkv, feed_grad_out = call(
        feed_kernel,
        ((groups, feeder_count, width), (rows, width), (3, width, width), (width, width)),
        (
            ((rows, width), bf16),
            ((rows, width), bf16),
            ((rows, 3 * width), bf16),
            ((groups, pairs, 2 * feeder_count, feeder_count), bf16),
            ((rows, width), bf16),
            ((rows, width), bf16),
            ((rows, 3 * width), bf16),
        ),
        got,
        wire_to_feed,
        feed_to_wire,
        upstream,
        feed_qkv,
        feed_out,
    )
    predicted_load = jnp.transpose(
        load.reshape(batch, slot_local, feeder_count, width), (0, 2, 1, 3)
    )
    returned = exchange(back, count, 4)
    time_grad_qkv, time_grad_out = call(
        time_backward_kernel,
        ((3, width, width), (width, width)),
        (
            ((rows, width), bf16),
            ((rows, width), bf16),
            ((rows, 3 * width), bf16),
        ),
        returned,
        from_wire,
        normed,
        packed,
        weights,
        mixed,
        time_out,
    )
    parts = [time_grad_qkv, time_grad_out[None], feed_grad_qkv, feed_grad_out[None]]
    local_grads = jnp.concatenate(parts, axis=0).reshape(-1, width)
    tiles = local_grads.reshape(512, 8, 4, LANES).transpose(0, 2, 1, 3).reshape(-1, LANES)
    mean = pair_mean(tiles, round_index)
    mean = mean.reshape(512, 4, 8, LANES).transpose(0, 2, 1, 3).reshape(8, width, width)
    mean = mean.astype(jnp.float32)
    pieces = [
        mean[0:3].transpose(1, 0, 2).reshape(-1, width),
        mean[3],
        mean[4:7].transpose(1, 0, 2).reshape(-1, width),
        mean[7],
    ]
    return (predicted_load, jnp.concatenate(pieces, axis=0)[None])


def solution(mesh):
    placed = (
        P("gossip", "field", None, None),
        P("field"),
        P(),
        P(),
        P(),
        P(),
        P(),
        P("gossip", None, "field", None),
        P(),
    )
    return jax.shard_map(
        on_device,
        mesh=mesh,
        in_specs=placed,
        out_specs=(P("gossip", None, "field", None), P("gossip", None, None)),
        check_vma=False,
    )
```

```python
from functools import partial
import math

import jax
import jax.numpy as jnp
from jax import lax
from jax.experimental import pallas as pl
from jax.experimental.pallas import tpu as pltpu
from jax.sharding import PartitionSpec as P

epsilon = 1e-05


MESH = pl.DeviceIdType.MESH
LANES = 128
UNIT = 1024


def coordinates():
    gossip = lax.axis_index("gossip")
    field = lax.axis_index("field")
    x_hi, core = gossip // 2, gossip % 2
    x_lo, z, y = field // 16, (field // 4) % 4, field % 4

    def at(x_hi, core, x_lo, z, y):
        return (x_hi * 2 + core, (x_lo * 4 + z) * 4 + y)

    def even(position):
        return position + 1 - 2 * (position % 2)

    return {
        "ya": (((y + 1) // 2) % 2, at(x_hi, core, x_lo, z, even(y))),
        "yb": (y // 2, at(x_hi, core, x_lo, z, 3 - y)),
        "za": (((z + 1) // 2) % 2, at(x_hi, core, x_lo, even(z), y)),
        "zb": (z // 2, at(x_hi, core, x_lo, 3 - z, y)),
        "xa": ((x_hi + x_lo) % 2, at(x_hi, core, 1 - x_lo, z, y)),
        "xb": (x_hi, at(1 - x_hi, core, 1 - x_lo, z, y)),
        "core": (core, at(x_hi, 1 - core, x_lo, z, y)),
    }


def block_of(rows):
    for parts in range(1, rows + 1):
        if rows % parts == 0 and rows // parts <= 256 and (rows // parts) % 16 == 0:
            return rows // parts
    return rows


def reduce_kernel(chains, used, g_ref, out_ref, acc, full, inbox, rs_send, rs_recv, ag_send, ag_recv, out_sem):
    links = coordinates()
    barrier = pltpu.get_barrier_semaphore()
    for name in used:
        pl.semaphore_signal(barrier, inc=1, device_id=links[name][1], device_id_type=MESH)
    pl.semaphore_wait(barrier, len(used))

    steps = len(used)
    state = []
    for start, wave, order in chains:
        state.append({"at": [start], "start": start})

    def halves(j, s):
        start, wave, order = chains[j]
        bit, peer = links[order[s]]
        rows = UNIT >> (s + 1)
        base = state[j]["at"][s]
        return base + bit * rows, base + (1 - bit) * rows, rows, peer

    def rs_copy(j, s):
        keep, leave, rows, peer = halves(j, s)
        source = g_ref if s == 0 else acc
        slot = chains[j][0] + UNIT - 2 * rows
        return pltpu.make_async_remote_copy(
            src_ref=source.at[pl.ds(pl.multiple_of(leave, 16), rows)],
            dst_ref=inbox.at[pl.ds(slot, rows)],
            send_sem=rs_send.at[j, s],
            recv_sem=rs_recv.at[j, s],
            device_id=peer,
            device_id_type=MESH,
        )

    def rs_add(j, s):
        keep, leave, rows, peer = halves(j, s)
        slot = chains[j][0] + UNIT - 2 * rows
        source = g_ref if s == 0 else acc
        target = full if s == steps - 1 else acc
        block = block_of(rows)

        def add(i, carry):
            here = pl.ds(pl.multiple_of(keep + i * block, 16), block)
            there = pl.ds(pl.multiple_of(slot + i * block, 16), block)
            total = source[here, :].astype(jnp.float32) + inbox[there, :].astype(jnp.float32)
            if s == steps - 1:
                total = total * 0.5
            target[here, :] = total.astype(jnp.bfloat16)
            return carry

        lax.fori_loop(0, rows // block, add, 0)
        state[j]["at"].append(keep)

    def ag_copy(j, s):
        keep, leave, rows, peer = halves(j, s)
        mine = full.at[pl.ds(pl.multiple_of(keep, 16), rows)]
        return pltpu.make_async_remote_copy(
            src_ref=mine,
            dst_ref=mine,
            send_sem=ag_send.at[j, s],
            recv_sem=ag_recv.at[j, s],
            device_id=peer,
            device_id_type=MESH,
        )

    for j in range(len(chains)):
        rs_copy(j, 0).start()
    waves = 1 + max(chain[1] for chain in chains)
    for turn in range(2 * steps + waves - 1):
        for wave in range(waves):
            stage = turn - wave
            if not 0 <= stage < 2 * steps:
                continue
            for j in range(len(chains)):
                if chains[j][1] != wave:
                    continue
                if stage < steps:
                    rs_copy(j, stage).wait()
                    rs_add(j, stage)
                    if stage + 1 < steps:
                        rs_copy(j, stage + 1).start()
                    else:
                        ag_copy(j, steps - 1).start()
                else:
                    s = 2 * steps - 1 - stage
                    ag_copy(j, s).wait()
                    if s > 0:
                        ag_copy(j, s - 1).start()
                    else:
                        part = pl.ds(chains[j][0], UNIT)
                        pltpu.make_async_copy(full.at[part], out_ref.at[part], out_sem.at[j]).start()
    for j in range(len(chains)):
        part = pl.ds(chains[j][0], UNIT)
        pltpu.make_async_copy(full.at[part], out_ref.at[part], out_sem.at[j]).wait()


def reduce_over(first, links, collective_id):
    used = tuple(first) + tuple(links)

    def run(g):
        rows = g.shape[0]
        count = rows // UNIT
        chains = []
        for j in range(count):
            turn = j % len(links)
            order = tuple(first) + tuple(links[(turn + s) % len(links)] for s in range(len(links)))
            chains.append((j * UNIT, j // len(links), order))
        steps = len(used)
        return pl.pallas_call(
            partial(reduce_kernel, tuple(chains), used),
            out_shape=jax.ShapeDtypeStruct(g.shape, jnp.bfloat16),
            in_specs=[pl.BlockSpec(memory_space=pltpu.VMEM)],
            out_specs=pl.BlockSpec(memory_space=pl.ANY),
            scratch_shapes=[
                pltpu.VMEM(g.shape, jnp.bfloat16),
                pltpu.VMEM(g.shape, jnp.bfloat16),
                pltpu.VMEM(g.shape, jnp.bfloat16),
                pltpu.SemaphoreType.DMA((count, steps)),
                pltpu.SemaphoreType.DMA((count, steps)),
                pltpu.SemaphoreType.DMA((count, steps)),
                pltpu.SemaphoreType.DMA((count, steps)),
                pltpu.SemaphoreType.DMA((count,)),
            ],
            compiler_params=pltpu.CompilerParams(
                collective_id=collective_id, has_side_effects=True, vmem_limit_bytes=40 << 20
            ),
        )(g)

    return run


def pair_mean(g, round_index):
    links = ("ya", "za", "xa", "yb", "zb")
    return lax.cond(
        round_index[0] == 0,
        reduce_over(("core",), links, 1),
        reduce_over((), links + ("xb",), 2),
        g,
    )


def exchange_kernel(count, send_ref, got_ref, send_sem, recv_sem, own_sem):
    gossip = lax.axis_index("gossip")
    me = lax.axis_index("field")
    rows = send_ref.shape[0] // count

    def block(i):
        return pl.ds(pl.multiple_of(i * rows, 8), rows)

    def peer(i):
        return (gossip, lax.rem(me + i, count))

    barrier = pltpu.get_barrier_semaphore()

    def greet(i, carry):
        pl.semaphore_signal(barrier, inc=1, device_id=peer(i), device_id_type=MESH)
        return carry

    lax.fori_loop(1, count, greet, 0)
    own = pltpu.make_async_copy(send_ref.at[block(me)], got_ref.at[block(me)], own_sem)
    own.start()
    pl.semaphore_wait(barrier, count - 1)

    def copy(i):
        to = lax.rem(me + i, count)
        return pltpu.make_async_remote_copy(
            src_ref=send_ref.at[block(to)],
            dst_ref=got_ref.at[block(me)],
            send_sem=send_sem.at[i],
            recv_sem=recv_sem.at[i],
            device_id=(gossip, to),
            device_id_type=MESH,
        )

    def start(i, carry):
        copy(i).start()
        return carry

    def finish(i, carry):
        copy(i).wait()
        return carry

    lax.fori_loop(1, count, start, 0)
    lax.fori_loop(1, count, finish, 0)
    own.wait()


def exchange(blocks, count, collective_id):
    return pl.pallas_call(
        partial(exchange_kernel, count),
        out_shape=jax.ShapeDtypeStruct(blocks.shape, blocks.dtype),
        in_specs=[pl.BlockSpec(memory_space=pltpu.VMEM)],
        out_specs=pl.BlockSpec(memory_space=pltpu.VMEM),
        scratch_shapes=[
            pltpu.SemaphoreType.DMA((count,)),
            pltpu.SemaphoreType.DMA((count,)),
            pltpu.SemaphoreType.DMA(()),
        ],
        compiler_params=pltpu.CompilerParams(collective_id=collective_id, has_side_effects=True),
    )(blocks)


SIZE = 64
PAIR = 2 * SIZE


def dot(a, b, contract=((1,), (0,))):
    return lax.dot_general(a, b, (contract, ((), ())), preferred_element_type=jnp.float32)


NT = ((1,), (1,))
TN = ((0,), (0,))


def first_lanes(rows):
    return lax.broadcasted_iota(jnp.int32, (rows, PAIR), 1) < SIZE


def stacked(pair):
    low = first_lanes(pair.shape[0])
    nothing = jnp.zeros_like(pair)
    return jnp.concatenate([jnp.where(low, pair, nothing), jnp.where(low, nothing, pair)], axis=0)


def unstacked(both):
    rows = both.shape[0] // 2
    return jnp.where(first_lanes(rows), both[:rows], both[rows:])


def norm_factor(wide):
    return lax.rsqrt(jnp.mean(wide * wide, axis=-1, keepdims=True) + epsilon)


def weights_of(q, k, causal):
    length = k.shape[0]
    powers = jnp.exp(dot(stacked(q), k, NT) * (1.0 / math.sqrt(SIZE)))
    if causal:
        query = lax.broadcasted_iota(jnp.int32, powers.shape, 0) % length
        key = lax.broadcasted_iota(jnp.int32, powers.shape, 1)
        powers = jnp.where(query >= key, powers, 0.0)
    return powers / jnp.sum(powers, axis=-1, keepdims=True)


def attend_forward(packed, mixed, weights, sequences, length, causal):
    width = mixed.shape[1]

    def one(n, carry):
        rows = pl.ds(pl.multiple_of(n * length, 16), length)
        for p in range(width // PAIR):
            lanes = p * PAIR
            q = packed[rows, lanes : lanes + PAIR]
            k = packed[rows, width + lanes : width + lanes + PAIR]
            v = packed[rows, 2 * width + lanes : 2 * width + lanes + PAIR]
            w = weights_of(q, k, causal).astype(jnp.bfloat16)
            weights[n, p] = w
            mixed[rows, lanes : lanes + PAIR] = unstacked(dot(w, v)).astype(jnp.bfloat16)
        return carry

    lax.fori_loop(0, sequences, one, 0)


def attend_backward(packed, weights, d_mixed, d_packed, sequences, length):
    width = d_mixed.shape[1]

    def one(n, carry):
        rows = pl.ds(pl.multiple_of(n * length, 16), length)
        for p in range(width // PAIR):
            lanes = p * PAIR
            q = packed[rows, lanes : lanes + PAIR]
            k = packed[rows, width + lanes : width + lanes + PAIR]
            v = packed[rows, 2 * width + lanes : 2 * width + lanes + PAIR]
            up = stacked(d_mixed[rows, lanes : lanes + PAIR])
            w = weights[n, p]
            wide = w.astype(jnp.float32)
            d_w = dot(up, v, NT).astype(jnp.bfloat16).astype(jnp.float32)
            d_scores = wide * (d_w - jnp.sum(d_w * wide, axis=-1, keepdims=True))
            d_scores = (d_scores * (1.0 / math.sqrt(SIZE))).astype(jnp.bfloat16)
            d_q = unstacked(dot(d_scores, k))
            d_k = dot(d_scores, stacked(q), TN)
            d_v = dot(w, up, TN)
            d_packed[rows, lanes : lanes + PAIR] = d_q.astype(jnp.bfloat16)
            d_packed[rows, width + lanes : width + lanes + PAIR] = d_k.astype(jnp.bfloat16)
            d_packed[rows, 2 * width + lanes : 2 * width + lanes + PAIR] = d_v.astype(jnp.bfloat16)
        return carry

    lax.fori_loop(0, sequences, one, 0)


def permuted(order, values):
    rows = order.shape[0]
    lane = lax.broadcasted_iota(jnp.int32, (rows, values.shape[0]), 1)
    onehot = jnp.where(order == lane, 1.0, 0.0).astype(jnp.bfloat16)
    return dot(onehot, values).astype(jnp.bfloat16)


def store_gradients(grads, normed, d_packed, mixed, up):
    slabs, parts, width, lanes = grads.shape
    for part in range(parts):
        if part < 3:
            total = dot(normed[...], d_packed[:, part * width : (part + 1) * width], TN)
        else:
            total = dot(mixed[...], up, TN)
        for slab in range(slabs):
            grads[slab, part] = total[:, slab * lanes : (slab + 1) * lanes].astype(jnp.bfloat16)


def time_forward_kernel(
    batch, x_ref, row_ref, table_ref, qkv_ref, out_ref, order_ref, sent, normed, packed, weights, mixed, first
):
    sequences, length, width = x_ref.shape
    feeders = sequences // batch
    table_rows = table_ref.shape[0]
    onehot = (row_ref[...] == lax.broadcasted_iota(jnp.int32, (row_ref.shape[0], table_rows), 1)).astype(jnp.bfloat16)
    added = dot(onehot, table_ref[...])
    for n in range(sequences):
        rows = pl.ds(n * length, length)
        start = x_ref[n].astype(jnp.float32) + added[n % feeders : n % feeders + 1]
        first[rows, :] = start
        normed[rows, :] = (start * norm_factor(start)).astype(jnp.bfloat16)
    packed[...] = dot(normed[...], qkv_ref[...]).astype(jnp.bfloat16)
    attend_forward(packed, mixed, weights, sequences, length, True)
    result = (first[...] + dot(mixed[...], out_ref[...])).astype(jnp.bfloat16)
    sent[...] = permuted(order_ref[...], result)


def feed_kernel(
    got_ref, order_ref, back_ref, adjoint_ref, qkv_ref, out_ref,
    load, sent, grads, hidden, normed, packed, weights, mixed, d_mixed, d_packed,
):
    sequences, length, width = load.shape
    hidden[...] = permuted(order_ref[...], got_ref[...])
    wide = hidden[...].astype(jnp.float32)
    normed[...] = (wide * norm_factor(wide)).astype(jnp.bfloat16)
    packed[...] = dot(normed[...], qkv_ref[...]).astype(jnp.bfloat16)
    attend_forward(packed, mixed, weights, sequences, length, False)
    result = hidden[...].astype(jnp.float32) + dot(mixed[...], out_ref[...])
    load[...] = result.astype(jnp.bfloat16).reshape(load.shape)
    up = adjoint_ref[...]
    d_mixed[...] = dot(up, out_ref[...], NT).astype(jnp.bfloat16)
    attend_backward(packed, weights, d_mixed, d_packed, sequences, length)
    g = dot(d_packed[...], qkv_ref[...], NT).astype(jnp.bfloat16).astype(jnp.float32)
    wide = hidden[...].astype(jnp.float32)
    factor = norm_factor(wide)
    along = jnp.sum(g * wide, axis=-1, keepdims=True) * (factor * factor * factor) * (1.0 / width)
    d_hidden = (g * factor - wide * along).astype(jnp.bfloat16)
    total = (d_hidden.astype(jnp.float32) + up.astype(jnp.float32)).astype(jnp.bfloat16)
    sent[...] = permuted(back_ref[...], total)
    store_gradients(grads, normed, d_packed, mixed, up)


def time_backward_kernel(
    got_ref, order_ref, normed, packed, weights, mixed, out_ref, grads, up, d_mixed, d_packed
):
    sequences = weights.shape[0]
    length = weights.shape[3]
    width = mixed.shape[1]
    up[...] = permuted(order_ref[...], got_ref[...])
    d_mixed[...] = dot(up[...], out_ref[...], NT).astype(jnp.bfloat16)
    attend_backward(packed, weights, d_mixed, d_packed, sequences, length)
    store_gradients(grads, normed, d_packed, mixed, up[...])


def finish_kernel(mean_ref, out_ref, wide, sem):
    layers, slabs, parts, depth, lanes = mean_ref.shape
    rows = parts * depth
    copies = []
    for layer in range(layers):
        for slab in range(slabs):
            target = wide.at[layer * slabs + slab]
            columns = pl.ds(slab * lanes, lanes)
            for part in range(3):
                target[pl.ds(part, depth, stride=3), :] = mean_ref[layer, slab, part].astype(jnp.float32)
            target[3 * depth :, :] = mean_ref[layer, slab, 3].astype(jnp.float32)
            copies.append(
                pltpu.make_async_copy(
                    target, out_ref.at[pl.ds(layer * rows, rows), columns], sem.at[layer * slabs + slab]
                )
            )
            copies[-1].start()
    for copy in copies:
        copy.wait()


def finished(mean):
    layers, slabs, parts, depth, lanes = mean.shape
    shape = (layers * parts * depth, slabs * lanes)
    return pl.pallas_call(
        finish_kernel,
        out_shape=jax.ShapeDtypeStruct(shape, jnp.float32),
        in_specs=[pl.BlockSpec(memory_space=pltpu.VMEM)],
        out_specs=pl.BlockSpec(memory_space=pl.ANY),
        scratch_shapes=[pltpu.VMEM((layers * slabs, parts * depth, lanes), jnp.float32), pltpu.SemaphoreType.DMA((layers * slabs,))],
        compiler_params=pltpu.CompilerParams(vmem_limit_bytes=32 << 20),
    )(mean)


VMEM = pl.BlockSpec(memory_space=pltpu.VMEM)


def call(kernel, outs, scratch, *args):
    return pl.pallas_call(
        kernel,
        out_shape=tuple(jax.ShapeDtypeStruct(shape, jnp.bfloat16) for shape in outs),
        in_specs=[VMEM] * len(args),
        out_specs=tuple(VMEM for _ in outs),
        scratch_shapes=[pltpu.VMEM(shape, held) for shape, held in scratch],
        compiler_params=pltpu.CompilerParams(vmem_limit_bytes=48 << 20),
    )(*args)


def on_device(
    measured_features,
    feeder_of_row,
    feeder_table,
    time_qkv,
    time_out,
    feed_qkv,
    feed_out,
    adjoint_of_prediction,
    round_index,
):
    batch, feed_local, slot_count, width = measured_features.shape
    feeder_count = adjoint_of_prediction.shape[1]
    slot_local = adjoint_of_prediction.shape[2]
    count = feeder_count // feed_local
    rows = batch * feed_local * slot_count
    pairs = width // PAIR
    bf16 = jnp.bfloat16

    at = jnp.arange(rows, dtype=jnp.int32)
    wire = at.reshape(batch, feed_local, count, slot_local)
    to_wire = wire.transpose(2, 3, 0, 1).reshape(rows, 1)
    wired = at.reshape(count, slot_local, batch, feed_local)
    from_wire = wired.transpose(2, 3, 0, 1).reshape(rows, 1)
    feed = at.reshape(batch, slot_local, count, feed_local)
    feed_to_wire = feed.transpose(2, 1, 0, 3).reshape(rows, 1)
    wire_to_feed = wired.transpose(2, 1, 0, 3).reshape(rows, 1)

    row_column = jnp.pad(feeder_of_row, (0, 8 - feed_local)).reshape(8, 1)
    sequences = batch * feed_local
    sent, normed, packed, weights, mixed = call(
        partial(time_forward_kernel, batch),
        (
            (rows, width),
            (rows, width),
            (rows, 3 * width),
            (sequences, pairs, 2 * slot_count, slot_count),
            (rows, width),
        ),
        (((rows, width), jnp.float32),),
        measured_features.reshape(sequences, slot_count, width),
        row_column,
        feeder_table,
        time_qkv,
        time_out,
        to_wire,
    )
    slabs = (width // LANES, 4, width, LANES)
    got = exchange(sent, count, 3)
    groups = batch * slot_local
    upstream = jnp.transpose(adjoint_of_prediction, (0, 2, 1, 3)).reshape(rows, width)
    load, back, feed_grads = call(
        feed_kernel,
        ((groups, feeder_count, width), (rows, width), slabs),
        (
            ((rows, width), bf16),
            ((rows, width), bf16),
            ((rows, 3 * width), bf16),
            ((groups, pairs, 2 * feeder_count, feeder_count), bf16),
            ((rows, width), bf16),
            ((rows, width), bf16),
            ((rows, 3 * width), bf16),
        ),
        got,
        wire_to_feed,
        feed_to_wire,
        upstream,
        feed_qkv,
        feed_out,
    )
    predicted_load = jnp.transpose(
        load.reshape(batch, slot_local, feeder_count, width), (0, 2, 1, 3)
    )
    returned = exchange(back, count, 4)
    (time_grads,) = call(
        time_backward_kernel,
        (slabs,),
        (
            ((rows, width), bf16),
            ((rows, width), bf16),
            ((rows, 3 * width), bf16),
        ),
        returned,
        from_wire,
        normed,
        packed,
        weights,
        mixed,
        time_out,
    )
    grads = jnp.stack([time_grads, feed_grads])
    mean = pair_mean(grads.reshape(-1, LANES), round_index).reshape(grads.shape)
    return (predicted_load, finished(mean)[None])


def solution(mesh):
    placed = (
        P("gossip", "field", None, None),
        P("field"),
        P(),
        P(),
        P(),
        P(),
        P(),
        P("gossip", None, "field", None),
        P(),
    )
    return jax.shard_map(
        on_device,
        mesh=mesh,
        in_specs=placed,
        out_specs=(P("gossip", None, "field", None), P("gossip", None, None)),
        check_vma=False,
    )
```

```python
from functools import partial
import math

import jax
import jax.numpy as jnp
import numpy as np
from jax import lax
from jax.experimental import pallas as pl
from jax.experimental.pallas import tpu as pltpu
from jax.sharding import PartitionSpec as P

epsilon = 1e-05


MESH = pl.DeviceIdType.MESH
LANES = 128
LINKS = ("ya", "za", "xa", "yb", "zb")
PAIRS = ("core", "xb")
GROUPS = (1, 2, 2)
STEPS = len(GROUPS)
TURNS = 2 * STEPS + 1
COPIES = sum(2**size - 1 for size in GROUPS)


class Place:
    def __init__(self):
        gossip, field = lax.axis_index("gossip"), lax.axis_index("field")
        x_hi, core = gossip // 2, gossip % 2
        x_lo, z, y = field // 16, (field // 4) % 4, field % 4
        self.here = {"x_hi": x_hi, "core": core, "x_lo": x_lo, "z": z, "y": y}
        self.bit = {
            "ya": ((y + 1) // 2) % 2,
            "yb": y // 2,
            "za": ((z + 1) // 2) % 2,
            "zb": z // 2,
            "xa": (x_hi + x_lo) % 2,
        }
        self.flip = {
            "ya": {"y": y + 1 - 2 * (y % 2)},
            "yb": {"y": 3 - y},
            "za": {"z": z + 1 - 2 * (z % 2)},
            "zb": {"z": 3 - z},
            "xa": {"x_lo": 1 - x_lo},
            "xb": {"x_hi": 1 - x_hi, "x_lo": 1 - x_lo},
            "core": {"core": 1 - core},
        }

    def across(self, *names):
        at = dict(self.here)
        for name in names:
            at.update(self.flip[name])
        return (at["x_hi"] * 2 + at["core"], (at["x_lo"] * 4 + at["z"]) * 4 + at["y"])


def chains_of(rows):
    unit = 512
    count, more = divmod(rows // unit, len(LINKS))
    chains, first = [], 0
    for turn in range(len(LINKS)):
        names = [LINKS[(turn + s) % len(LINKS)] for s in range(len(LINKS))]
        groups = tuple(tuple(names[sum(GROUPS[:s]) : sum(GROUPS[: s + 1])]) for s in range(STEPS))
        size = (count + (turn < more)) * unit
        chains.append((first, size, groups))
        first += size
    assert first == rows
    return chains


def block_of(rows):
    for parts in range(1, rows + 1):
        if rows % parts == 0 and rows // parts <= 256 and (rows // parts) % 16 == 0:
            return rows // parts
    return rows


class Reduction:
    def __init__(self, place, partner, g, inbox, pairbox, full, out, sems):
        self.place, self.partner = place, partner
        self.g, self.inbox, self.pairbox, self.full, self.out = g, inbox, pairbox, full, out
        self.rs_send, self.rs_recv, self.pair_send, self.pair_recv, self.ag_send, self.ag_recv, self.out_sem = sems
        self.chains = chains_of(g.shape[0])
        self.at = []
        self.steps = []
        for first, rows, groups in self.chains:
            at, size, sem, steps = [first], rows, 0, []
            for names in groups:
                part = size >> len(names)
                peers = []
                for mask in range(1, 2 ** len(names)):
                    flipped = [name for n, name in enumerate(names) if mask >> n & 1]
                    offset = at[-1]
                    for n, name in enumerate(names):
                        bit = place.bit[name]
                        offset = offset + (1 - bit if name in flipped else bit) * (size >> (n + 1))
                    slot = first + rows - size + (mask - 1) * part
                    peers.append((place.across(*flipped), offset, slot, sem))
                    sem += 1
                mine = at[-1]
                for n, name in enumerate(names):
                    mine = mine + place.bit[name] * (size >> (n + 1))
                steps.append((part, peers))
                at.append(mine)
                size = part
            self.at.append(at)
            self.steps.append(steps)

    def rs_copies(self, j, s):
        part, peers = self.steps[j][s]
        return [
            pltpu.make_async_remote_copy(
                src_ref=self.g.at[pl.ds(pl.multiple_of(offset, 16), part)],
                dst_ref=self.inbox.at[pl.ds(slot, part)],
                send_sem=self.rs_send.at[j, sem],
                recv_sem=self.rs_recv.at[j, sem],
                device_id=peer,
                device_id_type=MESH,
            )
            for peer, offset, slot, sem in peers
        ]

    def rs_add(self, j, s):
        part, peers = self.steps[j][s]
        keep = self.at[j][s + 1]
        block = block_of(part)

        def add(i, carry):
            here = pl.ds(pl.multiple_of(keep + i * block, 16), block)
            total = self.g[here, :].astype(jnp.float32)
            for peer, offset, slot, sem in peers:
                there = pl.ds(pl.multiple_of(slot + i * block, 16), block)
                total = total + self.inbox[there, :].astype(jnp.float32)
            self.g[here, :] = total.astype(jnp.bfloat16)
            return carry

        lax.fori_loop(0, part // block, add, 0)

    def shard(self, j):
        first, rows, groups = self.chains[j]
        count = rows >> len(LINKS)
        return pl.ds(pl.multiple_of(self.at[j][STEPS], 16), count), pl.ds(first >> len(LINKS), count)

    def pair_copy(self, j, n):
        here, there = self.shard(j)
        return pltpu.make_async_remote_copy(
            src_ref=self.g.at[here],
            dst_ref=self.pairbox.at[n, there],
            send_sem=self.pair_send.at[j, n],
            recv_sem=self.pair_recv.at[j, n],
            device_id=self.place.across(PAIRS[n]),
            device_id_type=MESH,
        )

    def pair_mean(self, j):
        here, there = self.shard(j)
        other = jnp.where(
            self.partner[0:1, :] > 0.0,
            self.pairbox[1, there, :].astype(jnp.float32),
            self.pairbox[0, there, :].astype(jnp.float32),
        )
        self.full[here, :] = ((self.g[here, :].astype(jnp.float32) + other) * 0.5).astype(jnp.bfloat16)

    def ag_copies(self, j, s):
        part, peers = self.steps[j][s]
        mine = self.full.at[pl.ds(pl.multiple_of(self.at[j][s + 1], 16), part)]
        return [
            pltpu.make_async_remote_copy(
                src_ref=mine,
                dst_ref=mine,
                send_sem=self.ag_send.at[j, sem],
                recv_sem=self.ag_recv.at[j, sem],
                device_id=peer,
                device_id_type=MESH,
            )
            for peer, offset, slot, sem in peers
        ]

    def out_copy(self, j):
        part = pl.ds(self.chains[j][0], self.chains[j][1])
        return pltpu.make_async_copy(self.full.at[part], self.out.at[part], self.out_sem.at[j])

    def start(self, begin, end):
        for j, (first, rows, groups) in enumerate(self.chains):
            if begin < first + rows <= end:
                for copy in self.rs_copies(j, 0):
                    copy.start()

    def turn(self, t, chains=None):
        if 0 <= t < TURNS:
            for j in range(len(self.chains)) if chains is None else chains:
                self.advance(j, t)

    def advance(self, j, stage):
        following = []
        if stage < STEPS:
            for copy in self.rs_copies(j, stage):
                copy.wait()
            self.rs_add(j, stage)
            if stage + 1 < STEPS:
                following = self.rs_copies(j, stage + 1)
            else:
                following = [self.pair_copy(j, n) for n in range(len(PAIRS))]
        elif stage == STEPS:
            for n in range(len(PAIRS)):
                self.pair_copy(j, n).wait()
            self.pair_mean(j)
            following = self.ag_copies(j, STEPS - 1)
        else:
            s = 2 * STEPS - stage
            for copy in self.ag_copies(j, s):
                copy.wait()
            following = self.ag_copies(j, s - 1) if s > 0 else [self.out_copy(j)]
        for copy in following:
            copy.start()

    def finish(self):
        for j in range(len(self.chains)):
            self.out_copy(j).wait()


class Exchange:
    def __init__(self, count, send, got, send_sem, recv_sem, own_sem):
        self.count, self.send, self.got = count, send, got
        self.send_sem, self.recv_sem, self.own_sem = send_sem, recv_sem, own_sem
        self.gossip, self.me = lax.axis_index("gossip"), lax.axis_index("field")
        self.rows = send.shape[0] // count

    def block(self, i):
        return pl.ds(pl.multiple_of(i * self.rows, 8), self.rows)

    def own(self):
        here = self.block(self.me)
        return pltpu.make_async_copy(self.send.at[here], self.got.at[here], self.own_sem)

    def copy(self, i):
        to = lax.rem(self.me + i, self.count)
        return pltpu.make_async_remote_copy(
            src_ref=self.send.at[self.block(to)],
            dst_ref=self.got.at[self.block(self.me)],
            send_sem=self.send_sem.at[i],
            recv_sem=self.recv_sem.at[i],
            device_id=(self.gossip, to),
            device_id_type=MESH,
        )

    def start(self):
        def one(i, carry):
            self.copy(i).start()
            return carry

        lax.fori_loop(1, self.count, one, 0)
        self.own().start()

    def wait(self):
        def one(i, carry):
            self.copy(i).wait()
            return carry

        lax.fori_loop(1, self.count, one, 0)
        self.own().wait()


def greet(place, count):
    barrier = pltpu.get_barrier_semaphore()
    gossip, me = lax.axis_index("gossip"), lax.axis_index("field")

    def one(i, carry):
        peer = (gossip, lax.rem(me + i, count))
        pl.semaphore_signal(barrier, inc=1, device_id=peer, device_id_type=MESH)
        return carry

    lax.fori_loop(1, count, one, 0)
    for name in PAIRS:
        pl.semaphore_signal(barrier, inc=1, device_id=place.across(name), device_id_type=MESH)


def all_greeted(count):
    pl.semaphore_wait(pltpu.get_barrier_semaphore(), count - 1 + len(PAIRS))


SIZE = 64
PAIR = 2 * SIZE


def dot(a, b, contract=((1,), (0,))):
    return lax.dot_general(a, b, (contract, ((), ())), preferred_element_type=jnp.float32)


NT = ((1,), (1,))
TN = ((0,), (0,))


def first_lanes(rows):
    return lax.broadcasted_iota(jnp.int32, (rows, PAIR), 1) < SIZE


def stacked(pair):
    low = first_lanes(pair.shape[0])
    nothing = jnp.zeros_like(pair)
    return jnp.concatenate([jnp.where(low, pair, nothing), jnp.where(low, nothing, pair)], axis=0)


def unstacked(both):
    rows = both.shape[0] // 2
    return jnp.where(first_lanes(rows), both[:rows], both[rows:])


def norm_factor(wide):
    return lax.rsqrt(jnp.mean(wide * wide, axis=-1, keepdims=True) + epsilon)


def weights_of(q, k, causal):
    length = k.shape[0]
    powers = jnp.exp(dot(stacked(q), k, NT) * (1.0 / math.sqrt(SIZE)))
    if causal:
        query = lax.broadcasted_iota(jnp.int32, powers.shape, 0) % length
        key = lax.broadcasted_iota(jnp.int32, powers.shape, 1)
        powers = jnp.where(query >= key, powers, 0.0)
    return powers / jnp.sum(powers, axis=-1, keepdims=True)


def attend_forward(packed, mixed, weights, begin, end, causal):
    length = weights.shape[3]
    width = mixed.shape[1]

    def one(n, carry):
        rows = pl.ds(pl.multiple_of(n * length, 16), length)
        for p in range(width // PAIR):
            lanes = p * PAIR
            q = packed[rows, lanes : lanes + PAIR]
            k = packed[rows, width + lanes : width + lanes + PAIR]
            v = packed[rows, 2 * width + lanes : 2 * width + lanes + PAIR]
            w = weights_of(q, k, causal).astype(jnp.bfloat16)
            weights[n, p] = w
            mixed[rows, lanes : lanes + PAIR] = unstacked(dot(w, v)).astype(jnp.bfloat16)
        return carry

    lax.fori_loop(begin, end, one, 0)


def attend_backward(packed, weights, d_mixed, d_packed, begin, end):
    length = weights.shape[3]
    width = d_mixed.shape[1]

    def one(n, carry):
        rows = pl.ds(pl.multiple_of(n * length, 16), length)
        for p in range(width // PAIR):
            lanes = p * PAIR
            q = packed[rows, lanes : lanes + PAIR]
            k = packed[rows, width + lanes : width + lanes + PAIR]
            v = packed[rows, 2 * width + lanes : 2 * width + lanes + PAIR]
            up = stacked(d_mixed[rows, lanes : lanes + PAIR])
            w = weights[n, p]
            wide = w.astype(jnp.float32)
            d_w = dot(up, v, NT).astype(jnp.bfloat16).astype(jnp.float32)
            d_scores = wide * (d_w - jnp.sum(d_w * wide, axis=-1, keepdims=True))
            d_scores = (d_scores * (1.0 / math.sqrt(SIZE))).astype(jnp.bfloat16)
            d_q = unstacked(dot(d_scores, k))
            d_k = dot(d_scores, stacked(q), TN)
            d_v = dot(w, up, TN)
            d_packed[rows, lanes : lanes + PAIR] = d_q.astype(jnp.bfloat16)
            d_packed[rows, width + lanes : width + lanes + PAIR] = d_k.astype(jnp.bfloat16)
            d_packed[rows, 2 * width + lanes : 2 * width + lanes + PAIR] = d_v.astype(jnp.bfloat16)
        return carry

    lax.fori_loop(begin, end, one, 0)


def selected(targets, rows, values):
    onehot = jnp.where(targets == lax.broadcasted_iota(jnp.int32, (rows, values.shape[0]), 0), 1.0, 0.0)
    return dot(onehot.astype(jnp.bfloat16), values)


def packed_rows(wire, at, values, block):
    rows, width = wire.shape[0], values.shape[1]
    tokens = values.shape[0]
    half = width // 2
    wire[:, :width] = selected(at[0:1, :tokens], rows, values).astype(jnp.bfloat16)
    low = selected(at[1:2, :tokens], rows, values[:, :half])
    high = selected(at[2:3, :tokens], rows, values[:, half:])
    wire[:, width:] = (low + high).astype(jnp.bfloat16)


def unpacked_rows(wire, at, tokens, width):
    rows = wire.shape[0]
    main = selected(at[0:1, :rows], tokens, wire[:, :width])
    low = selected(at[1:2, :rows], tokens, wire[:, width:])
    high = selected(at[2:3, :rows], tokens, wire[:, width:])
    return (main + jnp.concatenate([low, high], axis=1)).astype(jnp.bfloat16)


def routes(slots, count, feeders):
    device, slot, feeder = np.meshgrid(np.arange(count), np.arange(slots), np.arange(feeders), indexing="ij")
    place = slot * feeders + feeder
    tokens, rows = slots * count * feeders, count * 8
    found = []
    for order in (feeder * count * slots + device * slots + slot, slot * count * feeders + device * feeders + feeder):
        to, back = np.full((3, tokens), -1), np.full((3, tokens), -1)
        for kind, mine, row in (
            (0, place < 8, device * 8 + place),
            (1, place >= 8, device * 8 + place - 8),
            (2, place >= 8, device * 8 + place - 8 + (slots * feeders - 8)),
        ):
            to[kind, order[mine]] = row[mine]
            back[kind, row[mine]] = order[mine]
        found.append((to, back))
    assert 8 + 2 * (slots * feeders - 8) == 16
    (time_to, time_back), (feed_to, feed_back) = found
    table = np.full((32, tokens), -1)
    for n, rows in enumerate((time_to, feed_back, feed_to, time_back)):
        table[8 * n : 8 * n + 3] = rows
    return table.astype(np.int32)


def gradient_part(g, to, total):
    width = total.shape[0]
    slabs = width // LANES
    for slab in range(slabs):
        first = (to * slabs + slab) * width
        g[first : first + width, :] = total[:, slab * LANES : (slab + 1) * LANES].astype(jnp.bfloat16)


def step_kernel(
    batch, count,
    x_ref, row_ref, table_ref, time_qkv, time_out, feed_qkv_ref, feed_out_ref, route_ref, up_ref, partner_ref,
    load_ref, time_mean_ref, feed_mean_ref,
    feed_qkv, feed_out, adjoint,
    first, t_normed, t_packed, t_weights, t_mixed, f_normed, f_packed, f_weights, f_mixed,
    hidden, d_mixed, d_packed, sent, got, back, returned,
    t_g, t_inbox, t_pair, t_full, f_g, f_inbox, f_pair, f_full,
    wire_send, wire_recv, own_sem, fetch_sem, *sems,
):
    sequences, length, width = x_ref.shape
    feeders = sequences // batch
    groups = f_weights.shape[0] // batch
    tokens = feeders * length
    place = Place()
    greet(place, count)
    fetches = [
        pltpu.make_async_copy(source, target, fetch_sem.at[n])
        for n, (source, target) in enumerate(((feed_qkv_ref, feed_qkv), (feed_out_ref, feed_out), (up_ref, adjoint)))
    ]
    for fetch in fetches:
        fetch.start()
    t_sum = Reduction(place, partner_ref, t_g, t_inbox, t_pair, t_full, time_mean_ref, sems[:7])
    f_sum = Reduction(place, partner_ref, f_g, f_inbox, f_pair, f_full, feed_mean_ref, sems[7:])
    there, home = [], []
    for b in range(batch):
        pairs = ((there, sent, got, b), (home, back, returned, batch + b))
        for exchanges, source, target, n in pairs:
            exchanges.append(
                Exchange(count, source.at[b], target.at[b], wire_send.at[n], wire_recv.at[n], own_sem.at[n])
            )
    part_rows = 4 * width
    table_rows = table_ref.shape[0]
    onehot = (row_ref[...] == lax.broadcasted_iota(jnp.int32, (row_ref.shape[0], table_rows), 1)).astype(jnp.bfloat16)
    added = dot(onehot, table_ref[...])

    def time_forward(b):
        here = slice(b * tokens, (b + 1) * tokens)
        for n in range(feeders):
            rows = slice(b * tokens + n * length, b * tokens + (n + 1) * length)
            start = x_ref[b * feeders + n].astype(jnp.float32) + added[n : n + 1]
            first[rows, :] = start
            t_normed[rows, :] = (start * norm_factor(start)).astype(jnp.bfloat16)
        t_packed[here, :] = dot(t_normed[here, :], time_qkv[...]).astype(jnp.bfloat16)
        attend_forward(t_packed, t_mixed, t_weights, b * feeders, (b + 1) * feeders, True)
        result = (first[here, :] + dot(t_mixed[here, :], time_out[...])).astype(jnp.bfloat16)
        packed_rows(sent.at[b], route_ref[0:8, :], result, count)

    def feed_layer(b):
        here = slice(b * tokens, (b + 1) * tokens)
        hidden[here, :] = unpacked_rows(got[b], route_ref[8:16, :], tokens, width)
        wide = hidden[here, :].astype(jnp.float32)
        f_normed[here, :] = (wide * norm_factor(wide)).astype(jnp.bfloat16)
        f_packed[here, :] = dot(f_normed[here, :], feed_qkv[...]).astype(jnp.bfloat16)
        attend_forward(f_packed, f_mixed, f_weights, b * groups, (b + 1) * groups, False)
        result = hidden[here, :].astype(jnp.float32) + dot(f_mixed[here, :], feed_out[...])
        load_ref[b * groups : (b + 1) * groups] = result.astype(jnp.bfloat16).reshape(groups, -1, width)
        d_mixed[here, :] = dot(adjoint[here, :], feed_out[...], NT).astype(jnp.bfloat16)
        attend_backward(f_packed, f_weights, d_mixed, d_packed, b * groups, (b + 1) * groups)
        g = dot(d_packed[here, :], feed_qkv[...], NT).astype(jnp.bfloat16).astype(jnp.float32)
        wide = hidden[here, :].astype(jnp.float32)
        factor = norm_factor(wide)
        along = jnp.sum(g * wide, axis=-1, keepdims=True) * (factor * factor * factor) * (1.0 / width)
        d_hidden = (g * factor - wide * along).astype(jnp.bfloat16)
        total = (d_hidden.astype(jnp.float32) + adjoint[here, :].astype(jnp.float32)).astype(jnp.bfloat16)
        packed_rows(back.at[b], route_ref[16:24, :], total, count)

    def time_upstream(b):
        here = slice(b * tokens, (b + 1) * tokens)
        hidden[here, :] = unpacked_rows(returned[b], route_ref[24:32, :], tokens, width)

    def time_backward(b):
        here = slice(b * tokens, (b + 1) * tokens)
        d_mixed[here, :] = dot(hidden[here, :], time_out[...], NT).astype(jnp.bfloat16)
        attend_backward(t_packed, t_weights, d_mixed, d_packed, b * feeders, (b + 1) * feeders)

    for b in range(batch):
        time_forward(b)
        if b == 0:
            all_greeted(count)
        there[b].start()
    for fetch in fetches:
        fetch.wait()
    for b in range(batch):
        there[b].wait()
        feed_layer(b)
        home[b].start()

    early = range(4)
    for part in early:
        if part < 3:
            f_total = dot(f_normed[...], d_packed[:, part * width : (part + 1) * width], TN)
        else:
            f_total = dot(f_mixed[...], adjoint[...], TN)
        gradient_part(f_g, part, f_total)
        f_sum.start(part * part_rows, (part + 1) * part_rows)
    for b in range(batch):
        home[b].wait()
        time_upstream(b)
        if b == batch - 1:
            gradient_part(f_g, 4, dot(t_mixed[...], hidden[...], TN))
            f_sum.start(4 * part_rows, 5 * part_rows)
        time_backward(b)
        f_sum.turn(b, early)
    for part in range(3):
        gradient_part(t_g, part, dot(t_normed[...], d_packed[:, part * width : (part + 1) * width], TN))
        t_sum.start(part * part_rows, (part + 1) * part_rows)
        if part == 0:
            f_sum.turn(0, (4,))
    f_sum.turn(batch, early)
    f_sum.turn(1, (4,))
    for turn in range(TURNS):
        t_sum.turn(turn)
        f_sum.turn(turn + batch + 1, early)
        f_sum.turn(turn + 2, (4,))
    f_sum.finish()
    t_sum.finish()


def finish_kernel(time_ref, feed_ref, out_ref, held, wide, in_sem, out_sem):
    slabs, depth, lanes = time_ref.shape[1:]
    rows = 4 * depth

    def get(n):
        layer, slab = n // slabs, n % slabs
        if layer:
            pieces = ((feed_ref.at[pl.ds(0, 4), slab], held.at[n]),)
        else:
            pieces = (
                (time_ref.at[:, slab], held.at[n, pl.ds(0, 3)]),
                (feed_ref.at[4, slab], held.at[n, 3]),
            )
        return [pltpu.make_async_copy(*piece, in_sem.at[n, i]) for i, piece in enumerate(pieces)]

    def put(n):
        target = out_ref.at[pl.ds(n // slabs * rows, rows), pl.ds(n % slabs * lanes, lanes)]
        return pltpu.make_async_copy(wide.at[n], target, out_sem.at[n])

    for n in range(2 * slabs):
        for copy in get(n):
            copy.start()
    for n in range(2 * slabs):
        for copy in get(n):
            copy.wait()
        for part in range(3):
            wide[n, pl.ds(part, depth, stride=3), :] = held[n, part].astype(jnp.float32)
        wide[n, 3 * depth :, :] = held[n, 3].astype(jnp.float32)
        put(n).start()
    for n in range(2 * slabs):
        put(n).wait()


def finished(time_mean, feed_mean):
    slabs, depth, lanes = time_mean.shape[1:]
    rows = 4 * depth
    return pl.pallas_call(
        finish_kernel,
        out_shape=jax.ShapeDtypeStruct((2 * rows, slabs * lanes), jnp.float32),
        in_specs=[ANY, ANY],
        out_specs=ANY,
        scratch_shapes=[
            pltpu.VMEM((2 * slabs, 4, depth, lanes), jnp.bfloat16),
            pltpu.VMEM((2 * slabs, rows, lanes), jnp.float32),
            pltpu.SemaphoreType.DMA((2 * slabs, 2)),
            pltpu.SemaphoreType.DMA((2 * slabs,)),
        ],
        compiler_params=pltpu.CompilerParams(vmem_limit_bytes=60 * 1024 * 1024),
    )(time_mean, feed_mean)


VMEM = pl.BlockSpec(memory_space=pltpu.VMEM)
ANY = pl.BlockSpec(memory_space=pl.ANY)


def on_device(
    measured_features,
    feeder_of_row,
    feeder_table,
    time_qkv,
    time_out,
    feed_qkv,
    feed_out,
    adjoint_of_prediction,
    round_index,
):
    batch, feed_local, slot_count, width = measured_features.shape
    feeder_count = adjoint_of_prediction.shape[1]
    slot_local = adjoint_of_prediction.shape[2]
    count = feeder_count // feed_local
    rows = batch * feed_local * slot_count
    pairs = width // PAIR
    bf16 = jnp.bfloat16
    sequences, groups = batch * feed_local, batch * slot_local

    route = jnp.asarray(routes(slot_local, count, feed_local))
    row_column = jnp.pad(feeder_of_row, (0, 8 - feed_local)).reshape(8, 1)
    partner = jnp.broadcast_to(round_index.astype(jnp.float32), (8, LANES))
    upstream = jnp.transpose(adjoint_of_prediction, (0, 2, 1, 3)).reshape(rows, width)
    part_rows = width * width // LANES
    time_rows, feed_rows = 3 * part_rows, 5 * part_rows
    chains = len(LINKS)

    def held(*shape):
        return pltpu.VMEM(shape, bf16)

    def reduction(n):
        return [held(n, LANES), held(n, LANES), held(len(PAIRS), n >> len(LINKS), LANES), held(n, LANES)]

    def semaphores():
        steps = [COPIES, COPIES, len(PAIRS), len(PAIRS), COPIES, COPIES]
        return [pltpu.SemaphoreType.DMA((chains, s)) for s in steps] + [pltpu.SemaphoreType.DMA((chains,))]

    wire = held(batch, count * 8, width + width // 2)
    load, time_mean, feed_mean = pl.pallas_call(
        partial(step_kernel, batch, count),
        out_shape=(
            jax.ShapeDtypeStruct((groups, feeder_count, width), bf16),
            jax.ShapeDtypeStruct((time_rows, LANES), bf16),
            jax.ShapeDtypeStruct((feed_rows, LANES), bf16),
        ),
        in_specs=[VMEM, VMEM, VMEM, VMEM, VMEM, ANY, ANY, VMEM, ANY, VMEM],
        out_specs=(VMEM, ANY, ANY),
        scratch_shapes=[
            held(width, 3 * width),
            held(width, width),
            held(rows, width),
            pltpu.VMEM((rows, width), jnp.float32),
            held(rows, width),
            held(rows, 3 * width),
            held(sequences, pairs, 2 * slot_count, slot_count),
            held(rows, width),
            held(rows, width),
            held(rows, 3 * width),
            held(groups, pairs, 2 * feeder_count, feeder_count),
            held(rows, width),
            held(rows, width),
            held(rows, width),
            held(rows, 3 * width),
            wire,
            wire,
            wire,
            wire,
        ]
        + reduction(time_rows)
        + reduction(feed_rows)
        + [pltpu.SemaphoreType.DMA((2 * batch, count))] * 2
        + [pltpu.SemaphoreType.DMA((2 * batch,)), pltpu.SemaphoreType.DMA((3,))]
        + semaphores()
        + semaphores(),
        compiler_params=pltpu.CompilerParams(collective_id=1, has_side_effects=True, vmem_limit_bytes=60 * 1024 * 1024),
    )(
        measured_features.reshape(sequences, slot_count, width),
        row_column,
        feeder_table,
        time_qkv,
        time_out,
        feed_qkv,
        feed_out,
        route,
        upstream,
        partner,
    )
    predicted_load = jnp.transpose(load.reshape(batch, slot_local, feeder_count, width), (0, 2, 1, 3))
    slabs = (width // LANES, width, LANES)
    gradients = finished(time_mean.reshape(3, *slabs), feed_mean.reshape(5, *slabs))
    return (predicted_load, gradients[None])


def solution(mesh):
    placed = (
        P("gossip", "field", None, None),
        P("field"),
        P(),
        P(),
        P(),
        P(),
        P(),
        P("gossip", None, "field", None),
        P(),
    )
    return jax.shard_map(
        on_device,
        mesh=mesh,
        in_specs=placed,
        out_specs=(P("gossip", None, "field", None), P("gossip", None, None)),
        check_vma=False,
    )
```

```python
from functools import partial
import math

import jax
import jax.numpy as jnp
import numpy as np
from jax import lax
from jax.experimental import pallas as pl
from jax.experimental.pallas import tpu as pltpu
from jax.sharding import PartitionSpec as P

epsilon = 1e-05


MESH = pl.DeviceIdType.MESH
LANES = 128
LINKS = ("ya", "za", "xa", "yb", "zb")
PAIRS = ("core", "xb")
GROUPS = (1, 1, 1, 2)
STEPS = len(GROUPS)
TURNS = 2 * STEPS + 1
COPIES = sum(2**size - 1 for size in GROUPS)

ORDER = (
    100, 110, 120, 130, 140, 20, 0, 10, 121, 131, 111, 141, 101, 30, 40, 21,
    122, 132, 1, 11, 112, 142, 102, 31, 41, 22, 123, 12, 133, 2, 113, 32,
    42, 143, 103, 124, 23, 134, 13, 114, 3, 144, 33, 43, 104, 24, 14, 125,
    4, 135, 34, 115, 44, 145, 25, 105, 15, 126, 136, 35, 5, 26, 116, 146,
    45, 16, 106, 36, 6, 137, 127, 46, 27, 147, 117, 37, 107, 17, 47, 7,
    138, 128, 148, 118, 38, 108, 28, 48, 18, 8,
)


class Place:
    def __init__(self):
        gossip, field = lax.axis_index("gossip"), lax.axis_index("field")
        x_hi, core = gossip // 2, gossip % 2
        x_lo, z, y = field // 16, (field // 4) % 4, field % 4
        self.here = {"x_hi": x_hi, "core": core, "x_lo": x_lo, "z": z, "y": y}
        self.bit = {
            "ya": ((y + 1) // 2) % 2,
            "yb": y // 2,
            "za": ((z + 1) // 2) % 2,
            "zb": z // 2,
            "xa": (x_hi + x_lo) % 2,
        }
        self.flip = {
            "ya": {"y": y + 1 - 2 * (y % 2)},
            "yb": {"y": 3 - y},
            "za": {"z": z + 1 - 2 * (z % 2)},
            "zb": {"z": 3 - z},
            "xa": {"x_lo": 1 - x_lo},
            "xb": {"x_hi": 1 - x_hi, "x_lo": 1 - x_lo},
            "core": {"core": 1 - core},
        }

    def across(self, *names):
        at = dict(self.here)
        for name in names:
            at.update(self.flip[name])
        return (at["x_hi"] * 2 + at["core"], (at["x_lo"] * 4 + at["z"]) * 4 + at["y"])


def chains_of(rows):
    unit = 512
    count, more = divmod(rows // unit, len(LINKS))
    chains, first = [], 0
    for turn in range(len(LINKS)):
        names = [LINKS[(turn + s) % len(LINKS)] for s in range(len(LINKS))]
        groups = tuple(tuple(names[sum(GROUPS[:s]) : sum(GROUPS[: s + 1])]) for s in range(STEPS))
        size = (count + (turn < more)) * unit
        chains.append((first, size, groups))
        first += size
    assert first == rows
    return chains


def block_of(rows):
    for parts in range(1, rows + 1):
        if rows % parts == 0 and rows // parts <= 256 and (rows // parts) % 16 == 0:
            return rows // parts
    return rows


class Reduction:
    def __init__(self, place, partner, g, inbox, pairbox, full, out, sems):
        self.place, self.partner = place, partner
        self.g, self.inbox, self.pairbox, self.full, self.out = g, inbox, pairbox, full, out
        self.rs_send, self.rs_recv, self.pair_send, self.pair_recv, self.ag_send, self.ag_recv, self.out_sem = sems
        self.chains = chains_of(g.shape[0])
        self.at = []
        self.steps = []
        for first, rows, groups in self.chains:
            at, size, sem, steps = [first], rows, 0, []
            for names in groups:
                part = size >> len(names)
                peers = []
                for mask in range(1, 2 ** len(names)):
                    flipped = [name for n, name in enumerate(names) if mask >> n & 1]
                    offset = at[-1]
                    for n, name in enumerate(names):
                        bit = place.bit[name]
                        offset = offset + (1 - bit if name in flipped else bit) * (size >> (n + 1))
                    slot = first + rows - size + (mask - 1) * part
                    peers.append((place.across(*flipped), offset, slot, sem))
                    sem += 1
                mine = at[-1]
                for n, name in enumerate(names):
                    mine = mine + place.bit[name] * (size >> (n + 1))
                steps.append((part, peers))
                at.append(mine)
                size = part
            self.at.append(at)
            self.steps.append(steps)

    def rs_copies(self, j, s):
        part, peers = self.steps[j][s]
        return [
            pltpu.make_async_remote_copy(
                src_ref=self.g.at[pl.ds(pl.multiple_of(offset, 16), part)],
                dst_ref=self.inbox.at[pl.ds(slot, part)],
                send_sem=self.rs_send.at[j, sem],
                recv_sem=self.rs_recv.at[j, sem],
                device_id=peer,
                device_id_type=MESH,
            )
            for peer, offset, slot, sem in peers
        ]

    def rs_add(self, j, s):
        part, peers = self.steps[j][s]
        keep = self.at[j][s + 1]
        block = block_of(part)

        def add(i, carry):
            here = pl.ds(pl.multiple_of(keep + i * block, 16), block)
            total = self.g[here, :].astype(jnp.float32)
            for peer, offset, slot, sem in peers:
                there = pl.ds(pl.multiple_of(slot + i * block, 16), block)
                total = total + self.inbox[there, :].astype(jnp.float32)
            self.g[here, :] = total.astype(jnp.bfloat16)
            return carry

        lax.fori_loop(0, part // block, add, 0)

    def shard(self, j):
        first, rows, groups = self.chains[j]
        count = rows >> len(LINKS)
        return pl.ds(pl.multiple_of(self.at[j][STEPS], 16), count), pl.ds(first >> len(LINKS), count)

    def pair_copy(self, j, n):
        here, there = self.shard(j)
        return pltpu.make_async_remote_copy(
            src_ref=self.g.at[here],
            dst_ref=self.pairbox.at[n, there],
            send_sem=self.pair_send.at[j, n],
            recv_sem=self.pair_recv.at[j, n],
            device_id=self.place.across(PAIRS[n]),
            device_id_type=MESH,
        )

    def pair_mean(self, j):
        here, there = self.shard(j)
        other = jnp.where(
            self.partner[0:1, :] > 0.0,
            self.pairbox[1, there, :].astype(jnp.float32),
            self.pairbox[0, there, :].astype(jnp.float32),
        )
        self.full[here, :] = ((self.g[here, :].astype(jnp.float32) + other) * 0.5).astype(jnp.bfloat16)

    def ag_copies(self, j, s):
        part, peers = self.steps[j][s]
        mine = self.full.at[pl.ds(pl.multiple_of(self.at[j][s + 1], 16), part)]
        return [
            pltpu.make_async_remote_copy(
                src_ref=mine,
                dst_ref=mine,
                send_sem=self.ag_send.at[j, sem],
                recv_sem=self.ag_recv.at[j, sem],
                device_id=peer,
                device_id_type=MESH,
            )
            for peer, offset, slot, sem in peers
        ]

    def out_copy(self, j):
        part = pl.ds(self.chains[j][0], self.chains[j][1])
        return pltpu.make_async_copy(self.full.at[part], self.out.at[part], self.out_sem.at[j])

    def start(self, begin, end):
        for j, (first, rows, groups) in enumerate(self.chains):
            if begin < first + rows <= end:
                for copy in self.rs_copies(j, 0):
                    copy.start()

    def turn(self, t, chains=None):
        if 0 <= t < TURNS:
            for j in range(len(self.chains)) if chains is None else chains:
                self.advance(j, t)

    def advance(self, j, stage):
        following = []
        if stage < STEPS:
            for copy in self.rs_copies(j, stage):
                copy.wait()
            self.rs_add(j, stage)
            if stage + 1 < STEPS:
                following = self.rs_copies(j, stage + 1)
            else:
                following = [self.pair_copy(j, n) for n in range(len(PAIRS))]
        elif stage == STEPS:
            for n in range(len(PAIRS)):
                self.pair_copy(j, n).wait()
            self.pair_mean(j)
            following = self.ag_copies(j, STEPS - 1)
        else:
            s = 2 * STEPS - stage
            for copy in self.ag_copies(j, s):
                copy.wait()
            following = self.ag_copies(j, s - 1) if s > 0 else [self.out_copy(j)]
        for copy in following:
            copy.start()

    def finish(self):
        for j in range(len(self.chains)):
            self.out_copy(j).wait()


class Exchange:
    def __init__(self, count, send, got, send_sem, recv_sem, own_sem):
        self.count, self.send, self.got = count, send, got
        self.send_sem, self.recv_sem, self.own_sem = send_sem, recv_sem, own_sem
        self.gossip, self.me = lax.axis_index("gossip"), lax.axis_index("field")
        self.rows = send.shape[0] // count

    def block(self, i):
        return pl.ds(pl.multiple_of(i * self.rows, 8), self.rows)

    def own(self):
        here = self.block(self.me)
        return pltpu.make_async_copy(self.send.at[here], self.got.at[here], self.own_sem)

    def copy(self, i):
        to = lax.rem(self.me + i, self.count)
        return pltpu.make_async_remote_copy(
            src_ref=self.send.at[self.block(to)],
            dst_ref=self.got.at[self.block(self.me)],
            send_sem=self.send_sem.at[i],
            recv_sem=self.recv_sem.at[i],
            device_id=(self.gossip, to),
            device_id_type=MESH,
        )

    def start(self):
        def one(i, carry):
            self.copy(i).start()
            return carry

        lax.fori_loop(1, self.count, one, 0)
        self.own().start()

    def wait(self):
        def one(i, carry):
            self.copy(i).wait()
            return carry

        lax.fori_loop(1, self.count, one, 0)
        self.own().wait()


def greet(place, count):
    barrier = pltpu.get_barrier_semaphore()
    gossip, me = lax.axis_index("gossip"), lax.axis_index("field")

    def one(i, carry):
        peer = (gossip, lax.rem(me + i, count))
        pl.semaphore_signal(barrier, inc=1, device_id=peer, device_id_type=MESH)
        return carry

    lax.fori_loop(1, count, one, 0)
    for name in PAIRS:
        pl.semaphore_signal(barrier, inc=1, device_id=place.across(name), device_id_type=MESH)


def all_greeted(count):
    pl.semaphore_wait(pltpu.get_barrier_semaphore(), count - 1 + len(PAIRS))


SIZE = 64
PAIR = 2 * SIZE


def dot(a, b, contract=((1,), (0,))):
    return lax.dot_general(a, b, (contract, ((), ())), preferred_element_type=jnp.float32)


NT = ((1,), (1,))
TN = ((0,), (0,))


def first_lanes(rows):
    return lax.broadcasted_iota(jnp.int32, (rows, PAIR), 1) < SIZE


def stacked(pair):
    low = first_lanes(pair.shape[0])
    nothing = jnp.zeros_like(pair)
    return jnp.concatenate([jnp.where(low, pair, nothing), jnp.where(low, nothing, pair)], axis=0)


def unstacked(both):
    rows = both.shape[0] // 2
    return jnp.where(first_lanes(rows), both[:rows], both[rows:])


def norm_factor(wide):
    return lax.rsqrt(jnp.mean(wide * wide, axis=-1, keepdims=True) + epsilon)


def weights_of(q, k, causal):
    length = k.shape[0]
    powers = jnp.exp(dot(stacked(q), k, NT) * (1.0 / math.sqrt(SIZE)))
    if causal:
        query = lax.broadcasted_iota(jnp.int32, powers.shape, 0) % length
        key = lax.broadcasted_iota(jnp.int32, powers.shape, 1)
        powers = jnp.where(query >= key, powers, 0.0)
    return powers / jnp.sum(powers, axis=-1, keepdims=True)


def attend_forward(packed, mixed, weights, begin, end, causal):
    length = weights.shape[3]
    width = mixed.shape[1]

    def one(n, carry):
        rows = pl.ds(pl.multiple_of(n * length, 16), length)
        for p in range(width // PAIR):
            lanes = p * PAIR
            q = packed[rows, lanes : lanes + PAIR]
            k = packed[rows, width + lanes : width + lanes + PAIR]
            v = packed[rows, 2 * width + lanes : 2 * width + lanes + PAIR]
            w = weights_of(q, k, causal).astype(jnp.bfloat16)
            weights[n, p] = w
            mixed[rows, lanes : lanes + PAIR] = unstacked(dot(w, v)).astype(jnp.bfloat16)
        return carry

    lax.fori_loop(begin, end, one, 0)


def attend_backward(packed, weights, d_mixed, d_packed, begin, end):
    length = weights.shape[3]
    width = d_mixed.shape[1]

    def one(n, carry):
        rows = pl.ds(pl.multiple_of(n * length, 16), length)
        for p in range(width // PAIR):
            lanes = p * PAIR
            q = packed[rows, lanes : lanes + PAIR]
            k = packed[rows, width + lanes : width + lanes + PAIR]
            v = packed[rows, 2 * width + lanes : 2 * width + lanes + PAIR]
            up = stacked(d_mixed[rows, lanes : lanes + PAIR])
            w = weights[n, p]
            wide = w.astype(jnp.float32)
            d_w = dot(up, v, NT).astype(jnp.bfloat16).astype(jnp.float32)
            d_scores = wide * (d_w - jnp.sum(d_w * wide, axis=-1, keepdims=True))
            d_scores = (d_scores * (1.0 / math.sqrt(SIZE))).astype(jnp.bfloat16)
            d_q = unstacked(dot(d_scores, k))
            d_k = dot(d_scores, stacked(q), TN)
            d_v = dot(w, up, TN)
            d_packed[rows, lanes : lanes + PAIR] = d_q.astype(jnp.bfloat16)
            d_packed[rows, width + lanes : width + lanes + PAIR] = d_k.astype(jnp.bfloat16)
            d_packed[rows, 2 * width + lanes : 2 * width + lanes + PAIR] = d_v.astype(jnp.bfloat16)
        return carry

    lax.fori_loop(begin, end, one, 0)


def selected(targets, rows, values):
    onehot = jnp.where(targets == lax.broadcasted_iota(jnp.int32, (rows, values.shape[0]), 0), 1.0, 0.0)
    return dot(onehot.astype(jnp.bfloat16), values)


def packed_rows(wire, at, values, block):
    rows, width = wire.shape[0], values.shape[1]
    tokens = values.shape[0]
    half = width // 2
    wire[:, :width] = selected(at[0:1, :tokens], rows, values).astype(jnp.bfloat16)
    low = selected(at[1:2, :tokens], rows, values[:, :half])
    high = selected(at[2:3, :tokens], rows, values[:, half:])
    wire[:, width:] = (low + high).astype(jnp.bfloat16)


def unpacked_rows(wire, at, tokens, width):
    rows = wire.shape[0]
    main = selected(at[0:1, :rows], tokens, wire[:, :width])
    low = selected(at[1:2, :rows], tokens, wire[:, width:])
    high = selected(at[2:3, :rows], tokens, wire[:, width:])
    return (main + jnp.concatenate([low, high], axis=1)).astype(jnp.bfloat16)


def routes(slots, count, feeders):
    device, slot, feeder = np.meshgrid(np.arange(count), np.arange(slots), np.arange(feeders), indexing="ij")
    place = slot * feeders + feeder
    tokens, rows = slots * count * feeders, count * 8
    found = []
    for order in (feeder * count * slots + device * slots + slot, slot * count * feeders + device * feeders + feeder):
        to, back = np.full((3, tokens), -1), np.full((3, tokens), -1)
        for kind, mine, row in (
            (0, place < 8, device * 8 + place),
            (1, place >= 8, device * 8 + place - 8),
            (2, place >= 8, device * 8 + place - 8 + (slots * feeders - 8)),
        ):
            to[kind, order[mine]] = row[mine]
            back[kind, row[mine]] = order[mine]
        found.append((to, back))
    assert 8 + 2 * (slots * feeders - 8) == 16
    (time_to, time_back), (feed_to, feed_back) = found
    table = np.full((32, tokens), -1)
    for n, rows in enumerate((time_to, feed_back, feed_to, time_back)):
        table[8 * n : 8 * n + 3] = rows
    return table.astype(np.int32)


def gradient_part(g, to, total):
    width = total.shape[0]
    slabs = width // LANES
    for slab in range(slabs):
        first = (to * slabs + slab) * width
        g[first : first + width, :] = total[:, slab * LANES : (slab + 1) * LANES].astype(jnp.bfloat16)


def step_kernel(
    batch, count,
    x_ref, row_ref, table_ref, time_qkv, time_out, feed_qkv_ref, feed_out_ref, route_ref, up_ref, partner_ref,
    load_ref, time_mean_ref, feed_mean_ref,
    feed_qkv, feed_out, adjoint,
    first, t_normed, t_packed, t_weights, t_mixed, f_normed, f_packed, f_weights, f_mixed,
    hidden, d_mixed, d_packed, sent, got, back, returned,
    t_g, t_inbox, t_pair, t_full, f_g, f_inbox, f_pair, f_full,
    wire_send, wire_recv, own_sem, fetch_sem, *sems,
):
    sequences, length, width = x_ref.shape
    feeders = sequences // batch
    groups = f_weights.shape[0] // batch
    tokens = feeders * length
    place = Place()
    greet(place, count)
    fetches = [
        pltpu.make_async_copy(source, target, fetch_sem.at[n])
        for n, (source, target) in enumerate(((feed_qkv_ref, feed_qkv), (feed_out_ref, feed_out), (up_ref, adjoint)))
    ]
    for fetch in fetches:
        fetch.start()
    t_sum = Reduction(place, partner_ref, t_g, t_inbox, t_pair, t_full, time_mean_ref, sems[:7])
    f_sum = Reduction(place, partner_ref, f_g, f_inbox, f_pair, f_full, feed_mean_ref, sems[7:])
    there, home = [], []
    for b in range(batch):
        pairs = ((there, sent, got, b), (home, back, returned, batch + b))
        for exchanges, source, target, n in pairs:
            exchanges.append(
                Exchange(count, source.at[b], target.at[b], wire_send.at[n], wire_recv.at[n], own_sem.at[n])
            )
    part_rows = 4 * width
    table_rows = table_ref.shape[0]
    onehot = (row_ref[...] == lax.broadcasted_iota(jnp.int32, (row_ref.shape[0], table_rows), 1)).astype(jnp.bfloat16)
    added = dot(onehot, table_ref[...])

    def time_forward(b):
        here = slice(b * tokens, (b + 1) * tokens)
        for n in range(feeders):
            rows = slice(b * tokens + n * length, b * tokens + (n + 1) * length)
            start = x_ref[b * feeders + n].astype(jnp.float32) + added[n : n + 1]
            first[rows, :] = start
            t_normed[rows, :] = (start * norm_factor(start)).astype(jnp.bfloat16)
        t_packed[here, :] = dot(t_normed[here, :], time_qkv[...]).astype(jnp.bfloat16)
        attend_forward(t_packed, t_mixed, t_weights, b * feeders, (b + 1) * feeders, True)
        result = (first[here, :] + dot(t_mixed[here, :], time_out[...])).astype(jnp.bfloat16)
        packed_rows(sent.at[b], route_ref[0:8, :], result, count)

    def feed_layer(b):
        here = slice(b * tokens, (b + 1) * tokens)
        hidden[here, :] = unpacked_rows(got[b], route_ref[8:16, :], tokens, width)
        wide = hidden[here, :].astype(jnp.float32)
        f_normed[here, :] = (wide * norm_factor(wide)).astype(jnp.bfloat16)
        f_packed[here, :] = dot(f_normed[here, :], feed_qkv[...]).astype(jnp.bfloat16)
        attend_forward(f_packed, f_mixed, f_weights, b * groups, (b + 1) * groups, False)
        result = hidden[here, :].astype(jnp.float32) + dot(f_mixed[here, :], feed_out[...])
        load_ref[b * groups : (b + 1) * groups] = result.astype(jnp.bfloat16).reshape(groups, -1, width)
        d_mixed[here, :] = dot(adjoint[here, :], feed_out[...], NT).astype(jnp.bfloat16)
        attend_backward(f_packed, f_weights, d_mixed, d_packed, b * groups, (b + 1) * groups)
        g = dot(d_packed[here, :], feed_qkv[...], NT).astype(jnp.bfloat16).astype(jnp.float32)
        wide = hidden[here, :].astype(jnp.float32)
        factor = norm_factor(wide)
        along = jnp.sum(g * wide, axis=-1, keepdims=True) * (factor * factor * factor) * (1.0 / width)
        d_hidden = (g * factor - wide * along).astype(jnp.bfloat16)
        total = (d_hidden.astype(jnp.float32) + adjoint[here, :].astype(jnp.float32)).astype(jnp.bfloat16)
        packed_rows(back.at[b], route_ref[16:24, :], total, count)

    def time_upstream(b):
        here = slice(b * tokens, (b + 1) * tokens)
        hidden[here, :] = unpacked_rows(returned[b], route_ref[24:32, :], tokens, width)

    def time_backward(b):
        here = slice(b * tokens, (b + 1) * tokens)
        d_mixed[here, :] = dot(hidden[here, :], time_out[...], NT).astype(jnp.bfloat16)
        attend_backward(t_packed, t_weights, d_mixed, d_packed, b * feeders, (b + 1) * feeders)

    for b in range(batch):
        time_forward(b)
        if b == 0:
            all_greeted(count)
        there[b].start()
    for fetch in fetches:
        fetch.wait()
    for b in range(batch):
        there[b].wait()
        feed_layer(b)
        home[b].start()

    for part in range(4):
        if part < 3:
            f_total = dot(f_normed[...], d_packed[:, part * width : (part + 1) * width], TN)
        else:
            f_total = dot(f_mixed[...], adjoint[...], TN)
        gradient_part(f_g, part, f_total)
        f_sum.start(part * part_rows, (part + 1) * part_rows)
    for b in range(batch):
        home[b].wait()
        time_upstream(b)
        if b == batch - 1:
            gradient_part(f_g, 4, dot(t_mixed[...], hidden[...], TN))
            f_sum.start(4 * part_rows, 5 * part_rows)
        time_backward(b)
    f_sum.turn(0, ())
    for part in range(3):
        gradient_part(t_g, part, dot(t_normed[...], d_packed[:, part * width : (part + 1) * width], TN))
        t_sum.start(part * part_rows, (part + 1) * part_rows)
    for code in ORDER:
        (f_sum if code >= 100 else t_sum).advance(code // 10 % 10, code % 10)
    f_sum.finish()
    t_sum.finish()


def finish_kernel(time_ref, feed_ref, out_ref, held, wide, in_sem, out_sem):
    slabs, depth, lanes = time_ref.shape[1:]
    rows = 4 * depth

    def get(n):
        layer, slab = n // slabs, n % slabs
        if layer:
            pieces = ((feed_ref.at[pl.ds(0, 4), slab], held.at[n]),)
        else:
            pieces = (
                (time_ref.at[:, slab], held.at[n, pl.ds(0, 3)]),
                (feed_ref.at[4, slab], held.at[n, 3]),
            )
        return [pltpu.make_async_copy(*piece, in_sem.at[n, i]) for i, piece in enumerate(pieces)]

    def put(n):
        target = out_ref.at[pl.ds(n // slabs * rows, rows), pl.ds(n % slabs * lanes, lanes)]
        return pltpu.make_async_copy(wide.at[n], target, out_sem.at[n])

    for n in range(2 * slabs):
        for copy in get(n):
            copy.start()
    for n in range(2 * slabs):
        for copy in get(n):
            copy.wait()
        for part in range(3):
            wide[n, pl.ds(part, depth, stride=3), :] = held[n, part].astype(jnp.float32)
        wide[n, 3 * depth :, :] = held[n, 3].astype(jnp.float32)
        put(n).start()
    for n in range(2 * slabs):
        put(n).wait()


def finished(time_mean, feed_mean):
    slabs, depth, lanes = time_mean.shape[1:]
    rows = 4 * depth
    return pl.pallas_call(
        finish_kernel,
        out_shape=jax.ShapeDtypeStruct((2 * rows, slabs * lanes), jnp.float32),
        in_specs=[ANY, ANY],
        out_specs=ANY,
        scratch_shapes=[
            pltpu.VMEM((2 * slabs, 4, depth, lanes), jnp.bfloat16),
            pltpu.VMEM((2 * slabs, rows, lanes), jnp.float32),
            pltpu.SemaphoreType.DMA((2 * slabs, 2)),
            pltpu.SemaphoreType.DMA((2 * slabs,)),
        ],
        compiler_params=pltpu.CompilerParams(vmem_limit_bytes=60 * 1024 * 1024),
    )(time_mean, feed_mean)


VMEM = pl.BlockSpec(memory_space=pltpu.VMEM)
ANY = pl.BlockSpec(memory_space=pl.ANY)


def on_device(
    measured_features,
    feeder_of_row,
    feeder_table,
    time_qkv,
    time_out,
    feed_qkv,
    feed_out,
    adjoint_of_prediction,
    round_index,
):
    batch, feed_local, slot_count, width = measured_features.shape
    feeder_count = adjoint_of_prediction.shape[1]
    slot_local = adjoint_of_prediction.shape[2]
    count = feeder_count // feed_local
    rows = batch * feed_local * slot_count
    pairs = width // PAIR
    bf16 = jnp.bfloat16
    sequences, groups = batch * feed_local, batch * slot_local

    route = jnp.asarray(routes(slot_local, count, feed_local))
    row_column = jnp.pad(feeder_of_row, (0, 8 - feed_local)).reshape(8, 1)
    partner = jnp.broadcast_to(round_index.astype(jnp.float32), (8, LANES))
    upstream = jnp.transpose(adjoint_of_prediction, (0, 2, 1, 3)).reshape(rows, width)
    part_rows = width * width // LANES
    time_rows, feed_rows = 3 * part_rows, 5 * part_rows
    chains = len(LINKS)

    def held(*shape):
        return pltpu.VMEM(shape, bf16)

    def reduction(n):
        return [held(n, LANES), held(n, LANES), held(len(PAIRS), n >> len(LINKS), LANES), held(n, LANES)]

    def semaphores():
        steps = [COPIES, COPIES, len(PAIRS), len(PAIRS), COPIES, COPIES]
        return [pltpu.SemaphoreType.DMA((chains, s)) for s in steps] + [pltpu.SemaphoreType.DMA((chains,))]

    wire = held(batch, count * 8, width + width // 2)
    load, time_mean, feed_mean = pl.pallas_call(
        partial(step_kernel, batch, count),
        out_shape=(
            jax.ShapeDtypeStruct((groups, feeder_count, width), bf16),
            jax.ShapeDtypeStruct((time_rows, LANES), bf16),
            jax.ShapeDtypeStruct((feed_rows, LANES), bf16),
        ),
        in_specs=[VMEM, VMEM, VMEM, VMEM, VMEM, ANY, ANY, VMEM, ANY, VMEM],
        out_specs=(VMEM, ANY, ANY),
        scratch_shapes=[
            held(width, 3 * width),
            held(width, width),
            held(rows, width),
            pltpu.VMEM((rows, width), jnp.float32),
            held(rows, width),
            held(rows, 3 * width),
            held(sequences, pairs, 2 * slot_count, slot_count),
            held(rows, width),
            held(rows, width),
            held(rows, 3 * width),
            held(groups, pairs, 2 * feeder_count, feeder_count),
            held(rows, width),
            held(rows, width),
            held(rows, width),
            held(rows, 3 * width),
            wire,
            wire,
            wire,
            wire,
        ]
        + reduction(time_rows)
        + reduction(feed_rows)
        + [pltpu.SemaphoreType.DMA((2 * batch, count))] * 2
        + [pltpu.SemaphoreType.DMA((2 * batch,)), pltpu.SemaphoreType.DMA((3,))]
        + semaphores()
        + semaphores(),
        compiler_params=pltpu.CompilerParams(collective_id=1, has_side_effects=True, vmem_limit_bytes=60 * 1024 * 1024),
    )(
        measured_features.reshape(sequences, slot_count, width),
        row_column,
        feeder_table,
        time_qkv,
        time_out,
        feed_qkv,
        feed_out,
        route,
        upstream,
        partner,
    )
    predicted_load = jnp.transpose(load.reshape(batch, slot_local, feeder_count, width), (0, 2, 1, 3))
    slabs = (width // LANES, width, LANES)
    gradients = finished(time_mean.reshape(3, *slabs), feed_mean.reshape(5, *slabs))
    return (predicted_load, gradients[None])


def solution(mesh):
    placed = (
        P("gossip", "field", None, None),
        P("field"),
        P(),
        P(),
        P(),
        P(),
        P(),
        P("gossip", None, "field", None),
        P(),
    )
    return jax.shard_map(
        on_device,
        mesh=mesh,
        in_specs=placed,
        out_specs=(P("gossip", None, "field", None), P("gossip", None, None)),
        check_vma=False,
    )
```

```python
from functools import partial
import math

import jax
import jax.numpy as jnp
import numpy as np
from jax import lax
from jax.experimental import pallas as pl
from jax.experimental.pallas import tpu as pltpu
from jax.sharding import PartitionSpec as P

epsilon = 1e-05


MESH = pl.DeviceIdType.MESH
LANES = 128
LINKS = ("ya", "za", "xa", "yb", "zb")
PAIRS = ("core", "xb")
GROUPS = (1, 1, 1, 2)
STEPS = len(GROUPS)
TURNS = 2 * STEPS + 1
COPIES = sum(2**size - 1 for size in GROUPS)
TIME_PLAN = (
    (1, (3, 2, 4, 1, 0)),
    (2, (1, 4, 0, 3, 2)),
    (1, (4, 0, 2, 3, 1)),
    (2, (4, 0, 2, 3, 1)),
    (2, (3, 1, 0, 4, 2)),
    (2, (0, 3, 4, 2, 1)),
    (1, (3, 1, 4, 0, 2)),
    (1, (0, 2, 4, 3, 1)),
)
FEED_PLAN = (
    (3, (2, 1, 3, 4, 0)),
    (2, (2, 3, 1, 0, 4)),
    (1, (0, 4, 1, 3, 2)),
    (2, (4, 0, 3, 2, 1)),
    (1, (1, 0, 3, 2, 4)),
    (1, (3, 2, 4, 0, 1)),
    (3, (0, 2, 4, 1, 3)),
    (3, (1, 2, 3, 0, 4)),
    (2, (3, 2, 1, 0, 4)),
    (2, (4, 1, 0, 3, 2)),
)

ORDER = (
    (),
    (120, 140, 150),
    (130,),
    (100, 180),
    (
        160, 170, 190, 121, 141, 110, 151, 0, 20, 131, 10, 181, 30, 40, 152, 101,
        161, 50, 60, 142, 191, 70, 122, 11, 171, 21, 111, 182, 1, 132, 31, 41,
        162, 102, 61, 153, 192, 143, 71, 51, 12, 22, 112, 2, 123, 172, 183, 32,
        133, 42, 154, 144, 163, 62, 72, 103, 193, 52, 124, 13, 23, 184, 134, 113,
        3, 173, 33, 164, 43, 155, 104, 145, 194, 63, 73, 14, 24, 53, 125, 114,
        4, 185, 174, 135, 34, 44, 156, 146, 64, 74, 165, 54, 105, 195, 126, 15,
        25, 115, 186, 5, 136, 175, 157, 45, 147, 35, 75, 166, 65, 196, 55, 106,
        26, 127, 16, 116, 6, 187, 176, 137, 76, 36, 46, 66, 148, 158, 56, 27,
        197, 167, 17, 117, 7, 128, 107, 37, 177, 138, 47, 188, 77, 67, 28, 57,
        8, 118, 18, 168, 198, 78, 48, 38, 68, 108, 178, 58,
    ),
)


class Place:
    def __init__(self):
        gossip, field = lax.axis_index("gossip"), lax.axis_index("field")
        x_hi, core = gossip // 2, gossip % 2
        x_lo, z, y = field // 16, (field // 4) % 4, field % 4
        self.here = {"x_hi": x_hi, "core": core, "x_lo": x_lo, "z": z, "y": y}
        self.bit = {
            "ya": ((y + 1) // 2) % 2,
            "yb": y // 2,
            "za": ((z + 1) // 2) % 2,
            "zb": z // 2,
            "xa": (x_hi + x_lo) % 2,
        }
        self.flip = {
            "ya": {"y": y + 1 - 2 * (y % 2)},
            "yb": {"y": 3 - y},
            "za": {"z": z + 1 - 2 * (z % 2)},
            "zb": {"z": 3 - z},
            "xa": {"x_lo": 1 - x_lo},
            "xb": {"x_hi": 1 - x_hi, "x_lo": 1 - x_lo},
            "core": {"core": 1 - core},
        }

    def across(self, *names):
        at = dict(self.here)
        for name in names:
            at.update(self.flip[name])
        return (at["x_hi"] * 2 + at["core"], (at["x_lo"] * 4 + at["z"]) * 4 + at["y"])


def chains_of(plan):
    chains, first = [], 0
    for units, turns in plan:
        names = [LINKS[turn] for turn in turns]
        groups = tuple(tuple(names[sum(GROUPS[:s]) : sum(GROUPS[: s + 1])]) for s in range(STEPS))
        chains.append((first, units * 512, groups))
        first += units * 512
    return chains


def block_of(rows):
    for parts in range(1, rows + 1):
        if rows % parts == 0 and rows // parts <= 256 and (rows // parts) % 16 == 0:
            return rows // parts
    return rows


class Reduction:
    def __init__(self, plan, place, partner, g, inbox, pairbox, full, out, sems):
        self.place, self.partner = place, partner
        self.g, self.inbox, self.pairbox, self.full, self.out = g, inbox, pairbox, full, out
        self.rs_send, self.rs_recv, self.pair_send, self.pair_recv, self.ag_send, self.ag_recv, self.out_sem = sems
        self.chains = chains_of(plan)
        assert sum(rows for first, rows, groups in self.chains) == g.shape[0]
        self.at = []
        self.steps = []
        for first, rows, groups in self.chains:
            at, size, sem, steps = [first], rows, 0, []
            for names in groups:
                part = size >> len(names)
                peers = []
                for mask in range(1, 2 ** len(names)):
                    flipped = [name for n, name in enumerate(names) if mask >> n & 1]
                    offset = at[-1]
                    for n, name in enumerate(names):
                        bit = place.bit[name]
                        offset = offset + (1 - bit if name in flipped else bit) * (size >> (n + 1))
                    slot = first + rows - size + (mask - 1) * part
                    peers.append((place.across(*flipped), offset, slot, sem))
                    sem += 1
                mine = at[-1]
                for n, name in enumerate(names):
                    mine = mine + place.bit[name] * (size >> (n + 1))
                steps.append((part, peers))
                at.append(mine)
                size = part
            self.at.append(at)
            self.steps.append(steps)

    def rs_copies(self, j, s):
        part, peers = self.steps[j][s]
        return [
            pltpu.make_async_remote_copy(
                src_ref=self.g.at[pl.ds(pl.multiple_of(offset, 16), part)],
                dst_ref=self.inbox.at[pl.ds(slot, part)],
                send_sem=self.rs_send.at[j, sem],
                recv_sem=self.rs_recv.at[j, sem],
                device_id=peer,
                device_id_type=MESH,
            )
            for peer, offset, slot, sem in peers
        ]

    def rs_add(self, j, s):
        part, peers = self.steps[j][s]
        keep = self.at[j][s + 1]
        block = block_of(part)

        def add(i, carry):
            here = pl.ds(pl.multiple_of(keep + i * block, 16), block)
            total = self.g[here, :].astype(jnp.float32)
            for peer, offset, slot, sem in peers:
                there = pl.ds(pl.multiple_of(slot + i * block, 16), block)
                total = total + self.inbox[there, :].astype(jnp.float32)
            self.g[here, :] = total.astype(jnp.bfloat16)
            return carry

        lax.fori_loop(0, part // block, add, 0)

    def shard(self, j):
        first, rows, groups = self.chains[j]
        count = rows >> len(LINKS)
        return pl.ds(pl.multiple_of(self.at[j][STEPS], 16), count), pl.ds(first >> len(LINKS), count)

    def pair_copy(self, j, n):
        here, there = self.shard(j)
        return pltpu.make_async_remote_copy(
            src_ref=self.g.at[here],
            dst_ref=self.pairbox.at[n, there],
            send_sem=self.pair_send.at[j, n],
            recv_sem=self.pair_recv.at[j, n],
            device_id=self.place.across(PAIRS[n]),
            device_id_type=MESH,
        )

    def pair_mean(self, j):
        here, there = self.shard(j)
        other = jnp.where(
            self.partner[0:1, :] > 0.0,
            self.pairbox[1, there, :].astype(jnp.float32),
            self.pairbox[0, there, :].astype(jnp.float32),
        )
        self.full[here, :] = ((self.g[here, :].astype(jnp.float32) + other) * 0.5).astype(jnp.bfloat16)

    def ag_copies(self, j, s):
        part, peers = self.steps[j][s]
        mine = self.full.at[pl.ds(pl.multiple_of(self.at[j][s + 1], 16), part)]
        return [
            pltpu.make_async_remote_copy(
                src_ref=mine,
                dst_ref=mine,
                send_sem=self.ag_send.at[j, sem],
                recv_sem=self.ag_recv.at[j, sem],
                device_id=peer,
                device_id_type=MESH,
            )
            for peer, offset, slot, sem in peers
        ]

    def out_copy(self, j):
        part = pl.ds(self.chains[j][0], self.chains[j][1])
        return pltpu.make_async_copy(self.full.at[part], self.out.at[part], self.out_sem.at[j])

    def start(self, begin, end):
        for j, (first, rows, groups) in enumerate(self.chains):
            if begin < first + rows <= end:
                for copy in self.rs_copies(j, 0):
                    copy.start()

    def advance(self, j, stage):
        following = []
        if stage < STEPS:
            for copy in self.rs_copies(j, stage):
                copy.wait()
            self.rs_add(j, stage)
            if stage + 1 < STEPS:
                following = self.rs_copies(j, stage + 1)
            else:
                following = [self.pair_copy(j, n) for n in range(len(PAIRS))]
        elif stage == STEPS:
            for n in range(len(PAIRS)):
                self.pair_copy(j, n).wait()
            self.pair_mean(j)
            following = self.ag_copies(j, STEPS - 1)
        else:
            s = 2 * STEPS - stage
            for copy in self.ag_copies(j, s):
                copy.wait()
            following = self.ag_copies(j, s - 1) if s > 0 else [self.out_copy(j)]
        for copy in following:
            copy.start()

    def finish(self):
        for j in range(len(self.chains)):
            self.out_copy(j).wait()


class Exchange:
    def __init__(self, count, send, got, send_sem, recv_sem, own_sem):
        self.count, self.send, self.got = count, send, got
        self.send_sem, self.recv_sem, self.own_sem = send_sem, recv_sem, own_sem
        self.gossip, self.me = lax.axis_index("gossip"), lax.axis_index("field")
        self.rows = send.shape[0] // count

    def block(self, i):
        return pl.ds(pl.multiple_of(i * self.rows, 8), self.rows)

    def own(self):
        here = self.block(self.me)
        return pltpu.make_async_copy(self.send.at[here], self.got.at[here], self.own_sem)

    def copy(self, i):
        to = lax.rem(self.me + i, self.count)
        return pltpu.make_async_remote_copy(
            src_ref=self.send.at[self.block(to)],
            dst_ref=self.got.at[self.block(self.me)],
            send_sem=self.send_sem.at[i],
            recv_sem=self.recv_sem.at[i],
            device_id=(self.gossip, to),
            device_id_type=MESH,
        )

    def start(self):
        def one(i, carry):
            self.copy(i).start()
            return carry

        lax.fori_loop(1, self.count, one, 0)
        self.own().start()

    def wait(self):
        def one(i, carry):
            self.copy(i).wait()
            return carry

        lax.fori_loop(1, self.count, one, 0)
        self.own().wait()


def greet(place, count):
    barrier = pltpu.get_barrier_semaphore()
    gossip, me = lax.axis_index("gossip"), lax.axis_index("field")

    def one(i, carry):
        peer = (gossip, lax.rem(me + i, count))
        pl.semaphore_signal(barrier, inc=1, device_id=peer, device_id_type=MESH)
        return carry

    lax.fori_loop(1, count, one, 0)
    for name in PAIRS:
        pl.semaphore_signal(barrier, inc=1, device_id=place.across(name), device_id_type=MESH)


def all_greeted(count):
    pl.semaphore_wait(pltpu.get_barrier_semaphore(), count - 1 + len(PAIRS))


SIZE = 64
PAIR = 2 * SIZE


def dot(a, b, contract=((1,), (0,))):
    return lax.dot_general(a, b, (contract, ((), ())), preferred_element_type=jnp.float32)


NT = ((1,), (1,))
TN = ((0,), (0,))


def first_lanes(rows):
    return lax.broadcasted_iota(jnp.int32, (rows, PAIR), 1) < SIZE


def stacked(pair):
    low = first_lanes(pair.shape[0])
    nothing = jnp.zeros_like(pair)
    return jnp.concatenate([jnp.where(low, pair, nothing), jnp.where(low, nothing, pair)], axis=0)


def unstacked(both):
    rows = both.shape[0] // 2
    return jnp.where(first_lanes(rows), both[:rows], both[rows:])


def norm_factor(wide):
    return lax.rsqrt(jnp.mean(wide * wide, axis=-1, keepdims=True) + epsilon)


def weights_of(q, k, causal):
    length = k.shape[0]
    powers = jnp.exp(dot(stacked(q), k, NT) * (1.0 / math.sqrt(SIZE)))
    if causal:
        query = lax.broadcasted_iota(jnp.int32, powers.shape, 0) % length
        key = lax.broadcasted_iota(jnp.int32, powers.shape, 1)
        powers = jnp.where(query >= key, powers, 0.0)
    return powers / jnp.sum(powers, axis=-1, keepdims=True)


def attend_forward(packed, mixed, weights, begin, end, causal):
    length = weights.shape[3]
    width = mixed.shape[1]

    def one(n, carry):
        rows = pl.ds(pl.multiple_of(n * length, 16), length)
        for p in range(width // PAIR):
            lanes = p * PAIR
            q = packed[rows, lanes : lanes + PAIR]
            k = packed[rows, width + lanes : width + lanes + PAIR]
            v = packed[rows, 2 * width + lanes : 2 * width + lanes + PAIR]
            w = weights_of(q, k, causal).astype(jnp.bfloat16)
            weights[n, p] = w
            mixed[rows, lanes : lanes + PAIR] = unstacked(dot(w, v)).astype(jnp.bfloat16)
        return carry

    lax.fori_loop(begin, end, one, 0)


def attend_backward(packed, weights, d_mixed, d_packed, begin, end):
    length = weights.shape[3]
    width = d_mixed.shape[1]

    def one(n, carry):
        rows = pl.ds(pl.multiple_of(n * length, 16), length)
        for p in range(width // PAIR):
            lanes = p * PAIR
            q = packed[rows, lanes : lanes + PAIR]
            k = packed[rows, width + lanes : width + lanes + PAIR]
            v = packed[rows, 2 * width + lanes : 2 * width + lanes + PAIR]
            up = stacked(d_mixed[rows, lanes : lanes + PAIR])
            w = weights[n, p]
            wide = w.astype(jnp.float32)
            d_w = dot(up, v, NT).astype(jnp.bfloat16).astype(jnp.float32)
            d_scores = wide * (d_w - jnp.sum(d_w * wide, axis=-1, keepdims=True))
            d_scores = (d_scores * (1.0 / math.sqrt(SIZE))).astype(jnp.bfloat16)
            d_q = unstacked(dot(d_scores, k))
            d_k = dot(d_scores, stacked(q), TN)
            d_v = dot(w, up, TN)
            d_packed[rows, lanes : lanes + PAIR] = d_q.astype(jnp.bfloat16)
            d_packed[rows, width + lanes : width + lanes + PAIR] = d_k.astype(jnp.bfloat16)
            d_packed[rows, 2 * width + lanes : 2 * width + lanes + PAIR] = d_v.astype(jnp.bfloat16)
        return carry

    lax.fori_loop(begin, end, one, 0)


def selected(targets, rows, values):
    onehot = jnp.where(targets == lax.broadcasted_iota(jnp.int32, (rows, values.shape[0]), 0), 1.0, 0.0)
    return dot(onehot.astype(jnp.bfloat16), values)


def packed_rows(wire, at, values, block):
    rows, width = wire.shape[0], values.shape[1]
    tokens = values.shape[0]
    half = width // 2
    wire[:, :width] = selected(at[0:1, :tokens], rows, values).astype(jnp.bfloat16)
    low = selected(at[1:2, :tokens], rows, values[:, :half])
    high = selected(at[2:3, :tokens], rows, values[:, half:])
    wire[:, width:] = (low + high).astype(jnp.bfloat16)


def unpacked_rows(wire, at, tokens, width):
    rows = wire.shape[0]
    main = selected(at[0:1, :rows], tokens, wire[:, :width])
    low = selected(at[1:2, :rows], tokens, wire[:, width:])
    high = selected(at[2:3, :rows], tokens, wire[:, width:])
    return (main + jnp.concatenate([low, high], axis=1)).astype(jnp.bfloat16)


def routes(slots, count, feeders):
    device, slot, feeder = np.meshgrid(np.arange(count), np.arange(slots), np.arange(feeders), indexing="ij")
    place = slot * feeders + feeder
    tokens, rows = slots * count * feeders, count * 8
    found = []
    for order in (feeder * count * slots + device * slots + slot, slot * count * feeders + device * feeders + feeder):
        to, back = np.full((3, tokens), -1), np.full((3, tokens), -1)
        for kind, mine, row in (
            (0, place < 8, device * 8 + place),
            (1, place >= 8, device * 8 + place - 8),
            (2, place >= 8, device * 8 + place - 8 + (slots * feeders - 8)),
        ):
            to[kind, order[mine]] = row[mine]
            back[kind, row[mine]] = order[mine]
        found.append((to, back))
    assert 8 + 2 * (slots * feeders - 8) == 16
    (time_to, time_back), (feed_to, feed_back) = found
    table = np.full((32, tokens), -1)
    for n, rows in enumerate((time_to, feed_back, feed_to, time_back)):
        table[8 * n : 8 * n + 3] = rows
    return table.astype(np.int32)


def gradient_part(g, to, total):
    width = total.shape[0]
    slabs = width // LANES
    for slab in range(slabs):
        first = (to * slabs + slab) * width
        g[first : first + width, :] = total[:, slab * LANES : (slab + 1) * LANES].astype(jnp.bfloat16)


def step_kernel(
    batch, count,
    x_ref, row_ref, table_ref, time_qkv, time_out, feed_qkv_ref, feed_out_ref, route_ref, up_ref, partner_ref,
    load_ref, time_mean_ref, feed_mean_ref,
    feed_qkv, feed_out, adjoint,
    first, t_normed, t_packed, t_weights, t_mixed, f_normed, f_packed, f_weights, f_mixed,
    hidden, d_mixed, d_packed, sent, got, back, returned,
    t_g, t_inbox, t_pair, t_full, f_g, f_inbox, f_pair, f_full,
    wire_send, wire_recv, own_sem, fetch_sem, *sems,
):
    sequences, length, width = x_ref.shape
    feeders = sequences // batch
    groups = f_weights.shape[0] // batch
    tokens = feeders * length
    place = Place()
    greet(place, count)
    fetches = [
        pltpu.make_async_copy(source, target, fetch_sem.at[n])
        for n, (source, target) in enumerate(((feed_qkv_ref, feed_qkv), (feed_out_ref, feed_out), (up_ref, adjoint)))
    ]
    for fetch in fetches:
        fetch.start()
    t_sum = Reduction(TIME_PLAN, place, partner_ref, t_g, t_inbox, t_pair, t_full, time_mean_ref, sems[:7])
    f_sum = Reduction(FEED_PLAN, place, partner_ref, f_g, f_inbox, f_pair, f_full, feed_mean_ref, sems[7:])
    there, home = [], []
    for b in range(batch):
        pairs = ((there, sent, got, b), (home, back, returned, batch + b))
        for exchanges, source, target, n in pairs:
            exchanges.append(
                Exchange(count, source.at[b], target.at[b], wire_send.at[n], wire_recv.at[n], own_sem.at[n])
            )
    part_rows = 4 * width
    table_rows = table_ref.shape[0]
    onehot = (row_ref[...] == lax.broadcasted_iota(jnp.int32, (row_ref.shape[0], table_rows), 1)).astype(jnp.bfloat16)
    added = dot(onehot, table_ref[...])

    def time_forward(b):
        here = slice(b * tokens, (b + 1) * tokens)
        for n in range(feeders):
            rows = slice(b * tokens + n * length, b * tokens + (n + 1) * length)
            start = x_ref[b * feeders + n].astype(jnp.float32) + added[n : n + 1]
            first[rows, :] = start
            t_normed[rows, :] = (start * norm_factor(start)).astype(jnp.bfloat16)
        t_packed[here, :] = dot(t_normed[here, :], time_qkv[...]).astype(jnp.bfloat16)
        attend_forward(t_packed, t_mixed, t_weights, b * feeders, (b + 1) * feeders, True)
        result = (first[here, :] + dot(t_mixed[here, :], time_out[...])).astype(jnp.bfloat16)
        packed_rows(sent.at[b], route_ref[0:8, :], result, count)

    def feed_layer(b):
        here = slice(b * tokens, (b + 1) * tokens)
        hidden[here, :] = unpacked_rows(got[b], route_ref[8:16, :], tokens, width)
        wide = hidden[here, :].astype(jnp.float32)
        f_normed[here, :] = (wide * norm_factor(wide)).astype(jnp.bfloat16)
        f_packed[here, :] = dot(f_normed[here, :], feed_qkv[...]).astype(jnp.bfloat16)
        attend_forward(f_packed, f_mixed, f_weights, b * groups, (b + 1) * groups, False)
        result = hidden[here, :].astype(jnp.float32) + dot(f_mixed[here, :], feed_out[...])
        load_ref[b * groups : (b + 1) * groups] = result.astype(jnp.bfloat16).reshape(groups, -1, width)
        d_mixed[here, :] = dot(adjoint[here, :], feed_out[...], NT).astype(jnp.bfloat16)
        attend_backward(f_packed, f_weights, d_mixed, d_packed, b * groups, (b + 1) * groups)
        g = dot(d_packed[here, :], feed_qkv[...], NT).astype(jnp.bfloat16).astype(jnp.float32)
        wide = hidden[here, :].astype(jnp.float32)
        factor = norm_factor(wide)
        along = jnp.sum(g * wide, axis=-1, keepdims=True) * (factor * factor * factor) * (1.0 / width)
        d_hidden = (g * factor - wide * along).astype(jnp.bfloat16)
        total = (d_hidden.astype(jnp.float32) + adjoint[here, :].astype(jnp.float32)).astype(jnp.bfloat16)
        packed_rows(back.at[b], route_ref[16:24, :], total, count)

    def time_upstream(b):
        here = slice(b * tokens, (b + 1) * tokens)
        hidden[here, :] = unpacked_rows(returned[b], route_ref[24:32, :], tokens, width)

    def time_backward(b):
        here = slice(b * tokens, (b + 1) * tokens)
        d_mixed[here, :] = dot(hidden[here, :], time_out[...], NT).astype(jnp.bfloat16)
        attend_backward(t_packed, t_weights, d_mixed, d_packed, b * feeders, (b + 1) * feeders)

    def advance(codes):
        for code in codes:
            (f_sum if code >= 100 else t_sum).advance(code // 10 % 10, code % 10)

    for b in range(batch):
        time_forward(b)
        if b == 0:
            all_greeted(count)
        there[b].start()
    for fetch in fetches:
        fetch.wait()
    for b in range(batch):
        there[b].wait()
        feed_layer(b)
        home[b].start()

    for part in range(4):
        if part < 3:
            f_total = dot(f_normed[...], d_packed[:, part * width : (part + 1) * width], TN)
        else:
            f_total = dot(f_mixed[...], adjoint[...], TN)
        gradient_part(f_g, part, f_total)
        f_sum.start(part * part_rows, (part + 1) * part_rows)
    for b in range(batch):
        home[b].wait()
        time_upstream(b)
        if b == batch - 1:
            gradient_part(f_g, 4, dot(t_mixed[...], hidden[...], TN))
            f_sum.start(4 * part_rows, 5 * part_rows)
        time_backward(b)
        advance(ORDER[b])
    for part in range(3):
        gradient_part(t_g, part, dot(t_normed[...], d_packed[:, part * width : (part + 1) * width], TN))
        t_sum.start(part * part_rows, (part + 1) * part_rows)
        if part < 2:
            advance(ORDER[batch + part])
    advance(ORDER[4])
    f_sum.finish()
    t_sum.finish()


def finish_kernel(time_ref, feed_ref, out_ref, held, wide, in_sem, out_sem):
    slabs, depth, lanes = time_ref.shape[1:]
    rows = 4 * depth

    def get(n):
        layer, slab = n // slabs, n % slabs
        if layer:
            pieces = ((feed_ref.at[pl.ds(0, 4), slab], held.at[n]),)
        else:
            pieces = (
                (time_ref.at[:, slab], held.at[n, pl.ds(0, 3)]),
                (feed_ref.at[4, slab], held.at[n, 3]),
            )
        return [pltpu.make_async_copy(*piece, in_sem.at[n, i]) for i, piece in enumerate(pieces)]

    def put(n):
        target = out_ref.at[pl.ds(n // slabs * rows, rows), pl.ds(n % slabs * lanes, lanes)]
        return pltpu.make_async_copy(wide.at[n], target, out_sem.at[n])

    for n in range(2 * slabs):
        for copy in get(n):
            copy.start()
    for n in range(2 * slabs):
        for copy in get(n):
            copy.wait()
        for part in range(3):
            wide[n, pl.ds(part, depth, stride=3), :] = held[n, part].astype(jnp.float32)
        wide[n, 3 * depth :, :] = held[n, 3].astype(jnp.float32)
        put(n).start()
    for n in range(2 * slabs):
        put(n).wait()


def finished(time_mean, feed_mean):
    slabs, depth, lanes = time_mean.shape[1:]
    rows = 4 * depth
    return pl.pallas_call(
        finish_kernel,
        out_shape=jax.ShapeDtypeStruct((2 * rows, slabs * lanes), jnp.float32),
        in_specs=[ANY, ANY],
        out_specs=ANY,
        scratch_shapes=[
            pltpu.VMEM((2 * slabs, 4, depth, lanes), jnp.bfloat16),
            pltpu.VMEM((2 * slabs, rows, lanes), jnp.float32),
            pltpu.SemaphoreType.DMA((2 * slabs, 2)),
            pltpu.SemaphoreType.DMA((2 * slabs,)),
        ],
        compiler_params=pltpu.CompilerParams(vmem_limit_bytes=60 * 1024 * 1024),
    )(time_mean, feed_mean)


VMEM = pl.BlockSpec(memory_space=pltpu.VMEM)
ANY = pl.BlockSpec(memory_space=pl.ANY)


def on_device(
    measured_features,
    feeder_of_row,
    feeder_table,
    time_qkv,
    time_out,
    feed_qkv,
    feed_out,
    adjoint_of_prediction,
    round_index,
):
    batch, feed_local, slot_count, width = measured_features.shape
    feeder_count = adjoint_of_prediction.shape[1]
    slot_local = adjoint_of_prediction.shape[2]
    count = feeder_count // feed_local
    rows = batch * feed_local * slot_count
    pairs = width // PAIR
    bf16 = jnp.bfloat16
    sequences, groups = batch * feed_local, batch * slot_local

    route = jnp.asarray(routes(slot_local, count, feed_local))
    row_column = jnp.pad(feeder_of_row, (0, 8 - feed_local)).reshape(8, 1)
    partner = jnp.broadcast_to(round_index.astype(jnp.float32), (8, LANES))
    upstream = jnp.transpose(adjoint_of_prediction, (0, 2, 1, 3)).reshape(rows, width)
    part_rows = width * width // LANES
    time_rows, feed_rows = 3 * part_rows, 5 * part_rows

    def held(*shape):
        return pltpu.VMEM(shape, bf16)

    def reduction(n):
        return [held(n, LANES), held(n, LANES), held(len(PAIRS), n >> len(LINKS), LANES), held(n, LANES)]

    def semaphores(chains):
        steps = [COPIES, COPIES, len(PAIRS), len(PAIRS), COPIES, COPIES]
        return [pltpu.SemaphoreType.DMA((chains, s)) for s in steps] + [pltpu.SemaphoreType.DMA((chains,))]

    wire = held(batch, count * 8, width + width // 2)
    load, time_mean, feed_mean = pl.pallas_call(
        partial(step_kernel, batch, count),
        out_shape=(
            jax.ShapeDtypeStruct((groups, feeder_count, width), bf16),
            jax.ShapeDtypeStruct((time_rows, LANES), bf16),
            jax.ShapeDtypeStruct((feed_rows, LANES), bf16),
        ),
        in_specs=[VMEM, VMEM, VMEM, VMEM, VMEM, ANY, ANY, VMEM, ANY, VMEM],
        out_specs=(VMEM, ANY, ANY),
        scratch_shapes=[
            held(width, 3 * width),
            held(width, width),
            held(rows, width),
            pltpu.VMEM((rows, width), jnp.float32),
            held(rows, width),
            held(rows, 3 * width),
            held(sequences, pairs, 2 * slot_count, slot_count),
            held(rows, width),
            held(rows, width),
            held(rows, 3 * width),
            held(groups, pairs, 2 * feeder_count, feeder_count),
            held(rows, width),
            held(rows, width),
            held(rows, width),
            held(rows, 3 * width),
            wire,
            wire,
            wire,
            wire,
        ]
        + reduction(time_rows)
        + reduction(feed_rows)
        + [pltpu.SemaphoreType.DMA((2 * batch, count))] * 2
        + [pltpu.SemaphoreType.DMA((2 * batch,)), pltpu.SemaphoreType.DMA((3,))]
        + semaphores(len(TIME_PLAN))
        + semaphores(len(FEED_PLAN)),
        compiler_params=pltpu.CompilerParams(collective_id=1, has_side_effects=True, vmem_limit_bytes=60 * 1024 * 1024),
    )(
        measured_features.reshape(sequences, slot_count, width),
        row_column,
        feeder_table,
        time_qkv,
        time_out,
        feed_qkv,
        feed_out,
        route,
        upstream,
        partner,
    )
    predicted_load = jnp.transpose(load.reshape(batch, slot_local, feeder_count, width), (0, 2, 1, 3))
    slabs = (width // LANES, width, LANES)
    gradients = finished(time_mean.reshape(3, *slabs), feed_mean.reshape(5, *slabs))
    return (predicted_load, gradients[None])


def solution(mesh):
    placed = (
        P("gossip", "field", None, None),
        P("field"),
        P(),
        P(),
        P(),
        P(),
        P(),
        P("gossip", None, "field", None),
        P(),
    )
    return jax.shard_map(
        on_device,
        mesh=mesh,
        in_specs=placed,
        out_specs=(P("gossip", None, "field", None), P("gossip", None, None)),
        check_vma=False,
    )
```

```python
from functools import partial
import math

import jax
import jax.numpy as jnp
import numpy as np
from jax import lax
from jax.experimental import pallas as pl
from jax.experimental.pallas import tpu as pltpu
from jax.sharding import PartitionSpec as P

epsilon = 1e-05


MESH = pl.DeviceIdType.MESH
LANES = 128
LINKS = ("ya", "za", "xa", "yb", "zb")
PAIRS = ("core", "xb")
GROUPS = (1, 1, 1, 2)
STEPS = len(GROUPS)
TURNS = 2 * STEPS + 1
COPIES = sum(2**size - 1 for size in GROUPS)

TIME_PLAN = (
    (2, (3, 1, 0, 4, 2)),
    (2, (2, 0, 1, 3, 4)),
    (1, (1, 2, 3, 4, 0)),
    (2, (1, 0, 3, 2, 4)),
    (1, (3, 4, 1, 0, 2)),
    (1, (4, 3, 1, 2, 0)),
    (2, (2, 4, 3, 0, 1)),
    (1, (0, 3, 1, 4, 2)),
)
FEED_PLAN = (
    (1, (0, 1, 3, 2, 4)),
    (2, (2, 4, 3, 0, 1)),
    (1, (3, 1, 2, 0, 4)),
    (3, (1, 4, 0, 3, 2)),
    (3, (0, 3, 1, 4, 2)),
    (3, (4, 0, 3, 2, 1)),
    (2, (4, 2, 3, 0, 1)),
    (1, (0, 3, 4, 2, 1)),
    (2, (3, 4, 2, 1, 0)),
    (2, (2, 1, 0, 3, 4)),
)

ORDER = (
    (),
    (100, 120),
    (),
    (110,),
    (
        130, 150, 180, 140, 190, 101, 121, 160, 170, 20, 0, 10, 111, 40, 131, 151,
        30, 60, 122, 141, 181, 70, 102, 191, 161, 171, 50, 11, 21, 112, 1, 41,
        132, 152, 61, 182, 142, 71, 31, 162, 172, 192, 123, 103, 12, 51, 22, 42,
        2, 113, 133, 62, 72, 153, 183, 32, 143, 124, 104, 163, 173, 52, 193, 13,
        114, 23, 43, 134, 3, 154, 184, 63, 73, 144, 164, 174, 33, 125, 194, 105,
        14, 24, 53, 44, 4, 115, 64, 74, 135, 155, 34, 185, 126, 145, 165, 175,
        106, 54, 195, 15, 25, 116, 45, 5, 65, 75, 136, 156, 186, 127, 35, 176,
        166, 146, 196, 55, 26, 107, 16, 6, 66, 117, 46, 76, 128, 157, 137, 167,
        36, 197, 27, 177, 56, 108, 187, 7, 17, 67, 147, 47, 77, 118, 37, 57,
        178, 198, 138, 158, 188, 28, 18, 168, 148, 8, 38, 58, 78, 48, 68,
    ),
)


class Place:
    def __init__(self):
        gossip, field = lax.axis_index("gossip"), lax.axis_index("field")
        x_hi, core = gossip // 2, gossip % 2
        x_lo, z, y = field // 16, (field // 4) % 4, field % 4
        self.here = {"x_hi": x_hi, "core": core, "x_lo": x_lo, "z": z, "y": y}
        self.bit = {
            "ya": ((y + 1) // 2) % 2,
            "yb": y // 2,
            "za": ((z + 1) // 2) % 2,
            "zb": z // 2,
            "xa": (x_hi + x_lo) % 2,
        }
        self.flip = {
            "ya": {"y": y + 1 - 2 * (y % 2)},
            "yb": {"y": 3 - y},
            "za": {"z": z + 1 - 2 * (z % 2)},
            "zb": {"z": 3 - z},
            "xa": {"x_lo": 1 - x_lo},
            "xb": {"x_hi": 1 - x_hi, "x_lo": 1 - x_lo},
            "core": {"core": 1 - core},
        }

    def across(self, *names):
        at = dict(self.here)
        for name in names:
            at.update(self.flip[name])
        return (at["x_hi"] * 2 + at["core"], (at["x_lo"] * 4 + at["z"]) * 4 + at["y"])


def chains_of(plan):
    chains, first = [], 0
    for units, turns in plan:
        names = [LINKS[turn] for turn in turns]
        groups = tuple(tuple(names[sum(GROUPS[:s]) : sum(GROUPS[: s + 1])]) for s in range(STEPS))
        chains.append((first, units * 512, groups))
        first += units * 512
    return chains


def block_of(rows):
    for parts in range(1, rows + 1):
        if rows % parts == 0 and rows // parts <= 256 and (rows // parts) % 16 == 0:
            return rows // parts
    return rows


class Reduction:
    def __init__(self, plan, place, partner, g, inbox, pairbox, full, out, sems):
        self.place, self.partner = place, partner
        self.g, self.inbox, self.pairbox, self.full, self.out = g, inbox, pairbox, full, out
        self.rs_send, self.rs_recv, self.pair_send, self.pair_recv, self.ag_send, self.ag_recv, self.out_sem = sems
        self.chains = chains_of(plan)
        assert sum(rows for first, rows, groups in self.chains) == g.shape[0]
        self.at = []
        self.steps = []
        for first, rows, groups in self.chains:
            at, size, sem, steps = [first], rows, 0, []
            for names in groups:
                part = size >> len(names)
                peers = []
                for mask in range(1, 2 ** len(names)):
                    flipped = [name for n, name in enumerate(names) if mask >> n & 1]
                    offset = at[-1]
                    for n, name in enumerate(names):
                        bit = place.bit[name]
                        offset = offset + (1 - bit if name in flipped else bit) * (size >> (n + 1))
                    slot = first + rows - size + (mask - 1) * part
                    peers.append((place.across(*flipped), offset, slot, sem))
                    sem += 1
                mine = at[-1]
                for n, name in enumerate(names):
                    mine = mine + place.bit[name] * (size >> (n + 1))
                steps.append((part, peers))
                at.append(mine)
                size = part
            self.at.append(at)
            self.steps.append(steps)

    def rs_copies(self, j, s):
        part, peers = self.steps[j][s]
        return [
            pltpu.make_async_remote_copy(
                src_ref=self.g.at[pl.ds(pl.multiple_of(offset, 16), part)],
                dst_ref=self.inbox.at[pl.ds(slot, part)],
                send_sem=self.rs_send.at[j, sem],
                recv_sem=self.rs_recv.at[j, sem],
                device_id=peer,
                device_id_type=MESH,
            )
            for peer, offset, slot, sem in peers
        ]

    def rs_add(self, j, s):
        part, peers = self.steps[j][s]
        keep = self.at[j][s + 1]
        block = block_of(part)

        def add(i, carry):
            here = pl.ds(pl.multiple_of(keep + i * block, 16), block)
            total = self.g[here, :]
            if len(peers) > 1:
                total = total.astype(jnp.float32)
            for peer, offset, slot, sem in peers:
                there = pl.ds(pl.multiple_of(slot + i * block, 16), block)
                total = total + self.inbox[there, :].astype(total.dtype)
            self.g[here, :] = total.astype(jnp.bfloat16)
            return carry

        lax.fori_loop(0, part // block, add, 0)

    def shard(self, j):
        first, rows, groups = self.chains[j]
        count = rows >> len(LINKS)
        return pl.ds(pl.multiple_of(self.at[j][STEPS], 16), count), pl.ds(first >> len(LINKS), count)

    def pair_copy(self, j, n):
        here, there = self.shard(j)
        return pltpu.make_async_remote_copy(
            src_ref=self.g.at[here],
            dst_ref=self.pairbox.at[n, there],
            send_sem=self.pair_send.at[j, n],
            recv_sem=self.pair_recv.at[j, n],
            device_id=self.place.across(PAIRS[n]),
            device_id_type=MESH,
        )

    def pair_mean(self, j):
        here, there = self.shard(j)
        other = jnp.where(
            self.partner[0:1, :] > 0.0,
            self.pairbox[1, there, :].astype(jnp.float32),
            self.pairbox[0, there, :].astype(jnp.float32),
        )
        self.full[here, :] = ((self.g[here, :].astype(jnp.float32) + other) * 0.5).astype(jnp.bfloat16)

    def ag_copies(self, j, s):
        part, peers = self.steps[j][s]
        mine = self.full.at[pl.ds(pl.multiple_of(self.at[j][s + 1], 16), part)]
        return [
            pltpu.make_async_remote_copy(
                src_ref=mine,
                dst_ref=mine,
                send_sem=self.ag_send.at[j, sem],
                recv_sem=self.ag_recv.at[j, sem],
                device_id=peer,
                device_id_type=MESH,
            )
            for peer, offset, slot, sem in peers
        ]

    def out_copy(self, j):
        part = pl.ds(self.chains[j][0], self.chains[j][1])
        return pltpu.make_async_copy(self.full.at[part], self.out.at[part], self.out_sem.at[j])

    def start(self, begin, end):
        for j, (first, rows, groups) in enumerate(self.chains):
            if begin < first + rows <= end:
                for copy in self.rs_copies(j, 0):
                    copy.start()

    def advance(self, j, stage):
        following = []
        if stage < STEPS:
            for copy in self.rs_copies(j, stage):
                copy.wait()
            self.rs_add(j, stage)
            if stage + 1 < STEPS:
                following = self.rs_copies(j, stage + 1)
            else:
                following = [self.pair_copy(j, n) for n in range(len(PAIRS))]
        elif stage == STEPS:
            for n in range(len(PAIRS)):
                self.pair_copy(j, n).wait()
            self.pair_mean(j)
            following = self.ag_copies(j, STEPS - 1)
        else:
            s = 2 * STEPS - stage
            for copy in self.ag_copies(j, s):
                copy.wait()
            following = self.ag_copies(j, s - 1) if s > 0 else [self.out_copy(j)]
        for copy in following:
            copy.start()

    def finish(self):
        for j in range(len(self.chains)):
            self.out_copy(j).wait()


class Exchange:
    def __init__(self, count, send, got, send_sem, recv_sem, own_sem):
        self.count, self.send, self.got = count, send, got
        self.send_sem, self.recv_sem, self.own_sem = send_sem, recv_sem, own_sem
        self.gossip, self.me = lax.axis_index("gossip"), lax.axis_index("field")
        self.rows = send.shape[0] // count

    def block(self, i):
        return pl.ds(pl.multiple_of(i * self.rows, 8), self.rows)

    def own(self):
        here = self.block(self.me)
        return pltpu.make_async_copy(self.send.at[here], self.got.at[here], self.own_sem)

    def copy(self, i):
        to = lax.rem(self.me + i, self.count)
        return pltpu.make_async_remote_copy(
            src_ref=self.send.at[self.block(to)],
            dst_ref=self.got.at[self.block(self.me)],
            send_sem=self.send_sem.at[i],
            recv_sem=self.recv_sem.at[i],
            device_id=(self.gossip, to),
            device_id_type=MESH,
        )

    def start(self):
        def one(i, carry):
            self.copy(i).start()
            return carry

        lax.fori_loop(1, self.count, one, 0)
        self.own().start()

    def wait(self):
        def one(i, carry):
            self.copy(i).wait()
            return carry

        lax.fori_loop(1, self.count, one, 0)
        self.own().wait()


def greet(place, count):
    barrier = pltpu.get_barrier_semaphore()
    gossip, me = lax.axis_index("gossip"), lax.axis_index("field")

    def one(i, carry):
        peer = (gossip, lax.rem(me + i, count))
        pl.semaphore_signal(barrier, inc=1, device_id=peer, device_id_type=MESH)
        return carry

    lax.fori_loop(1, count, one, 0)
    for name in PAIRS:
        pl.semaphore_signal(barrier, inc=1, device_id=place.across(name), device_id_type=MESH)


def all_greeted(count):
    pl.semaphore_wait(pltpu.get_barrier_semaphore(), count - 1 + len(PAIRS))


SIZE = 64
PAIR = 2 * SIZE


def dot(a, b, contract=((1,), (0,))):
    return lax.dot_general(a, b, (contract, ((), ())), preferred_element_type=jnp.float32)


NT = ((1,), (1,))
TN = ((0,), (0,))


def first_lanes(rows):
    return lax.broadcasted_iota(jnp.int32, (rows, PAIR), 1) < SIZE


def stacked(pair):
    low = first_lanes(pair.shape[0])
    nothing = jnp.zeros_like(pair)
    return jnp.concatenate([jnp.where(low, pair, nothing), jnp.where(low, nothing, pair)], axis=0)


def unstacked(both):
    rows = both.shape[0] // 2
    return jnp.where(first_lanes(rows), both[:rows], both[rows:])


def norm_factor(wide):
    return lax.rsqrt(jnp.mean(wide * wide, axis=-1, keepdims=True) + epsilon)


def weights_of(q, k, causal):
    length = k.shape[0]
    powers = jnp.exp(dot(stacked(q), k, NT) * (1.0 / math.sqrt(SIZE)))
    if causal:
        query = lax.broadcasted_iota(jnp.int32, powers.shape, 0) % length
        key = lax.broadcasted_iota(jnp.int32, powers.shape, 1)
        powers = jnp.where(query >= key, powers, 0.0)
    return powers / jnp.sum(powers, axis=-1, keepdims=True)


def attend_forward(packed, mixed, weights, begin, end, causal):
    length = weights.shape[3]
    width = mixed.shape[1]

    def one(n, carry):
        rows = pl.ds(pl.multiple_of(n * length, 16), length)
        for p in range(width // PAIR):
            lanes = p * PAIR
            q = packed[rows, lanes : lanes + PAIR]
            k = packed[rows, width + lanes : width + lanes + PAIR]
            v = packed[rows, 2 * width + lanes : 2 * width + lanes + PAIR]
            w = weights_of(q, k, causal).astype(jnp.bfloat16)
            weights[n, p] = w
            mixed[rows, lanes : lanes + PAIR] = unstacked(dot(w, v)).astype(jnp.bfloat16)
        return carry

    lax.fori_loop(begin, end, one, 0)


def attend_backward(packed, weights, d_mixed, d_packed, begin, end):
    length = weights.shape[3]
    width = d_mixed.shape[1]

    def one(n, carry):
        rows = pl.ds(pl.multiple_of(n * length, 16), length)
        for p in range(width // PAIR):
            lanes = p * PAIR
            q = packed[rows, lanes : lanes + PAIR]
            k = packed[rows, width + lanes : width + lanes + PAIR]
            v = packed[rows, 2 * width + lanes : 2 * width + lanes + PAIR]
            up = stacked(d_mixed[rows, lanes : lanes + PAIR])
            w = weights[n, p]
            wide = w.astype(jnp.float32)
            d_w = dot(up, v, NT).astype(jnp.bfloat16).astype(jnp.float32)
            d_scores = wide * (d_w - jnp.sum(d_w * wide, axis=-1, keepdims=True))
            d_scores = (d_scores * (1.0 / math.sqrt(SIZE))).astype(jnp.bfloat16)
            d_q = unstacked(dot(d_scores, k))
            d_k = dot(d_scores, stacked(q), TN)
            d_v = dot(w, up, TN)
            d_packed[rows, lanes : lanes + PAIR] = d_q.astype(jnp.bfloat16)
            d_packed[rows, width + lanes : width + lanes + PAIR] = d_k.astype(jnp.bfloat16)
            d_packed[rows, 2 * width + lanes : 2 * width + lanes + PAIR] = d_v.astype(jnp.bfloat16)
        return carry

    lax.fori_loop(begin, end, one, 0)


def selected(targets, rows, values):
    onehot = jnp.where(targets == lax.broadcasted_iota(jnp.int32, (rows, values.shape[0]), 0), 1.0, 0.0)
    return dot(onehot.astype(jnp.bfloat16), values)


def packed_rows(wire, at, values, block):
    rows, width = wire.shape[0], values.shape[1]
    tokens = values.shape[0]
    half = width // 2
    wire[:, :width] = selected(at[0:1, :tokens], rows, values).astype(jnp.bfloat16)
    low = selected(at[1:2, :tokens], rows, values[:, :half])
    high = selected(at[2:3, :tokens], rows, values[:, half:])
    wire[:, width:] = (low + high).astype(jnp.bfloat16)


def unpacked_rows(wire, at, tokens, width):
    rows = wire.shape[0]
    main = selected(at[0:1, :rows], tokens, wire[:, :width])
    low = selected(at[1:2, :rows], tokens, wire[:, width:])
    high = selected(at[2:3, :rows], tokens, wire[:, width:])
    return (main + jnp.concatenate([low, high], axis=1)).astype(jnp.bfloat16)


def routes(slots, count, feeders):
    device, slot, feeder = np.meshgrid(np.arange(count), np.arange(slots), np.arange(feeders), indexing="ij")
    place = slot * feeders + feeder
    tokens, rows = slots * count * feeders, count * 8
    found = []
    for order in (feeder * count * slots + device * slots + slot, slot * count * feeders + device * feeders + feeder):
        to, back = np.full((3, tokens), -1), np.full((3, tokens), -1)
        for kind, mine, row in (
            (0, place < 8, device * 8 + place),
            (1, place >= 8, device * 8 + place - 8),
            (2, place >= 8, device * 8 + place - 8 + (slots * feeders - 8)),
        ):
            to[kind, order[mine]] = row[mine]
            back[kind, row[mine]] = order[mine]
        found.append((to, back))
    assert 8 + 2 * (slots * feeders - 8) == 16
    (time_to, time_back), (feed_to, feed_back) = found
    table = np.full((32, tokens), -1)
    for n, rows in enumerate((time_to, feed_back, feed_to, time_back)):
        table[8 * n : 8 * n + 3] = rows
    return table.astype(np.int32)


def gradient_part(g, to, total):
    width = total.shape[0]
    slabs = width // LANES
    for slab in range(slabs):
        first = (to * slabs + slab) * width
        g[first : first + width, :] = total[:, slab * LANES : (slab + 1) * LANES].astype(jnp.bfloat16)


def step_kernel(
    batch, count,
    x_ref, row_ref, table_ref, time_qkv, time_out, feed_qkv_ref, feed_out_ref, route_ref, up_ref, partner_ref,
    load_ref, time_mean_ref, feed_mean_ref,
    feed_qkv, feed_out, adjoint,
    first, t_normed, t_packed, t_weights, t_mixed, f_normed, f_packed, f_weights, f_mixed,
    hidden, d_mixed, d_packed, sent, got, back, returned,
    t_g, t_inbox, t_pair, t_full, f_g, f_inbox, f_pair, f_full,
    wire_send, wire_recv, own_sem, fetch_sem, *sems,
):
    sequences, length, width = x_ref.shape
    feeders = sequences // batch
    groups = f_weights.shape[0] // batch
    tokens = feeders * length
    place = Place()
    greet(place, count)
    fetches = [
        pltpu.make_async_copy(source, target, fetch_sem.at[n])
        for n, (source, target) in enumerate(((feed_qkv_ref, feed_qkv), (feed_out_ref, feed_out), (up_ref, adjoint)))
    ]
    for fetch in fetches:
        fetch.start()
    t_sum = Reduction(TIME_PLAN, place, partner_ref, t_g, t_inbox, t_pair, t_full, time_mean_ref, sems[:7])
    f_sum = Reduction(FEED_PLAN, place, partner_ref, f_g, f_inbox, f_pair, f_full, feed_mean_ref, sems[7:])
    there, home = [], []
    for b in range(batch):
        pairs = ((there, sent, got, b), (home, back, returned, batch + b))
        for exchanges, source, target, n in pairs:
            exchanges.append(
                Exchange(count, source.at[b], target.at[b], wire_send.at[n], wire_recv.at[n], own_sem.at[n])
            )
    part_rows = 4 * width
    table_rows = table_ref.shape[0]
    onehot = (row_ref[...] == lax.broadcasted_iota(jnp.int32, (row_ref.shape[0], table_rows), 1)).astype(jnp.bfloat16)
    added = dot(onehot, table_ref[...])

    def time_forward(b):
        here = slice(b * tokens, (b + 1) * tokens)
        for n in range(feeders):
            rows = slice(b * tokens + n * length, b * tokens + (n + 1) * length)
            start = x_ref[b * feeders + n].astype(jnp.float32) + added[n : n + 1]
            first[rows, :] = start
            t_normed[rows, :] = (start * norm_factor(start)).astype(jnp.bfloat16)
        t_packed[here, :] = dot(t_normed[here, :], time_qkv[...]).astype(jnp.bfloat16)
        attend_forward(t_packed, t_mixed, t_weights, b * feeders, (b + 1) * feeders, True)
        result = (first[here, :] + dot(t_mixed[here, :], time_out[...])).astype(jnp.bfloat16)
        packed_rows(sent.at[b], route_ref[0:8, :], result, count)

    def feed_layer(b):
        here = slice(b * tokens, (b + 1) * tokens)
        hidden[here, :] = unpacked_rows(got[b], route_ref[8:16, :], tokens, width)
        wide = hidden[here, :].astype(jnp.float32)
        f_normed[here, :] = (wide * norm_factor(wide)).astype(jnp.bfloat16)
        f_packed[here, :] = dot(f_normed[here, :], feed_qkv[...]).astype(jnp.bfloat16)
        attend_forward(f_packed, f_mixed, f_weights, b * groups, (b + 1) * groups, False)
        result = hidden[here, :].astype(jnp.float32) + dot(f_mixed[here, :], feed_out[...])
        load_ref[b * groups : (b + 1) * groups] = result.astype(jnp.bfloat16).reshape(groups, -1, width)
        attend_backward(f_packed, f_weights, d_mixed, d_packed, b * groups, (b + 1) * groups)
        g = dot(d_packed[here, :], feed_qkv[...], NT).astype(jnp.bfloat16).astype(jnp.float32)
        wide = hidden[here, :].astype(jnp.float32)
        factor = norm_factor(wide)
        along = jnp.sum(g * wide, axis=-1, keepdims=True) * (factor * factor * factor) * (1.0 / width)
        d_hidden = (g * factor - wide * along).astype(jnp.bfloat16)
        total = (d_hidden.astype(jnp.float32) + adjoint[here, :].astype(jnp.float32)).astype(jnp.bfloat16)
        packed_rows(back.at[b], route_ref[16:24, :], total, count)

    def time_upstream(b):
        here = slice(b * tokens, (b + 1) * tokens)
        hidden[here, :] = unpacked_rows(returned[b], route_ref[24:32, :], tokens, width)

    def time_backward(b):
        here = slice(b * tokens, (b + 1) * tokens)
        d_mixed[here, :] = dot(hidden[here, :], time_out[...], NT).astype(jnp.bfloat16)
        attend_backward(t_packed, t_weights, d_mixed, d_packed, b * feeders, (b + 1) * feeders)

    def advance(codes):
        for code in codes:
            (f_sum if code >= 100 else t_sum).advance(code // 10 % 10, code % 10)

    for b in range(batch):
        time_forward(b)
        if b == 0:
            all_greeted(count)
        there[b].start()
    for fetch in fetches:
        fetch.wait()
    d_mixed[...] = dot(adjoint[...], feed_out[...], NT).astype(jnp.bfloat16)
    for b in range(batch):
        there[b].wait()
        feed_layer(b)
        home[b].start()

    for part in range(4):
        if part < 3:
            f_total = dot(f_normed[...], d_packed[:, part * width : (part + 1) * width], TN)
        else:
            f_total = dot(f_mixed[...], adjoint[...], TN)
        gradient_part(f_g, part, f_total)
        f_sum.start(part * part_rows, (part + 1) * part_rows)
    for b in range(batch):
        home[b].wait()
        time_upstream(b)
        if b == batch - 1:
            gradient_part(f_g, 4, dot(t_mixed[...], hidden[...], TN))
            f_sum.start(4 * part_rows, 5 * part_rows)
        time_backward(b)
        advance(ORDER[b])
    for part in range(3):
        gradient_part(t_g, part, dot(t_normed[...], d_packed[:, part * width : (part + 1) * width], TN))
        t_sum.start(part * part_rows, (part + 1) * part_rows)
        if part < 2:
            advance(ORDER[batch + part])
    advance(ORDER[4])
    f_sum.finish()
    t_sum.finish()


def finish_kernel(time_ref, feed_ref, out_ref, held, wide, in_sem, out_sem):
    slabs, depth, lanes = time_ref.shape[1:]
    rows = 4 * depth

    def get(n):
        layer, slab = n // slabs, n % slabs
        if layer:
            pieces = ((feed_ref.at[pl.ds(0, 4), slab], held.at[n]),)
        else:
            pieces = (
                (time_ref.at[:, slab], held.at[n, pl.ds(0, 3)]),
                (feed_ref.at[4, slab], held.at[n, 3]),
            )
        return [pltpu.make_async_copy(*piece, in_sem.at[n, i]) for i, piece in enumerate(pieces)]

    def put(n):
        target = out_ref.at[pl.ds(n // slabs * rows, rows), pl.ds(n % slabs * lanes, lanes)]
        return pltpu.make_async_copy(wide.at[n], target, out_sem.at[n])

    for n in range(2 * slabs):
        for copy in get(n):
            copy.start()
    for n in range(2 * slabs):
        for copy in get(n):
            copy.wait()
        for part in range(3):
            wide[n, pl.ds(part, depth, stride=3), :] = held[n, part].astype(jnp.float32)
        wide[n, 3 * depth :, :] = held[n, 3].astype(jnp.float32)
        put(n).start()
    for n in range(2 * slabs):
        put(n).wait()


def finished(time_mean, feed_mean):
    slabs, depth, lanes = time_mean.shape[1:]
    rows = 4 * depth
    return pl.pallas_call(
        finish_kernel,
        out_shape=jax.ShapeDtypeStruct((2 * rows, slabs * lanes), jnp.float32),
        in_specs=[ANY, ANY],
        out_specs=ANY,
        scratch_shapes=[
            pltpu.VMEM((2 * slabs, 4, depth, lanes), jnp.bfloat16),
            pltpu.VMEM((2 * slabs, rows, lanes), jnp.float32),
            pltpu.SemaphoreType.DMA((2 * slabs, 2)),
            pltpu.SemaphoreType.DMA((2 * slabs,)),
        ],
        compiler_params=pltpu.CompilerParams(vmem_limit_bytes=60 * 1024 * 1024),
    )(time_mean, feed_mean)


VMEM = pl.BlockSpec(memory_space=pltpu.VMEM)
ANY = pl.BlockSpec(memory_space=pl.ANY)


def on_device(
    measured_features,
    feeder_of_row,
    feeder_table,
    time_qkv,
    time_out,
    feed_qkv,
    feed_out,
    adjoint_of_prediction,
    round_index,
):
    batch, feed_local, slot_count, width = measured_features.shape
    feeder_count = adjoint_of_prediction.shape[1]
    slot_local = adjoint_of_prediction.shape[2]
    count = feeder_count // feed_local
    rows = batch * feed_local * slot_count
    pairs = width // PAIR
    bf16 = jnp.bfloat16
    sequences, groups = batch * feed_local, batch * slot_local

    route = jnp.asarray(routes(slot_local, count, feed_local))
    row_column = jnp.pad(feeder_of_row, (0, 8 - feed_local)).reshape(8, 1)
    partner = jnp.broadcast_to(round_index.astype(jnp.float32), (8, LANES))
    upstream = jnp.transpose(adjoint_of_prediction, (0, 2, 1, 3)).reshape(rows, width)
    part_rows = width * width // LANES
    time_rows, feed_rows = 3 * part_rows, 5 * part_rows

    def held(*shape):
        return pltpu.VMEM(shape, bf16)

    def reduction(n):
        return [held(n, LANES), held(n, LANES), held(len(PAIRS), n >> len(LINKS), LANES), held(n, LANES)]

    def semaphores(chains):
        steps = [COPIES, COPIES, len(PAIRS), len(PAIRS), COPIES, COPIES]
        return [pltpu.SemaphoreType.DMA((chains, s)) for s in steps] + [pltpu.SemaphoreType.DMA((chains,))]

    wire = held(batch, count * 8, width + width // 2)
    load, time_mean, feed_mean = pl.pallas_call(
        partial(step_kernel, batch, count),
        out_shape=(
            jax.ShapeDtypeStruct((groups, feeder_count, width), bf16),
            jax.ShapeDtypeStruct((time_rows, LANES), bf16),
            jax.ShapeDtypeStruct((feed_rows, LANES), bf16),
        ),
        in_specs=[VMEM, VMEM, VMEM, VMEM, VMEM, ANY, ANY, VMEM, ANY, VMEM],
        out_specs=(VMEM, ANY, ANY),
        scratch_shapes=[
            held(width, 3 * width),
            held(width, width),
            held(rows, width),
            pltpu.VMEM((rows, width), jnp.float32),
            held(rows, width),
            held(rows, 3 * width),
            held(sequences, pairs, 2 * slot_count, slot_count),
            held(rows, width),
            held(rows, width),
            held(rows, 3 * width),
            held(groups, pairs, 2 * feeder_count, feeder_count),
            held(rows, width),
            held(rows, width),
            held(rows, width),
            held(rows, 3 * width),
            wire,
            wire,
            wire,
            wire,
        ]
        + reduction(time_rows)
        + reduction(feed_rows)
        + [pltpu.SemaphoreType.DMA((2 * batch, count))] * 2
        + [pltpu.SemaphoreType.DMA((2 * batch,)), pltpu.SemaphoreType.DMA((3,))]
        + semaphores(len(TIME_PLAN))
        + semaphores(len(FEED_PLAN)),
        compiler_params=pltpu.CompilerParams(collective_id=1, has_side_effects=True, vmem_limit_bytes=60 * 1024 * 1024),
    )(
        measured_features.reshape(sequences, slot_count, width),
        row_column,
        feeder_table,
        time_qkv,
        time_out,
        feed_qkv,
        feed_out,
        route,
        upstream,
        partner,
    )
    predicted_load = jnp.transpose(load.reshape(batch, slot_local, feeder_count, width), (0, 2, 1, 3))
    slabs = (width // LANES, width, LANES)
    gradients = finished(time_mean.reshape(3, *slabs), feed_mean.reshape(5, *slabs))
    return (predicted_load, gradients[None])


def solution(mesh):
    placed = (
        P("gossip", "field", None, None),
        P("field"),
        P(),
        P(),
        P(),
        P(),
        P(),
        P("gossip", None, "field", None),
        P(),
    )
    return jax.shard_map(
        on_device,
        mesh=mesh,
        in_specs=placed,
        out_specs=(P("gossip", None, "field", None), P("gossip", None, None)),
        check_vma=False,
    )
```

```python
from functools import partial
import math

import jax
import jax.numpy as jnp
import numpy as np
from jax import lax
from jax.experimental import pallas as pl
from jax.experimental.pallas import tpu as pltpu
from jax.sharding import PartitionSpec as P

epsilon = 1e-05


MESH = pl.DeviceIdType.MESH
LANES = 128
LINKS = ("ya", "za", "xa", "yb", "zb")
PAIRS = ("core", "xb")
GROUPS = (1, 1, 1, 2)
STEPS = len(GROUPS)
TURNS = 2 * STEPS + 1
COPIES = sum(2**size - 1 for size in GROUPS)

TIME_PLAN = (
    (1, (3, 2, 4, 1, 0)),
    (2, (1, 4, 0, 3, 2)),
    (1, (4, 0, 2, 3, 1)),
    (2, (4, 0, 2, 3, 1)),
    (2, (3, 1, 0, 4, 2)),
    (2, (0, 3, 4, 2, 1)),
    (1, (3, 1, 4, 0, 2)),
    (1, (0, 2, 4, 3, 1)),
)
FEED_PLAN = (
    (3, (2, 1, 3, 4, 0)),
    (2, (2, 3, 1, 0, 4)),
    (1, (0, 4, 1, 3, 2)),
    (2, (4, 0, 3, 2, 1)),
    (1, (1, 0, 3, 2, 4)),
    (1, (3, 2, 4, 0, 1)),
    (3, (0, 2, 4, 1, 3)),
    (3, (1, 2, 3, 0, 4)),
    (2, (3, 2, 1, 0, 4)),
    (2, (4, 1, 0, 3, 2)),
)

ORDER = (
    (),
    (120, 140, 150),
    (130,),
    (100, 180),
    (
        160, 170, 190, 121, 141, 110, 151, 0, 20, 131, 10, 181, 30, 40, 152, 101,
        161, 50, 60, 142, 191, 70, 122, 11, 171, 21, 111, 182, 1, 132, 31, 41,
        162, 102, 61, 153, 192, 143, 71, 51, 12, 22, 112, 2, 123, 172, 183, 32,
        133, 42, 154, 144, 163, 62, 72, 103, 193, 52, 124, 13, 23, 184, 134, 113,
        3, 173, 33, 164, 43, 155, 104, 145, 194, 63, 73, 14, 24, 53, 125, 114,
        4, 185, 174, 135, 34, 44, 156, 146, 64, 74, 165, 54, 105, 195, 126, 15,
        25, 115, 186, 5, 136, 175, 157, 45, 147, 35, 75, 166, 65, 196, 55, 106,
        26, 127, 16, 116, 6, 187, 176, 137, 76, 36, 46, 66, 148, 158, 56, 27,
        197, 167, 17, 117, 7, 128, 107, 37, 177, 138, 47, 188, 77, 67, 28, 57,
        8, 118, 18, 168, 198, 78, 48, 38, 68, 108, 178, 58,
    ),
)


class Place:
    def __init__(self):
        gossip, field = lax.axis_index("gossip"), lax.axis_index("field")
        x_hi, core = gossip // 2, gossip % 2
        x_lo, z, y = field // 16, (field // 4) % 4, field % 4
        self.here = {"x_hi": x_hi, "core": core, "x_lo": x_lo, "z": z, "y": y}
        self.bit = {
            "ya": ((y + 1) // 2) % 2,
            "yb": y // 2,
            "za": ((z + 1) // 2) % 2,
            "zb": z // 2,
            "xa": (x_hi + x_lo) % 2,
        }
        self.flip = {
            "ya": {"y": y + 1 - 2 * (y % 2)},
            "yb": {"y": 3 - y},
            "za": {"z": z + 1 - 2 * (z % 2)},
            "zb": {"z": 3 - z},
            "xa": {"x_lo": 1 - x_lo},
            "xb": {"x_hi": 1 - x_hi, "x_lo": 1 - x_lo},
            "core": {"core": 1 - core},
        }

    def across(self, *names):
        at = dict(self.here)
        for name in names:
            at.update(self.flip[name])
        return (at["x_hi"] * 2 + at["core"], (at["x_lo"] * 4 + at["z"]) * 4 + at["y"])


def chains_of(plan):
    chains, first = [], 0
    for units, turns in plan:
        names = [LINKS[turn] for turn in turns]
        groups = tuple(tuple(names[sum(GROUPS[:s]) : sum(GROUPS[: s + 1])]) for s in range(STEPS))
        chains.append((first, units * 512, groups))
        first += units * 512
    return chains


def block_of(rows):
    for parts in range(1, rows + 1):
        if rows % parts == 0 and rows // parts <= 256 and (rows // parts) % 16 == 0:
            return rows // parts
    return rows


class Reduction:
    def __init__(self, plan, place, partner, g, inbox, pairbox, full, out, sems):
        self.place, self.partner = place, partner
        self.g, self.inbox, self.pairbox, self.full, self.out = g, inbox, pairbox, full, out
        self.rs_send, self.rs_recv, self.pair_send, self.pair_recv, self.ag_send, self.ag_recv, self.out_sem = sems
        self.chains = chains_of(plan)
        assert sum(rows for first, rows, groups in self.chains) == g.shape[0]
        self.at = []
        self.steps = []
        for first, rows, groups in self.chains:
            at, size, sem, steps = [first], rows, 0, []
            for names in groups:
                part = size >> len(names)
                peers = []
                for mask in range(1, 2 ** len(names)):
                    flipped = [name for n, name in enumerate(names) if mask >> n & 1]
                    offset = at[-1]
                    for n, name in enumerate(names):
                        bit = place.bit[name]
                        offset = offset + (1 - bit if name in flipped else bit) * (size >> (n + 1))
                    slot = first + rows - size + (mask - 1) * part
                    peers.append((place.across(*flipped), offset, slot, sem))
                    sem += 1
                mine = at[-1]
                for n, name in enumerate(names):
                    mine = mine + place.bit[name] * (size >> (n + 1))
                steps.append((part, peers))
                at.append(mine)
                size = part
            self.at.append(at)
            self.steps.append(steps)

    def rs_copies(self, j, s):
        part, peers = self.steps[j][s]
        return [
            pltpu.make_async_remote_copy(
                src_ref=self.g.at[pl.ds(pl.multiple_of(offset, 16), part)],
                dst_ref=self.inbox.at[pl.ds(slot, part)],
                send_sem=self.rs_send.at[j, sem],
                recv_sem=self.rs_recv.at[j, sem],
                device_id=peer,
                device_id_type=MESH,
            )
            for peer, offset, slot, sem in peers
        ]

    def rs_add(self, j, s):
        part, peers = self.steps[j][s]
        keep = self.at[j][s + 1]
        block = block_of(part)

        def add(i, carry):
            here = pl.ds(pl.multiple_of(keep + i * block, 16), block)
            total = self.g[here, :]
            if len(peers) > 1:
                total = total.astype(jnp.float32)
            for peer, offset, slot, sem in peers:
                there = pl.ds(pl.multiple_of(slot + i * block, 16), block)
                total = total + self.inbox[there, :].astype(total.dtype)
            self.g[here, :] = total.astype(jnp.bfloat16)
            return carry

        lax.fori_loop(0, part // block, add, 0)

    def shard(self, j):
        first, rows, groups = self.chains[j]
        count = rows >> len(LINKS)
        return pl.ds(pl.multiple_of(self.at[j][STEPS], 16), count), pl.ds(first >> len(LINKS), count)

    def pair_copy(self, j, n):
        here, there = self.shard(j)
        return pltpu.make_async_remote_copy(
            src_ref=self.g.at[here],
            dst_ref=self.pairbox.at[n, there],
            send_sem=self.pair_send.at[j, n],
            recv_sem=self.pair_recv.at[j, n],
            device_id=self.place.across(PAIRS[n]),
            device_id_type=MESH,
        )

    def pair_mean(self, j):
        here, there = self.shard(j)
        other = jnp.where(
            self.partner[0:1, :] > 0.0,
            self.pairbox[1, there, :].astype(jnp.float32),
            self.pairbox[0, there, :].astype(jnp.float32),
        )
        self.full[here, :] = ((self.g[here, :].astype(jnp.float32) + other) * 0.5).astype(jnp.bfloat16)

    def ag_copies(self, j, s):
        part, peers = self.steps[j][s]
        mine = self.full.at[pl.ds(pl.multiple_of(self.at[j][s + 1], 16), part)]
        return [
            pltpu.make_async_remote_copy(
                src_ref=mine,
                dst_ref=mine,
                send_sem=self.ag_send.at[j, sem],
                recv_sem=self.ag_recv.at[j, sem],
                device_id=peer,
                device_id_type=MESH,
            )
            for peer, offset, slot, sem in peers
        ]

    def out_copy(self, j):
        part = pl.ds(self.chains[j][0], self.chains[j][1])
        return pltpu.make_async_copy(self.full.at[part], self.out.at[part], self.out_sem.at[j])

    def start(self, begin, end):
        for j, (first, rows, groups) in enumerate(self.chains):
            if begin < first + rows <= end:
                for copy in self.rs_copies(j, 0):
                    copy.start()

    def advance(self, j, stage):
        following = []
        if stage < STEPS:
            for copy in self.rs_copies(j, stage):
                copy.wait()
            self.rs_add(j, stage)
            if stage + 1 < STEPS:
                following = self.rs_copies(j, stage + 1)
            else:
                following = [self.pair_copy(j, n) for n in range(len(PAIRS))]
        elif stage == STEPS:
            for n in range(len(PAIRS)):
                self.pair_copy(j, n).wait()
            self.pair_mean(j)
            following = self.ag_copies(j, STEPS - 1)
        else:
            s = 2 * STEPS - stage
            for copy in self.ag_copies(j, s):
                copy.wait()
            following = self.ag_copies(j, s - 1) if s > 0 else [self.out_copy(j)]
        for copy in following:
            copy.start()

    def finish(self):
        for j in range(len(self.chains)):
            self.out_copy(j).wait()


class Exchange:
    def __init__(self, count, send, got, send_sem, recv_sem, own_sem):
        self.count, self.send, self.got = count, send, got
        self.send_sem, self.recv_sem, self.own_sem = send_sem, recv_sem, own_sem
        self.gossip, self.me = lax.axis_index("gossip"), lax.axis_index("field")
        self.rows = send.shape[0] // count

    def block(self, i):
        return pl.ds(pl.multiple_of(i * self.rows, 8), self.rows)

    def own(self):
        here = self.block(self.me)
        return pltpu.make_async_copy(self.send.at[here], self.got.at[here], self.own_sem)

    def copy(self, i):
        to = lax.rem(self.me + i, self.count)
        return pltpu.make_async_remote_copy(
            src_ref=self.send.at[self.block(to)],
            dst_ref=self.got.at[self.block(self.me)],
            send_sem=self.send_sem.at[i],
            recv_sem=self.recv_sem.at[i],
            device_id=(self.gossip, to),
            device_id_type=MESH,
        )

    def start(self):
        def one(i, carry):
            self.copy(i).start()
            return carry

        lax.fori_loop(1, self.count, one, 0)
        self.own().start()

    def wait(self):
        def one(i, carry):
            self.copy(i).wait()
            return carry

        lax.fori_loop(1, self.count, one, 0)
        self.own().wait()


def greet(place, count):
    barrier = pltpu.get_barrier_semaphore()
    gossip, me = lax.axis_index("gossip"), lax.axis_index("field")

    def one(i, carry):
        peer = (gossip, lax.rem(me + i, count))
        pl.semaphore_signal(barrier, inc=1, device_id=peer, device_id_type=MESH)
        return carry

    lax.fori_loop(1, count, one, 0)
    for name in PAIRS:
        pl.semaphore_signal(barrier, inc=1, device_id=place.across(name), device_id_type=MESH)


def all_greeted(count):
    pl.semaphore_wait(pltpu.get_barrier_semaphore(), count - 1 + len(PAIRS))


SIZE = 64
PAIR = 2 * SIZE


def dot(a, b, contract=((1,), (0,))):
    return lax.dot_general(a, b, (contract, ((), ())), preferred_element_type=jnp.float32)


NT = ((1,), (1,))
TN = ((0,), (0,))


def first_lanes(rows):
    return lax.broadcasted_iota(jnp.int32, (rows, PAIR), 1) < SIZE


def stacked(pair):
    low = first_lanes(pair.shape[0])
    nothing = jnp.zeros_like(pair)
    return jnp.concatenate([jnp.where(low, pair, nothing), jnp.where(low, nothing, pair)], axis=0)


def unstacked(both):
    rows = both.shape[0] // 2
    return jnp.where(first_lanes(rows), both[:rows], both[rows:])


def norm_factor(wide):
    return lax.rsqrt(jnp.mean(wide * wide, axis=-1, keepdims=True) + epsilon)


def weights_of(q, k, causal):
    length = k.shape[0]
    powers = jnp.exp(dot(stacked(q), k, NT) * (1.0 / math.sqrt(SIZE)))
    if causal:
        query = lax.broadcasted_iota(jnp.int32, powers.shape, 0) % length
        key = lax.broadcasted_iota(jnp.int32, powers.shape, 1)
        powers = jnp.where(query >= key, powers, 0.0)
    return powers / jnp.sum(powers, axis=-1, keepdims=True)


def attend_forward(packed, mixed, weights, begin, end, causal):
    length = weights.shape[3]
    width = mixed.shape[1]

    def one(n, carry):
        rows = pl.ds(pl.multiple_of(n * length, 16), length)
        for p in range(width // PAIR):
            lanes = p * PAIR
            q = packed[rows, lanes : lanes + PAIR]
            k = packed[rows, width + lanes : width + lanes + PAIR]
            v = packed[rows, 2 * width + lanes : 2 * width + lanes + PAIR]
            w = weights_of(q, k, causal).astype(jnp.bfloat16)
            weights[n, p] = w
            mixed[rows, lanes : lanes + PAIR] = unstacked(dot(w, v)).astype(jnp.bfloat16)
        return carry

    lax.fori_loop(begin, end, one, 0)


def attend_backward(packed, weights, d_mixed, d_packed, begin, end):
    length = weights.shape[3]
    width = d_mixed.shape[1]

    def one(n, carry):
        rows = pl.ds(pl.multiple_of(n * length, 16), length)
        for p in range(width // PAIR):
            lanes = p * PAIR
            q = packed[rows, lanes : lanes + PAIR]
            k = packed[rows, width + lanes : width + lanes + PAIR]
            v = packed[rows, 2 * width + lanes : 2 * width + lanes + PAIR]
            up = stacked(d_mixed[rows, lanes : lanes + PAIR])
            w = weights[n, p]
            wide = w.astype(jnp.float32)
            d_w = dot(up, v, NT).astype(jnp.bfloat16).astype(jnp.float32)
            d_scores = wide * (d_w - jnp.sum(d_w * wide, axis=-1, keepdims=True))
            d_scores = (d_scores * (1.0 / math.sqrt(SIZE))).astype(jnp.bfloat16)
            d_q = unstacked(dot(d_scores, k))
            d_k = dot(d_scores, stacked(q), TN)
            d_v = dot(w, up, TN)
            d_packed[rows, lanes : lanes + PAIR] = d_q.astype(jnp.bfloat16)
            d_packed[rows, width + lanes : width + lanes + PAIR] = d_k.astype(jnp.bfloat16)
            d_packed[rows, 2 * width + lanes : 2 * width + lanes + PAIR] = d_v.astype(jnp.bfloat16)
        return carry

    lax.fori_loop(begin, end, one, 0)


def selected(targets, rows, values):
    onehot = jnp.where(targets == lax.broadcasted_iota(jnp.int32, (rows, values.shape[0]), 0), 1.0, 0.0)
    return dot(onehot.astype(jnp.bfloat16), values)


def packed_rows(wire, at, values, block):
    rows, width = wire.shape[0], values.shape[1]
    tokens = values.shape[0]
    half = width // 2
    wire[:, :width] = selected(at[0:1, :tokens], rows, values).astype(jnp.bfloat16)
    low = selected(at[1:2, :tokens], rows, values[:, :half])
    high = selected(at[2:3, :tokens], rows, values[:, half:])
    wire[:, width:] = (low + high).astype(jnp.bfloat16)


def unpacked_rows(wire, at, tokens, width):
    rows = wire.shape[0]
    main = selected(at[0:1, :rows], tokens, wire[:, :width])
    low = selected(at[1:2, :rows], tokens, wire[:, width:])
    high = selected(at[2:3, :rows], tokens, wire[:, width:])
    return (main + jnp.concatenate([low, high], axis=1)).astype(jnp.bfloat16)


def routes(slots, count, feeders):
    device, slot, feeder = np.meshgrid(np.arange(count), np.arange(slots), np.arange(feeders), indexing="ij")
    place = slot * feeders + feeder
    tokens, rows = slots * count * feeders, count * 8
    found = []
    for order in (feeder * count * slots + device * slots + slot, slot * count * feeders + device * feeders + feeder):
        to, back = np.full((3, tokens), -1), np.full((3, tokens), -1)
        for kind, mine, row in (
            (0, place < 8, device * 8 + place),
            (1, place >= 8, device * 8 + place - 8),
            (2, place >= 8, device * 8 + place - 8 + (slots * feeders - 8)),
        ):
            to[kind, order[mine]] = row[mine]
            back[kind, row[mine]] = order[mine]
        found.append((to, back))
    assert 8 + 2 * (slots * feeders - 8) == 16
    (time_to, time_back), (feed_to, feed_back) = found
    table = np.full((32, tokens), -1)
    for n, rows in enumerate((time_to, feed_back, feed_to, time_back)):
        table[8 * n : 8 * n + 3] = rows
    return table.astype(np.int32)


def gradient_part(g, to, total):
    width = total.shape[0]
    slabs = width // LANES
    for slab in range(slabs):
        first = (to * slabs + slab) * width
        g[first : first + width, :] = total[:, slab * LANES : (slab + 1) * LANES].astype(jnp.bfloat16)


def step_kernel(
    batch, count,
    x_ref, row_ref, table_ref, time_qkv, time_out, feed_qkv_ref, feed_out_ref, route_ref, up_ref, partner_ref,
    load_ref, time_mean_ref, feed_mean_ref,
    feed_qkv, feed_out, adjoint,
    first, t_normed, t_packed, t_weights, t_mixed, f_normed, f_packed, f_weights, f_mixed,
    hidden, d_mixed, d_packed, sent, got, back, returned,
    t_g, t_inbox, t_pair, t_full, f_g, f_inbox, f_pair, f_full,
    wire_send, wire_recv, own_sem, fetch_sem, *sems,
):
    sequences, length, width = x_ref.shape
    feeders = sequences // batch
    groups = f_weights.shape[0] // batch
    tokens = feeders * length
    place = Place()
    greet(place, count)
    fetches = [
        pltpu.make_async_copy(source, target, fetch_sem.at[n])
        for n, (source, target) in enumerate(((feed_qkv_ref, feed_qkv), (feed_out_ref, feed_out), (up_ref, adjoint)))
    ]
    for fetch in fetches:
        fetch.start()
    t_sum = Reduction(TIME_PLAN, place, partner_ref, t_g, t_inbox, t_pair, t_full, time_mean_ref, sems[:7])
    f_sum = Reduction(FEED_PLAN, place, partner_ref, f_g, f_inbox, f_pair, f_full, feed_mean_ref, sems[7:])
    there, home = [], []
    for b in range(batch):
        pairs = ((there, sent, got, b), (home, back, returned, batch + b))
        for exchanges, source, target, n in pairs:
            exchanges.append(
                Exchange(count, source.at[b], target.at[b], wire_send.at[n], wire_recv.at[n], own_sem.at[n])
            )
    part_rows = 4 * width
    table_rows = table_ref.shape[0]
    onehot = (row_ref[...] == lax.broadcasted_iota(jnp.int32, (row_ref.shape[0], table_rows), 1)).astype(jnp.bfloat16)
    added = dot(onehot, table_ref[...])

    def time_forward(b):
        here = slice(b * tokens, (b + 1) * tokens)
        for n in range(feeders):
            rows = slice(b * tokens + n * length, b * tokens + (n + 1) * length)
            start = x_ref[b * feeders + n].astype(jnp.float32) + added[n : n + 1]
            first[rows, :] = start
            t_normed[rows, :] = (start * norm_factor(start)).astype(jnp.bfloat16)
        t_packed[here, :] = dot(t_normed[here, :], time_qkv[...]).astype(jnp.bfloat16)
        attend_forward(t_packed, t_mixed, t_weights, b * feeders, (b + 1) * feeders, True)
        result = (first[here, :] + dot(t_mixed[here, :], time_out[...])).astype(jnp.bfloat16)
        packed_rows(sent.at[b], route_ref[0:8, :], result, count)

    def feed_layer(b):
        here = slice(b * tokens, (b + 1) * tokens)
        hidden[here, :] = unpacked_rows(got[b], route_ref[8:16, :], tokens, width)
        wide = hidden[here, :].astype(jnp.float32)
        f_normed[here, :] = (wide * norm_factor(wide)).astype(jnp.bfloat16)
        f_packed[here, :] = dot(f_normed[here, :], feed_qkv[...]).astype(jnp.bfloat16)
        attend_forward(f_packed, f_mixed, f_weights, b * groups, (b + 1) * groups, False)
        result = hidden[here, :].astype(jnp.float32) + dot(f_mixed[here, :], feed_out[...])
        load_ref[b * groups : (b + 1) * groups] = result.astype(jnp.bfloat16).reshape(groups, -1, width)
        attend_backward(f_packed, f_weights, d_mixed, d_packed, b * groups, (b + 1) * groups)
        g = dot(d_packed[here, :], feed_qkv[...], NT).astype(jnp.bfloat16).astype(jnp.float32)
        wide = hidden[here, :].astype(jnp.float32)
        factor = norm_factor(wide)
        along = jnp.sum(g * wide, axis=-1, keepdims=True) * (factor * factor * factor) * (1.0 / width)
        d_hidden = (g * factor - wide * along).astype(jnp.bfloat16)
        total = (d_hidden.astype(jnp.float32) + adjoint[here, :].astype(jnp.float32)).astype(jnp.bfloat16)
        packed_rows(back.at[b], route_ref[16:24, :], total, count)

    def time_upstream(b):
        here = slice(b * tokens, (b + 1) * tokens)
        hidden[here, :] = unpacked_rows(returned[b], route_ref[24:32, :], tokens, width)

    def time_backward(b):
        here = slice(b * tokens, (b + 1) * tokens)
        d_mixed[here, :] = dot(hidden[here, :], time_out[...], NT).astype(jnp.bfloat16)
        attend_backward(t_packed, t_weights, d_mixed, d_packed, b * feeders, (b + 1) * feeders)

    def advance(codes):
        for code in codes:
            (f_sum if code >= 100 else t_sum).advance(code // 10 % 10, code % 10)

    for b in range(batch):
        time_forward(b)
        if b == 0:
            all_greeted(count)
        there[b].start()
    for fetch in fetches:
        fetch.wait()
    d_mixed[...] = dot(adjoint[...], feed_out[...], NT).astype(jnp.bfloat16)
    for b in range(batch):
        there[b].wait()
        feed_layer(b)
        home[b].start()

    for part in range(4):
        if part < 3:
            f_total = dot(f_normed[...], d_packed[:, part * width : (part + 1) * width], TN)
        else:
            f_total = dot(f_mixed[...], adjoint[...], TN)
        gradient_part(f_g, part, f_total)
        f_sum.start(part * part_rows, (part + 1) * part_rows)
    for b in range(batch):
        home[b].wait()
        time_upstream(b)
        if b == batch - 1:
            gradient_part(f_g, 4, dot(t_mixed[...], hidden[...], TN))
            f_sum.start(4 * part_rows, 5 * part_rows)
        time_backward(b)
        advance(ORDER[b])
    for part in range(3):
        gradient_part(t_g, part, dot(t_normed[...], d_packed[:, part * width : (part + 1) * width], TN))
        t_sum.start(part * part_rows, (part + 1) * part_rows)
        if part < 2:
            advance(ORDER[batch + part])
    advance(ORDER[4])
    f_sum.finish()
    t_sum.finish()


def finish_kernel(time_ref, feed_ref, out_ref, held, wide, in_sem, out_sem):
    slabs, depth, lanes = time_ref.shape[1:]
    rows = 4 * depth

    def get(n):
        layer, slab = n // slabs, n % slabs
        if layer:
            pieces = ((feed_ref.at[pl.ds(0, 4), slab], held.at[n]),)
        else:
            pieces = (
                (time_ref.at[:, slab], held.at[n, pl.ds(0, 3)]),
                (feed_ref.at[4, slab], held.at[n, 3]),
            )
        return [pltpu.make_async_copy(*piece, in_sem.at[n, i]) for i, piece in enumerate(pieces)]

    def put(n):
        target = out_ref.at[pl.ds(n // slabs * rows, rows), pl.ds(n % slabs * lanes, lanes)]
        return pltpu.make_async_copy(wide.at[n], target, out_sem.at[n])

    for n in range(2 * slabs):
        for copy in get(n):
            copy.start()
    for n in range(2 * slabs):
        for copy in get(n):
            copy.wait()
        for part in range(3):
            wide[n, pl.ds(part, depth, stride=3), :] = held[n, part].astype(jnp.float32)
        wide[n, 3 * depth :, :] = held[n, 3].astype(jnp.float32)
        put(n).start()
    for n in range(2 * slabs):
        put(n).wait()


def finished(time_mean, feed_mean):
    slabs, depth, lanes = time_mean.shape[1:]
    rows = 4 * depth
    return pl.pallas_call(
        finish_kernel,
        out_shape=jax.ShapeDtypeStruct((2 * rows, slabs * lanes), jnp.float32),
        in_specs=[ANY, ANY],
        out_specs=ANY,
        scratch_shapes=[
            pltpu.VMEM((2 * slabs, 4, depth, lanes), jnp.bfloat16),
            pltpu.VMEM((2 * slabs, rows, lanes), jnp.float32),
            pltpu.SemaphoreType.DMA((2 * slabs, 2)),
            pltpu.SemaphoreType.DMA((2 * slabs,)),
        ],
        compiler_params=pltpu.CompilerParams(vmem_limit_bytes=60 * 1024 * 1024),
    )(time_mean, feed_mean)


VMEM = pl.BlockSpec(memory_space=pltpu.VMEM)
ANY = pl.BlockSpec(memory_space=pl.ANY)


def on_device(
    measured_features,
    feeder_of_row,
    feeder_table,
    time_qkv,
    time_out,
    feed_qkv,
    feed_out,
    adjoint_of_prediction,
    round_index,
):
    batch, feed_local, slot_count, width = measured_features.shape
    feeder_count = adjoint_of_prediction.shape[1]
    slot_local = adjoint_of_prediction.shape[2]
    count = feeder_count // feed_local
    rows = batch * feed_local * slot_count
    pairs = width // PAIR
    bf16 = jnp.bfloat16
    sequences, groups = batch * feed_local, batch * slot_local

    route = jnp.asarray(routes(slot_local, count, feed_local))
    row_column = jnp.pad(feeder_of_row, (0, 8 - feed_local)).reshape(8, 1)
    partner = jnp.broadcast_to(round_index.astype(jnp.float32), (8, LANES))
    upstream = jnp.transpose(adjoint_of_prediction, (0, 2, 1, 3)).reshape(rows, width)
    part_rows = width * width // LANES
    time_rows, feed_rows = 3 * part_rows, 5 * part_rows

    def held(*shape):
        return pltpu.VMEM(shape, bf16)

    def reduction(n):
        return [held(n, LANES), held(n, LANES), held(len(PAIRS), n >> len(LINKS), LANES), held(n, LANES)]

    def semaphores(chains):
        steps = [COPIES, COPIES, len(PAIRS), len(PAIRS), COPIES, COPIES]
        return [pltpu.SemaphoreType.DMA((chains, s)) for s in steps] + [pltpu.SemaphoreType.DMA((chains,))]

    wire = held(batch, count * 8, width + width // 2)
    load, time_mean, feed_mean = pl.pallas_call(
        partial(step_kernel, batch, count),
        out_shape=(
            jax.ShapeDtypeStruct((groups, feeder_count, width), bf16),
            jax.ShapeDtypeStruct((time_rows, LANES), bf16),
            jax.ShapeDtypeStruct((feed_rows, LANES), bf16),
        ),
        in_specs=[VMEM, VMEM, VMEM, VMEM, VMEM, ANY, ANY, VMEM, ANY, VMEM],
        out_specs=(VMEM, ANY, ANY),
        scratch_shapes=[
            held(width, 3 * width),
            held(width, width),
            held(rows, width),
            pltpu.VMEM((rows, width), jnp.float32),
            held(rows, width),
            held(rows, 3 * width),
            held(sequences, pairs, 2 * slot_count, slot_count),
            held(rows, width),
            held(rows, width),
            held(rows, 3 * width),
            held(groups, pairs, 2 * feeder_count, feeder_count),
            held(rows, width),
            held(rows, width),
            held(rows, width),
            held(rows, 3 * width),
            wire,
            wire,
            wire,
            wire,
        ]
        + reduction(time_rows)
        + reduction(feed_rows)
        + [pltpu.SemaphoreType.DMA((2 * batch, count))] * 2
        + [pltpu.SemaphoreType.DMA((2 * batch,)), pltpu.SemaphoreType.DMA((3,))]
        + semaphores(len(TIME_PLAN))
        + semaphores(len(FEED_PLAN)),
        compiler_params=pltpu.CompilerParams(collective_id=1, has_side_effects=True, vmem_limit_bytes=60 * 1024 * 1024),
    )(
        measured_features.reshape(sequences, slot_count, width),
        row_column,
        feeder_table,
        time_qkv,
        time_out,
        feed_qkv,
        feed_out,
        route,
        upstream,
        partner,
    )
    predicted_load = jnp.transpose(load.reshape(batch, slot_local, feeder_count, width), (0, 2, 1, 3))
    slabs = (width // LANES, width, LANES)
    gradients = finished(time_mean.reshape(3, *slabs), feed_mean.reshape(5, *slabs))
    return (predicted_load, gradients[None])


def solution(mesh):
    placed = (
        P("gossip", "field", None, None),
        P("field"),
        P(),
        P(),
        P(),
        P(),
        P(),
        P("gossip", None, "field", None),
        P(),
    )
    return jax.shard_map(
        on_device,
        mesh=mesh,
        in_specs=placed,
        out_specs=(P("gossip", None, "field", None), P("gossip", None, None)),
        check_vma=False,
    )
```

```python
from functools import partial
import math

import jax
import jax.numpy as jnp
import numpy as np
from jax import lax
from jax.experimental import pallas as pl
from jax.experimental.pallas import tpu as pltpu
from jax.sharding import PartitionSpec as P

epsilon = 1e-05


MESH = pl.DeviceIdType.MESH
LANES = 128
LINKS = ("ya", "za", "xa", "yb", "zb")
PAIRS = ("core", "xb")
GROUPS = (1, 1, 1, 2)
STEPS = len(GROUPS)
TURNS = 2 * STEPS + 1
COPIES = sum(2**size - 1 for size in GROUPS)

TIME_PLAN = (
    (1, (3, 2, 4, 1, 0)),
    (2, (1, 4, 0, 3, 2)),
    (1, (4, 0, 2, 3, 1)),
    (2, (4, 0, 2, 3, 1)),
    (2, (3, 1, 0, 4, 2)),
    (2, (0, 3, 4, 2, 1)),
    (1, (3, 1, 4, 0, 2)),
    (1, (0, 2, 4, 3, 1)),
)
FEED_PLAN = (
    (3, (2, 1, 3, 4, 0)),
    (2, (2, 3, 1, 0, 4)),
    (1, (0, 4, 1, 3, 2)),
    (2, (4, 0, 3, 2, 1)),
    (1, (1, 0, 3, 2, 4)),
    (1, (3, 2, 4, 0, 1)),
    (3, (0, 2, 4, 1, 3)),
    (3, (1, 2, 3, 0, 4)),
    (2, (3, 2, 1, 0, 4)),
    (2, (4, 1, 0, 3, 2)),
)

ORDER = (
    (),
    (120, 140, 150),
    (130,),
    (100, 180),
    (
        160, 170, 190, 121, 141, 110, 151, 0, 20, 131, 10, 181, 30, 40, 152, 101,
        161, 50, 60, 142, 191, 70, 122, 11, 171, 21, 111, 182, 1, 132, 31, 41,
        162, 102, 61, 153, 192, 143, 71, 51, 12, 22, 112, 2, 123, 172, 183, 32,
        133, 42, 154, 144, 163, 62, 72, 103, 193, 52, 124, 13, 23, 184, 134, 113,
        3, 173, 33, 164, 43, 155, 104, 145, 194, 63, 73, 14, 24, 53, 125, 114,
        4, 185, 174, 135, 34, 44, 156, 146, 64, 74, 165, 54, 105, 195, 126, 15,
        25, 115, 186, 5, 136, 175, 157, 45, 147, 35, 75, 166, 65, 196, 55, 106,
        26, 127, 16, 116, 6, 187, 176, 137, 76, 36, 46, 66, 148, 158, 56, 27,
        197, 167, 17, 117, 7, 128, 107, 37, 177, 138, 47, 188, 77, 67, 28, 57,
        8, 118, 18, 168, 198, 78, 48, 38, 68, 108, 178, 58,
    ),
)


class Place:
    def __init__(self):
        gossip, field = lax.axis_index("gossip"), lax.axis_index("field")
        x_hi, core = gossip // 2, gossip % 2
        x_lo, z, y = field // 16, (field // 4) % 4, field % 4
        self.here = {"x_hi": x_hi, "core": core, "x_lo": x_lo, "z": z, "y": y}
        self.bit = {
            "ya": ((y + 1) // 2) % 2,
            "yb": y // 2,
            "za": ((z + 1) // 2) % 2,
            "zb": z // 2,
            "xa": (x_hi + x_lo) % 2,
        }
        self.flip = {
            "ya": {"y": y + 1 - 2 * (y % 2)},
            "yb": {"y": 3 - y},
            "za": {"z": z + 1 - 2 * (z % 2)},
            "zb": {"z": 3 - z},
            "xa": {"x_lo": 1 - x_lo},
            "xb": {"x_hi": 1 - x_hi, "x_lo": 1 - x_lo},
            "core": {"core": 1 - core},
        }

    def across(self, *names):
        at = dict(self.here)
        for name in names:
            at.update(self.flip[name])
        return (at["x_hi"] * 2 + at["core"], (at["x_lo"] * 4 + at["z"]) * 4 + at["y"])


def chains_of(plan):
    chains, first = [], 0
    for units, turns in plan:
        names = [LINKS[turn] for turn in turns]
        groups = tuple(tuple(names[sum(GROUPS[:s]) : sum(GROUPS[: s + 1])]) for s in range(STEPS))
        chains.append((first, units * 512, groups))
        first += units * 512
    return chains


def block_of(rows):
    for parts in range(1, rows + 1):
        if rows % parts == 0 and rows // parts <= 256 and (rows // parts) % 16 == 0:
            return rows // parts
    return rows


class Reduction:
    def __init__(self, plan, place, partner, g, inbox, pairbox, full, out, sems):
        self.place, self.partner = place, partner
        self.g, self.inbox, self.pairbox, self.full, self.out = g, inbox, pairbox, full, out
        self.rs_send, self.rs_recv, self.pair_send, self.pair_recv, self.ag_send, self.ag_recv, self.out_sem = sems
        self.chains = chains_of(plan)
        assert sum(rows for first, rows, groups in self.chains) == g.shape[0]
        self.at = []
        self.steps = []
        for first, rows, groups in self.chains:
            at, size, sem, steps = [first], rows, 0, []
            for names in groups:
                part = size >> len(names)
                peers = []
                for mask in range(1, 2 ** len(names)):
                    flipped = [name for n, name in enumerate(names) if mask >> n & 1]
                    offset = at[-1]
                    for n, name in enumerate(names):
                        bit = place.bit[name]
                        offset = offset + (1 - bit if name in flipped else bit) * (size >> (n + 1))
                    slot = first + rows - size + (mask - 1) * part
                    peers.append((place.across(*flipped), offset, slot, sem))
                    sem += 1
                mine = at[-1]
                for n, name in enumerate(names):
                    mine = mine + place.bit[name] * (size >> (n + 1))
                steps.append((part, peers))
                at.append(mine)
                size = part
            self.at.append(at)
            self.steps.append(steps)

    def rs_copies(self, j, s):
        part, peers = self.steps[j][s]
        return [
            pltpu.make_async_remote_copy(
                src_ref=self.g.at[pl.ds(pl.multiple_of(offset, 16), part)],
                dst_ref=self.inbox.at[pl.ds(slot, part)],
                send_sem=self.rs_send.at[j, sem],
                recv_sem=self.rs_recv.at[j, sem],
                device_id=peer,
                device_id_type=MESH,
            )
            for peer, offset, slot, sem in peers
        ]

    def rs_add(self, j, s):
        part, peers = self.steps[j][s]
        keep = self.at[j][s + 1]
        block = block_of(part)

        def add(i, carry):
            here = pl.ds(pl.multiple_of(keep + i * block, 16), block)
            total = self.g[here, :]
            if len(peers) > 1:
                total = total.astype(jnp.float32)
            for peer, offset, slot, sem in peers:
                there = pl.ds(pl.multiple_of(slot + i * block, 16), block)
                total = total + self.inbox[there, :].astype(total.dtype)
            self.g[here, :] = total.astype(jnp.bfloat16)
            return carry

        lax.fori_loop(0, part // block, add, 0)

    def shard(self, j):
        first, rows, groups = self.chains[j]
        count = rows >> len(LINKS)
        return pl.ds(pl.multiple_of(self.at[j][STEPS], 16), count), pl.ds(first >> len(LINKS), count)

    def pair_copy(self, j, n):
        here, there = self.shard(j)
        return pltpu.make_async_remote_copy(
            src_ref=self.g.at[here],
            dst_ref=self.pairbox.at[n, there],
            send_sem=self.pair_send.at[j, n],
            recv_sem=self.pair_recv.at[j, n],
            device_id=self.place.across(PAIRS[n]),
            device_id_type=MESH,
        )

    def pair_mean(self, j):
        here, there = self.shard(j)
        other = jnp.where(
            self.partner[0:1, :] > 0.0,
            self.pairbox[1, there, :].astype(jnp.float32),
            self.pairbox[0, there, :].astype(jnp.float32),
        )
        self.full[here, :] = ((self.g[here, :].astype(jnp.float32) + other) * 0.5).astype(jnp.bfloat16)

    def ag_copies(self, j, s):
        part, peers = self.steps[j][s]
        mine = self.full.at[pl.ds(pl.multiple_of(self.at[j][s + 1], 16), part)]
        return [
            pltpu.make_async_remote_copy(
                src_ref=mine,
                dst_ref=mine,
                send_sem=self.ag_send.at[j, sem],
                recv_sem=self.ag_recv.at[j, sem],
                device_id=peer,
                device_id_type=MESH,
            )
            for peer, offset, slot, sem in peers
        ]

    def out_copy(self, j):
        part = pl.ds(self.chains[j][0], self.chains[j][1])
        return pltpu.make_async_copy(self.full.at[part], self.out.at[part], self.out_sem.at[j])

    def start(self, begin, end):
        for j, (first, rows, groups) in enumerate(self.chains):
            if begin < first + rows <= end:
                for copy in self.rs_copies(j, 0):
                    copy.start()

    def advance(self, j, stage):
        following = []
        if stage < STEPS:
            for copy in self.rs_copies(j, stage):
                copy.wait_recv()
            self.rs_add(j, stage)
            if stage + 1 < STEPS:
                following = self.rs_copies(j, stage + 1)
            else:
                following = [self.pair_copy(j, n) for n in range(len(PAIRS))]
        elif stage == STEPS:
            for n in range(len(PAIRS)):
                self.pair_copy(j, n).wait_recv()
            self.pair_mean(j)
            following = self.ag_copies(j, STEPS - 1)
        else:
            s = 2 * STEPS - stage
            for copy in self.ag_copies(j, s):
                copy.wait_recv()
            following = self.ag_copies(j, s - 1) if s > 0 else [self.out_copy(j)]
        for copy in following:
            copy.start()

    def finish(self):
        for j in range(len(self.chains)):
            sent = [self.pair_copy(j, n) for n in range(len(PAIRS))]
            for s in range(STEPS):
                sent += self.rs_copies(j, s) + self.ag_copies(j, s)
            for copy in sent:
                copy.wait_send()
            self.out_copy(j).wait()


class Exchange:
    def __init__(self, count, send, got, send_sem, recv_sem, own_sem):
        self.count, self.send, self.got = count, send, got
        self.send_sem, self.recv_sem, self.own_sem = send_sem, recv_sem, own_sem
        self.gossip, self.me = lax.axis_index("gossip"), lax.axis_index("field")
        self.rows = send.shape[0] // count

    def block(self, i):
        return pl.ds(pl.multiple_of(i * self.rows, 8), self.rows)

    def own(self):
        here = self.block(self.me)
        return pltpu.make_async_copy(self.send.at[here], self.got.at[here], self.own_sem)

    def copy(self, i):
        to = lax.rem(self.me + i, self.count)
        return pltpu.make_async_remote_copy(
            src_ref=self.send.at[self.block(to)],
            dst_ref=self.got.at[self.block(self.me)],
            send_sem=self.send_sem.at[i],
            recv_sem=self.recv_sem.at[i],
            device_id=(self.gossip, to),
            device_id_type=MESH,
        )

    def start(self):
        def one(i, carry):
            self.copy(i).start()
            return carry

        lax.fori_loop(1, self.count, one, 0)
        self.own().start()

    def wait(self):
        def one(i, carry):
            self.copy(i).wait()
            return carry

        lax.fori_loop(1, self.count, one, 0)
        self.own().wait()


def greet(place, count):
    barrier = pltpu.get_barrier_semaphore()
    gossip, me = lax.axis_index("gossip"), lax.axis_index("field")

    def one(i, carry):
        peer = (gossip, lax.rem(me + i, count))
        pl.semaphore_signal(barrier, inc=1, device_id=peer, device_id_type=MESH)
        return carry

    lax.fori_loop(1, count, one, 0)
    for name in PAIRS:
        pl.semaphore_signal(barrier, inc=1, device_id=place.across(name), device_id_type=MESH)


def all_greeted(count):
    pl.semaphore_wait(pltpu.get_barrier_semaphore(), count - 1 + len(PAIRS))


SIZE = 64
PAIR = 2 * SIZE


def dot(a, b, contract=((1,), (0,))):
    return lax.dot_general(a, b, (contract, ((), ())), preferred_element_type=jnp.float32)


NT = ((1,), (1,))
TN = ((0,), (0,))


def first_lanes(rows):
    return lax.broadcasted_iota(jnp.int32, (rows, PAIR), 1) < SIZE


def stacked(pair):
    low = first_lanes(pair.shape[0])
    nothing = jnp.zeros_like(pair)
    return jnp.concatenate([jnp.where(low, pair, nothing), jnp.where(low, nothing, pair)], axis=0)


def unstacked(both):
    rows = both.shape[0] // 2
    return jnp.where(first_lanes(rows), both[:rows], both[rows:])


def norm_factor(wide):
    return lax.rsqrt(jnp.mean(wide * wide, axis=-1, keepdims=True) + epsilon)


def weights_of(q, k, causal):
    length = k.shape[0]
    powers = jnp.exp(dot(stacked(q), k, NT) * (1.0 / math.sqrt(SIZE)))
    if causal:
        query = lax.broadcasted_iota(jnp.int32, powers.shape, 0) % length
        key = lax.broadcasted_iota(jnp.int32, powers.shape, 1)
        powers = jnp.where(query >= key, powers, 0.0)
    return powers / jnp.sum(powers, axis=-1, keepdims=True)


def attend_forward(packed, mixed, weights, begin, end, causal):
    length = weights.shape[3]
    width = mixed.shape[1]

    def one(n, carry):
        rows = pl.ds(pl.multiple_of(n * length, 16), length)
        for p in range(width // PAIR):
            lanes = p * PAIR
            q = packed[rows, lanes : lanes + PAIR]
            k = packed[rows, width + lanes : width + lanes + PAIR]
            v = packed[rows, 2 * width + lanes : 2 * width + lanes + PAIR]
            w = weights_of(q, k, causal).astype(jnp.bfloat16)
            weights[n, p] = w
            mixed[rows, lanes : lanes + PAIR] = unstacked(dot(w, v)).astype(jnp.bfloat16)
        return carry

    lax.fori_loop(begin, end, one, 0)


def attend_backward(packed, weights, d_mixed, d_packed, begin, end):
    length = weights.shape[3]
    width = d_mixed.shape[1]

    def one(n, carry):
        rows = pl.ds(pl.multiple_of(n * length, 16), length)
        for p in range(width // PAIR):
            lanes = p * PAIR
            q = packed[rows, lanes : lanes + PAIR]
            k = packed[rows, width + lanes : width + lanes + PAIR]
            v = packed[rows, 2 * width + lanes : 2 * width + lanes + PAIR]
            up = stacked(d_mixed[rows, lanes : lanes + PAIR])
            w = weights[n, p]
            wide = w.astype(jnp.float32)
            d_w = dot(up, v, NT).astype(jnp.bfloat16).astype(jnp.float32)
            d_scores = wide * (d_w - jnp.sum(d_w * wide, axis=-1, keepdims=True))
            d_scores = (d_scores * (1.0 / math.sqrt(SIZE))).astype(jnp.bfloat16)
            d_q = unstacked(dot(d_scores, k))
            d_k = dot(d_scores, stacked(q), TN)
            d_v = dot(w, up, TN)
            d_packed[rows, lanes : lanes + PAIR] = d_q.astype(jnp.bfloat16)
            d_packed[rows, width + lanes : width + lanes + PAIR] = d_k.astype(jnp.bfloat16)
            d_packed[rows, 2 * width + lanes : 2 * width + lanes + PAIR] = d_v.astype(jnp.bfloat16)
        return carry

    lax.fori_loop(begin, end, one, 0)


def selected(targets, rows, values):
    onehot = jnp.where(targets == lax.broadcasted_iota(jnp.int32, (rows, values.shape[0]), 0), 1.0, 0.0)
    return dot(onehot.astype(jnp.bfloat16), values)


def packed_rows(wire, at, values, block):
    rows, width = wire.shape[0], values.shape[1]
    tokens = values.shape[0]
    half = width // 2
    wire[:, :width] = selected(at[0:1, :tokens], rows, values).astype(jnp.bfloat16)
    low = selected(at[1:2, :tokens], rows, values[:, :half])
    high = selected(at[2:3, :tokens], rows, values[:, half:])
    wire[:, width:] = (low + high).astype(jnp.bfloat16)


def unpacked_rows(wire, at, tokens, width):
    rows = wire.shape[0]
    main = selected(at[0:1, :rows], tokens, wire[:, :width])
    low = selected(at[1:2, :rows], tokens, wire[:, width:])
    high = selected(at[2:3, :rows], tokens, wire[:, width:])
    return (main + jnp.concatenate([low, high], axis=1)).astype(jnp.bfloat16)


def routes(slots, count, feeders):
    device, slot, feeder = np.meshgrid(np.arange(count), np.arange(slots), np.arange(feeders), indexing="ij")
    place = slot * feeders + feeder
    tokens, rows = slots * count * feeders, count * 8
    found = []
    for order in (feeder * count * slots + device * slots + slot, slot * count * feeders + device * feeders + feeder):
        to, back = np.full((3, tokens), -1), np.full((3, tokens), -1)
        for kind, mine, row in (
            (0, place < 8, device * 8 + place),
            (1, place >= 8, device * 8 + place - 8),
            (2, place >= 8, device * 8 + place - 8 + (slots * feeders - 8)),
        ):
            to[kind, order[mine]] = row[mine]
            back[kind, row[mine]] = order[mine]
        found.append((to, back))
    assert 8 + 2 * (slots * feeders - 8) == 16
    (time_to, time_back), (feed_to, feed_back) = found
    table = np.full((32, tokens), -1)
    for n, rows in enumerate((time_to, feed_back, feed_to, time_back)):
        table[8 * n : 8 * n + 3] = rows
    return table.astype(np.int32)


def gradient_part(g, to, total):
    width = total.shape[0]
    slabs = width // LANES
    for slab in range(slabs):
        first = (to * slabs + slab) * width
        g[first : first + width, :] = total[:, slab * LANES : (slab + 1) * LANES].astype(jnp.bfloat16)


def step_kernel(
    batch, count,
    x_ref, row_ref, table_ref, time_qkv, time_out, feed_qkv_ref, feed_out_ref, route_ref, up_ref, partner_ref,
    load_ref, time_mean_ref, feed_mean_ref,
    feed_qkv, feed_out, adjoint,
    first, t_normed, t_packed, t_weights, t_mixed, f_normed, f_packed, f_weights, f_mixed,
    hidden, d_mixed, d_packed, sent, got, back, returned,
    t_g, t_inbox, t_pair, t_full, f_g, f_inbox, f_pair, f_full,
    wire_send, wire_recv, own_sem, fetch_sem, *sems,
):
    sequences, length, width = x_ref.shape
    feeders = sequences // batch
    groups = f_weights.shape[0] // batch
    tokens = feeders * length
    place = Place()
    greet(place, count)
    fetches = [
        pltpu.make_async_copy(source, target, fetch_sem.at[n])
        for n, (source, target) in enumerate(((feed_qkv_ref, feed_qkv), (feed_out_ref, feed_out), (up_ref, adjoint)))
    ]
    for fetch in fetches:
        fetch.start()
    t_sum = Reduction(TIME_PLAN, place, partner_ref, t_g, t_inbox, t_pair, t_full, time_mean_ref, sems[:7])
    f_sum = Reduction(FEED_PLAN, place, partner_ref, f_g, f_inbox, f_pair, f_full, feed_mean_ref, sems[7:])
    there, home = [], []
    for b in range(batch):
        pairs = ((there, sent, got, b), (home, back, returned, batch + b))
        for exchanges, source, target, n in pairs:
            exchanges.append(
                Exchange(count, source.at[b], target.at[b], wire_send.at[n], wire_recv.at[n], own_sem.at[n])
            )
    part_rows = 4 * width
    table_rows = table_ref.shape[0]
    onehot = (row_ref[...] == lax.broadcasted_iota(jnp.int32, (row_ref.shape[0], table_rows), 1)).astype(jnp.bfloat16)
    added = dot(onehot, table_ref[...])

    def time_forward(b):
        here = slice(b * tokens, (b + 1) * tokens)
        for n in range(feeders):
            rows = slice(b * tokens + n * length, b * tokens + (n + 1) * length)
            start = x_ref[b * feeders + n].astype(jnp.float32) + added[n : n + 1]
            first[rows, :] = start
            t_normed[rows, :] = (start * norm_factor(start)).astype(jnp.bfloat16)
        t_packed[here, :] = dot(t_normed[here, :], time_qkv[...]).astype(jnp.bfloat16)
        attend_forward(t_packed, t_mixed, t_weights, b * feeders, (b + 1) * feeders, True)
        result = (first[here, :] + dot(t_mixed[here, :], time_out[...])).astype(jnp.bfloat16)
        packed_rows(sent.at[b], route_ref[0:8, :], result, count)

    def feed_layer(b):
        here = slice(b * tokens, (b + 1) * tokens)
        hidden[here, :] = unpacked_rows(got[b], route_ref[8:16, :], tokens, width)
        wide = hidden[here, :].astype(jnp.float32)
        f_normed[here, :] = (wide * norm_factor(wide)).astype(jnp.bfloat16)
        f_packed[here, :] = dot(f_normed[here, :], feed_qkv[...]).astype(jnp.bfloat16)
        attend_forward(f_packed, f_mixed, f_weights, b * groups, (b + 1) * groups, False)
        result = hidden[here, :].astype(jnp.float32) + dot(f_mixed[here, :], feed_out[...])
        load_ref[b * groups : (b + 1) * groups] = result.astype(jnp.bfloat16).reshape(groups, -1, width)
        attend_backward(f_packed, f_weights, d_mixed, d_packed, b * groups, (b + 1) * groups)
        g = dot(d_packed[here, :], feed_qkv[...], NT).astype(jnp.bfloat16).astype(jnp.float32)
        wide = hidden[here, :].astype(jnp.float32)
        factor = norm_factor(wide)
        along = jnp.sum(g * wide, axis=-1, keepdims=True) * (factor * factor * factor) * (1.0 / width)
        d_hidden = (g * factor - wide * along).astype(jnp.bfloat16)
        total = (d_hidden.astype(jnp.float32) + adjoint[here, :].astype(jnp.float32)).astype(jnp.bfloat16)
        packed_rows(back.at[b], route_ref[16:24, :], total, count)

    def time_upstream(b):
        here = slice(b * tokens, (b + 1) * tokens)
        hidden[here, :] = unpacked_rows(returned[b], route_ref[24:32, :], tokens, width)

    def time_backward(b):
        here = slice(b * tokens, (b + 1) * tokens)
        d_mixed[here, :] = dot(hidden[here, :], time_out[...], NT).astype(jnp.bfloat16)
        attend_backward(t_packed, t_weights, d_mixed, d_packed, b * feeders, (b + 1) * feeders)

    def advance(codes):
        for code in codes:
            (f_sum if code >= 100 else t_sum).advance(code // 10 % 10, code % 10)

    for b in range(batch):
        time_forward(b)
        if b == 0:
            all_greeted(count)
        there[b].start()
    for fetch in fetches:
        fetch.wait()
    d_mixed[...] = dot(adjoint[...], feed_out[...], NT).astype(jnp.bfloat16)
    for b in range(batch):
        there[b].wait()
        feed_layer(b)
        home[b].start()

    for part in range(4):
        if part < 3:
            f_total = dot(f_normed[...], d_packed[:, part * width : (part + 1) * width], TN)
        else:
            f_total = dot(f_mixed[...], adjoint[...], TN)
        gradient_part(f_g, part, f_total)
        f_sum.start(part * part_rows, (part + 1) * part_rows)
    for b in range(batch):
        home[b].wait()
        time_upstream(b)
        if b == batch - 1:
            gradient_part(f_g, 4, dot(t_mixed[...], hidden[...], TN))
            f_sum.start(4 * part_rows, 5 * part_rows)
        time_backward(b)
        advance(ORDER[b])
    for part in range(3):
        gradient_part(t_g, part, dot(t_normed[...], d_packed[:, part * width : (part + 1) * width], TN))
        t_sum.start(part * part_rows, (part + 1) * part_rows)
        if part < 2:
            advance(ORDER[batch + part])
    advance(ORDER[4])
    f_sum.finish()
    t_sum.finish()


def finish_kernel(time_ref, feed_ref, out_ref, held, wide, in_sem, out_sem):
    slabs, depth, lanes = time_ref.shape[1:]
    rows = 4 * depth

    def get(n):
        layer, slab = n // slabs, n % slabs
        if layer:
            pieces = ((feed_ref.at[pl.ds(0, 4), slab], held.at[n]),)
        else:
            pieces = (
                (time_ref.at[:, slab], held.at[n, pl.ds(0, 3)]),
                (feed_ref.at[4, slab], held.at[n, 3]),
            )
        return [pltpu.make_async_copy(*piece, in_sem.at[n, i]) for i, piece in enumerate(pieces)]

    def put(n):
        target = out_ref.at[pl.ds(n // slabs * rows, rows), pl.ds(n % slabs * lanes, lanes)]
        return pltpu.make_async_copy(wide.at[n], target, out_sem.at[n])

    for n in range(2 * slabs):
        for copy in get(n):
            copy.start()
    for n in range(2 * slabs):
        for copy in get(n):
            copy.wait()
        for part in range(3):
            wide[n, pl.ds(part, depth, stride=3), :] = held[n, part].astype(jnp.float32)
        wide[n, 3 * depth :, :] = held[n, 3].astype(jnp.float32)
        put(n).start()
    for n in range(2 * slabs):
        put(n).wait()


def finished(time_mean, feed_mean):
    slabs, depth, lanes = time_mean.shape[1:]
    rows = 4 * depth
    return pl.pallas_call(
        finish_kernel,
        out_shape=jax.ShapeDtypeStruct((2 * rows, slabs * lanes), jnp.float32),
        in_specs=[ANY, ANY],
        out_specs=ANY,
        scratch_shapes=[
            pltpu.VMEM((2 * slabs, 4, depth, lanes), jnp.bfloat16),
            pltpu.VMEM((2 * slabs, rows, lanes), jnp.float32),
            pltpu.SemaphoreType.DMA((2 * slabs, 2)),
            pltpu.SemaphoreType.DMA((2 * slabs,)),
        ],
        compiler_params=pltpu.CompilerParams(vmem_limit_bytes=60 * 1024 * 1024),
    )(time_mean, feed_mean)


VMEM = pl.BlockSpec(memory_space=pltpu.VMEM)
ANY = pl.BlockSpec(memory_space=pl.ANY)


def on_device(
    measured_features,
    feeder_of_row,
    feeder_table,
    time_qkv,
    time_out,
    feed_qkv,
    feed_out,
    adjoint_of_prediction,
    round_index,
):
    batch, feed_local, slot_count, width = measured_features.shape
    feeder_count = adjoint_of_prediction.shape[1]
    slot_local = adjoint_of_prediction.shape[2]
    count = feeder_count // feed_local
    rows = batch * feed_local * slot_count
    pairs = width // PAIR
    bf16 = jnp.bfloat16
    sequences, groups = batch * feed_local, batch * slot_local

    route = jnp.asarray(routes(slot_local, count, feed_local))
    row_column = jnp.pad(feeder_of_row, (0, 8 - feed_local)).reshape(8, 1)
    partner = jnp.broadcast_to(round_index.astype(jnp.float32), (8, LANES))
    upstream = jnp.transpose(adjoint_of_prediction, (0, 2, 1, 3)).reshape(rows, width)
    part_rows = width * width // LANES
    time_rows, feed_rows = 3 * part_rows, 5 * part_rows

    def held(*shape):
        return pltpu.VMEM(shape, bf16)

    def reduction(n):
        return [held(n, LANES), held(n, LANES), held(len(PAIRS), n >> len(LINKS), LANES), held(n, LANES)]

    def semaphores(chains):
        steps = [COPIES, COPIES, len(PAIRS), len(PAIRS), COPIES, COPIES]
        return [pltpu.SemaphoreType.DMA((chains, s)) for s in steps] + [pltpu.SemaphoreType.DMA((chains,))]

    wire = held(batch, count * 8, width + width // 2)
    load, time_mean, feed_mean = pl.pallas_call(
        partial(step_kernel, batch, count),
        out_shape=(
            jax.ShapeDtypeStruct((groups, feeder_count, width), bf16),
            jax.ShapeDtypeStruct((time_rows, LANES), bf16),
            jax.ShapeDtypeStruct((feed_rows, LANES), bf16),
        ),
        in_specs=[VMEM, VMEM, VMEM, VMEM, VMEM, ANY, ANY, VMEM, ANY, VMEM],
        out_specs=(VMEM, ANY, ANY),
        scratch_shapes=[
            held(width, 3 * width),
            held(width, width),
            held(rows, width),
            pltpu.VMEM((rows, width), jnp.float32),
            held(rows, width),
            held(rows, 3 * width),
            held(sequences, pairs, 2 * slot_count, slot_count),
            held(rows, width),
            held(rows, width),
            held(rows, 3 * width),
            held(groups, pairs, 2 * feeder_count, feeder_count),
            held(rows, width),
            held(rows, width),
            held(rows, width),
            held(rows, 3 * width),
            wire,
            wire,
            wire,
            wire,
        ]
        + reduction(time_rows)
        + reduction(feed_rows)
        + [pltpu.SemaphoreType.DMA((2 * batch, count))] * 2
        + [pltpu.SemaphoreType.DMA((2 * batch,)), pltpu.SemaphoreType.DMA((3,))]
        + semaphores(len(TIME_PLAN))
        + semaphores(len(FEED_PLAN)),
        compiler_params=pltpu.CompilerParams(collective_id=1, has_side_effects=True, vmem_limit_bytes=60 * 1024 * 1024),
    )(
        measured_features.reshape(sequences, slot_count, width),
        row_column,
        feeder_table,
        time_qkv,
        time_out,
        feed_qkv,
        feed_out,
        route,
        upstream,
        partner,
    )
    predicted_load = jnp.transpose(load.reshape(batch, slot_local, feeder_count, width), (0, 2, 1, 3))
    slabs = (width // LANES, width, LANES)
    gradients = finished(time_mean.reshape(3, *slabs), feed_mean.reshape(5, *slabs))
    return (predicted_load, gradients[None])


def solution(mesh):
    placed = (
        P("gossip", "field", None, None),
        P("field"),
        P(),
        P(),
        P(),
        P(),
        P(),
        P("gossip", None, "field", None),
        P(),
    )
    return jax.shard_map(
        on_device,
        mesh=mesh,
        in_specs=placed,
        out_specs=(P("gossip", None, "field", None), P("gossip", None, None)),
        check_vma=False,
    )
```
